32 devices in a mesh: space: 16 (over z, y, core), slab: 2 (over x).
Axes of the slice: x: 2, y: 2, z: 4, core: 2. Of those that a mesh axis runs over, the one named last changes fastest.
Arguments:
- wavefunctions: bfloat16 [64, 83232], P(None, ('space', 'slab')), may hold values from -6 to 6
- kinetic: bfloat16 [729, 729], replicated, may hold values from -1 to 2, as said below
- cell_scale: float32 [128], P(('space', 'slab')), may hold values from 0.5 to 2
- potential: float32 [128, 729], P(('space', 'slab')), may hold values from -1 to 1
- cell_nodes: int32 [128, 729], P(('space', 'slab')), may hold values from 0 to 2600, as said below
- face_space: int32 [64, 289], P(('space', 'slab')), may hold values from 0 to 2600, as said below
- face_slab: int32 [64, 153], P(('space', 'slab')), may hold values from 0 to 2600, as said below
- projectors: bfloat16 [128, 18, 729], P(('space', 'slab')), may hold values from -0.21875 to 0.21875
- cell_atom: int32 [128], P(('space', 'slab')), may hold values from 0 to 7
- coupling: float32 [128, 18, 18], P(('space', 'slab')), may hold values from -8 to 8
Outputs:
- filtered: float32 [64, 83232], P(None, ('space', 'slab'))
The draws below stay inside these ranges and needn't reach their ends.
Inputs may be any that keep to these rules, and one draw needn't show every extreme that they name: `cell_nodes`: each block's 4 cells tile a block of 1 x 2 x 2 cells of degree 8; within a block the cell nodes name the nodes of that block's node grid, numbered in an order of the block's own. `face_space`: row 2b lists the nodes of block b's lower face across the long direction and row 2b + 1 those of its upper face, both in one fixed order of the face's positions, so that a block's upper face and the next block's lower face list the same nodes at equal positions; each row names distinct nodes. `face_slab`: likewise for the faces across the cross-section between blocks l and l + 1 of a row. `kinetic`: A symmetric matrix.
All inputs are finite; a program needn't handle non-finite values.
Results may differ from the reference program's by a relative error of at most 0.0039.
Values may be sent and summed in bfloat16 or wider, within the bound.
A program may use at most 64 MiB of HBM per device.

```python
import math
import jax
import jax.numpy as jnp
from jax import lax

P_SIZE = 8
NW = 64
NP = 18
CX = 1
CY = 2
CZ = 2
ASLOT = 4
ITERS = 2
NPC = 729
CELLS = 4
NODE_DEV = 2601
FS = 289
FL = 153
NODES = 83232
CELLS_ALL = 128
ATOMS = 128
N_SPACE = 16
N_SLAB = 2


def node_numbering(key):
    devices_all = N_SPACE * N_SLAB
    base = jax.random.fold_in(key, 7)
    keys = jax.vmap(lambda index: jax.random.fold_in(base, index))(jnp.arange(devices_all))
    return jax.vmap(lambda sub: jax.random.permutation(sub, NODE_DEV))(keys).astype(jnp.int32)


def canonical(grid_x, grid_y, grid_z):
    return (grid_x * (P_SIZE * CY + 1) + grid_y) * (P_SIZE * CZ + 1) + grid_z


def draw_cell_nodes(key, part):
    numbering = node_numbering(key)
    cell_index = jnp.arange(CELLS, dtype=jnp.int32)
    cell_x = cell_index // (CY * CZ)
    cell_y = cell_index // CZ % CY
    cell_z = cell_index % CZ
    local_index = jnp.arange(NPC, dtype=jnp.int32)
    node_x = local_index // ((P_SIZE + 1) * (P_SIZE + 1))
    node_y = local_index // (P_SIZE + 1) % (P_SIZE + 1)
    node_z = local_index % (P_SIZE + 1)
    canon = canonical(cell_x[:, None] * P_SIZE + node_x[None, :], cell_y[:, None] * P_SIZE + node_y[None, :], cell_z[:, None] * P_SIZE + node_z[None, :])
    result = jnp.take(numbering, canon.reshape(-1), axis=1)
    return result.reshape(N_SPACE * N_SLAB * CELLS, NPC).astype(jnp.int32)


def draw_face_space(key, part):
    numbering = node_numbering(key)
    face_index = jnp.arange(FS, dtype=jnp.int32)
    grid_y = face_index // (P_SIZE * CZ + 1)
    grid_z = face_index % (P_SIZE * CZ + 1)
    lower = canonical(jnp.zeros_like(grid_y), grid_y, grid_z)
    upper = canonical(jnp.zeros_like(grid_y) + P_SIZE * CX, grid_y, grid_z)
    both = jnp.stack([jnp.take(numbering, lower, axis=1), jnp.take(numbering, upper, axis=1)], axis=1)
    return both.reshape(2 * N_SPACE * N_SLAB, FS).astype(jnp.int32)


def draw_face_slab(key, part):
    numbering = node_numbering(key)
    face_index = jnp.arange(FL, dtype=jnp.int32)
    grid_x = face_index // (P_SIZE * CZ + 1)
    grid_z = face_index % (P_SIZE * CZ + 1)
    lower = canonical(grid_x, jnp.zeros_like(grid_x), grid_z)
    upper = canonical(grid_x, jnp.zeros_like(grid_x) + P_SIZE * CY, grid_z)
    both = jnp.stack([jnp.take(numbering, lower, axis=1), jnp.take(numbering, upper, axis=1)], axis=1)
    return both.reshape(2 * N_SPACE * N_SLAB, FL).astype(jnp.int32)


def draw_kinetic(key, part):
    base = jax.random.fold_in(key, 11)
    noise = jax.random.normal(jax.random.fold_in(base, 1), (NPC, NPC), jnp.float32)
    diagonal = jax.random.uniform(jax.random.fold_in(base, 2), (NPC,), jnp.float32, 0.5, 1.5)
    symmetric = 0.5 * (noise + noise.T) / jnp.sqrt(2.0 * NPC)
    symmetric = jnp.clip(symmetric, -0.9, 0.9)
    return (symmetric + jnp.diag(diagonal)).astype(jnp.bfloat16)


def touch_ends(array, own_key, smallest, largest):
    longest = array.shape.index(max(array.shape))
    spots = []
    for shift in (0, 1):
        where = [jax.random.randint(jax.random.fold_in(own_key, axis), (), 0, length) for axis, length in enumerate(array.shape)]
        where[longest] = (where[longest] + shift) % array.shape[longest]
        spots.append(tuple(where))
    return array.at[spots[0]].set(smallest).at[spots[1]].set(largest)


def block_scale(stream_key, extent, cuts, smallest, high):
    def one(axis_at, blocks):
        draws = jax.random.uniform(jax.random.fold_in(jax.random.fold_in(stream_key, 6), axis_at), (blocks,), jnp.float32, smallest / len(cuts), high / len(cuts))
        return jnp.repeat(jnp.exp(draws), extent[axis_at] // blocks).reshape((-1,) + (1,) * (len(extent) - axis_at - 1))

    factor_of = one(*cuts[0])
    for cut in cuts[1:]:
        factor_of = factor_of * one(*cut)
    return factor_of


def bell_draw(key, shape, scale, most, split=(), held_as=jnp.bfloat16):
    entries = jax.random.normal(key, shape, jnp.float32) * scale
    if len(split) > 0:
        entries = block_scale(key, shape, split, -0.22, 0.18) * entries
    return jnp.clip(entries, min=-most, max=most).astype(held_as)


def setup_inputs(seed: int = 0) -> dict:
    arg_keys = jax.random.split(jax.random.key(seed), 11)
    wavefunctions = bell_draw(arg_keys[0], (NW, NODES), 1.0, 6.0, ((1, 32),))
    kinetic = draw_kinetic(jax.random.fold_in(arg_keys[10], 71), 0)
    cell_scale = jnp.clip(jnp.exp(math.log(2.0) - 1.3862944 * jax.random.uniform(arg_keys[2], (CELLS_ALL,), jnp.float32) ** block_scale(arg_keys[2], (CELLS_ALL,), ((0, 32),), -0.2, 0.2)), 0.5, 2.0)
    potential = jnp.clip(jax.random.uniform(arg_keys[3], (CELLS_ALL, NPC), jnp.float32, -1.0, 1.0) * block_scale(arg_keys[3], (CELLS_ALL, NPC), ((0, 32),), -0.4, 0.0), -1.0, 1.0)
    cell_nodes = draw_cell_nodes(jax.random.fold_in(arg_keys[10], 71), 0)
    face_space = draw_face_space(jax.random.fold_in(arg_keys[10], 71), 0)
    face_slab = draw_face_slab(jax.random.fold_in(arg_keys[10], 71), 0)
    projectors = bell_draw(arg_keys[7], (CELLS_ALL, NP, NPC), NPC ** -0.5, 0.21875, ((0, 32),))
    cell_atom = touch_ends(jax.random.randint(arg_keys[8], (CELLS_ALL,), 0, N_SLAB * ASLOT), jax.random.fold_in(arg_keys[8], 1), 0, (N_SLAB * ASLOT) - 1).astype(jnp.int32)
    coupling = bell_draw(arg_keys[9], (ATOMS, NP, NP), 2.0, 8.0, ((0, 32),), jnp.float32)
    return dict(wavefunctions=wavefunctions, kinetic=kinetic, cell_scale=cell_scale, potential=potential, cell_nodes=cell_nodes, face_space=face_space, face_slab=face_slab, projectors=projectors, cell_atom=cell_atom, coupling=coupling)


filter_centre = 8.0
filter_half = 8.0


def cell_values_of(field_dev, nodes_dev):
    values = jnp.take(field_dev, nodes_dev.reshape(-1), axis=1).astype(jnp.bfloat16)
    return values.reshape(NW, CELLS, NPC)


def margins_dev(inputs):
    field_dev, nodes_dev, projector_dev, atom_dev = inputs
    values = cell_values_of(field_dev, nodes_dev).astype(jnp.float32)
    margin = jnp.einsum("wcj,cpj->cpw", values, projector_dev.astype(jnp.float32))
    onehot = (atom_dev[:, None] == jnp.arange(N_SLAB * ASLOT, dtype=jnp.int32)[None, :]).astype(jnp.float32)
    return jnp.einsum("ca,cpw->apw", onehot, margin, precision=lax.Precision.HIGHEST)


def apply_dev(inputs, kinetic):
    field_dev, nodes_dev, projector_dev, atom_dev, scale_dev, potential_dev, coupled_row = inputs
    values = cell_values_of(field_dev, nodes_dev).astype(jnp.float32)
    kinetic_part = jnp.einsum("wcj,jk->wck", values, kinetic.astype(jnp.float32))
    per_cell = coupled_row[atom_dev].astype(jnp.float32)
    nonlocal_part = jnp.einsum("cpw,cpj->wcj", per_cell, projector_dev.astype(jnp.float32))
    total = scale_dev[None, :, None] * kinetic_part + potential_dev[None] * values + nonlocal_part
    zeros_field = jnp.zeros((NW, NODE_DEV), jnp.float32)
    return zeros_field.at[:, nodes_dev.reshape(-1)].add(total.reshape(NW, CELLS * NPC))


def take_faces(grid, index_grid):
    shape_full = grid.shape[:3] + (index_grid.shape[-1],)
    return jnp.take_along_axis(grid, jnp.broadcast_to(index_grid[:, :, None, :], shape_full), axis=3)


def add_faces(grid, lower_idx, upper_idx, add_lower, add_upper):
    def add_one(inputs):
        field_dev, idx_low, idx_high, value_low, value_high = inputs
        return field_dev.at[:, idx_low].add(value_low).at[:, idx_high].add(value_high)

    flat = lambda arr: arr.reshape((N_SPACE * N_SLAB,) + arr.shape[2:])
    result = lax.map(add_one, (flat(grid), flat(lower_idx), flat(upper_idx), flat(add_lower), flat(add_upper)))
    return result.reshape(grid.shape)


def space_sum(grid, faces):
    lower_vals = take_faces(grid, faces[:, :, 0])
    upper_vals = take_faces(grid, faces[:, :, 1])
    zeros_row = jnp.zeros_like(lower_vals[:1])
    from_below = jnp.concatenate([zeros_row, upper_vals[:-1]], axis=0)
    from_above = jnp.concatenate([lower_vals[1:], zeros_row], axis=0)
    return add_faces(grid, faces[:, :, 0], faces[:, :, 1], from_below, from_above)


def slab_sum(grid, faces):
    lower_vals = take_faces(grid, faces[:, :, 0])
    upper_vals = take_faces(grid, faces[:, :, 1])
    zeros_col = jnp.zeros_like(lower_vals[:, :1])
    from_below = jnp.concatenate([zeros_col, upper_vals[:, :-1]], axis=1)
    from_above = jnp.concatenate([lower_vals[:, 1:], zeros_col], axis=1)
    return add_faces(grid, faces[:, :, 0], faces[:, :, 1], from_below, from_above)


def reference(wavefunctions, kinetic, cell_scale, potential, cell_nodes, face_space, face_slab, projectors, cell_atom, coupling):
    devices_all = N_SPACE * N_SLAB
    nodes_r = cell_nodes.reshape(devices_all, CELLS, NPC)
    projector_r = projectors.reshape(devices_all, CELLS, NP, NPC)
    atom_r = cell_atom.reshape(devices_all, CELLS)
    scale_r = cell_scale.reshape(devices_all, CELLS)
    potential_r = potential.reshape(devices_all, CELLS, NPC)
    space_faces = face_space.reshape(N_SPACE, N_SLAB, 2, FS)
    slab_faces = face_slab.reshape(N_SPACE, N_SLAB, 2, FL)
    coupling_r = coupling.reshape(N_SPACE, N_SLAB * ASLOT, NP, NP)

    def operate(fields):
        partials = lax.map(margins_dev, (fields, nodes_r, projector_r, atom_r))
        rows = partials.reshape(N_SPACE, N_SLAB, N_SLAB * ASLOT, NP, NW).sum(axis=1)
        coupled = jnp.einsum("raqp,rapw->raqw", coupling_r, rows, precision=lax.Precision.HIGHEST).astype(jnp.bfloat16)
        coupled_dev = jnp.repeat(coupled, N_SLAB, axis=0)
        assembled = lax.map(lambda inputs: apply_dev(inputs, kinetic), (fields, nodes_r, projector_r, atom_r, scale_r, potential_r, coupled_dev))
        grid = assembled.reshape(N_SPACE, N_SLAB, NW, NODE_DEV)
        grid = space_sum(grid, space_faces)
        grid = slab_sum(grid, slab_faces)
        return grid.reshape(devices_all, NW, NODE_DEV)

    start = wavefunctions.astype(jnp.float32).reshape(NW, devices_all, NODE_DEV).transpose(1, 0, 2)
    previous = start
    current = (operate(start) - filter_centre * start) / filter_half
    for step_index in range(ITERS - 1):
        following = 2.0 * (operate(current) - filter_centre * current) / filter_half - previous
        previous = current
        current = following
    return current.transpose(1, 0, 2).reshape(NW, NODES)
```

```python
import functools

import jax
import jax.numpy as jnp
from jax import lax
from jax.experimental import pallas as pl
from jax.experimental.pallas import tpu as pltpu
from jax.sharding import PartitionSpec as P

filter_centre = 8.0
filter_half = 8.0
BLK = 256
SHIFT = 8
MESH = pl.DeviceIdType.MESH
NT = (((1,), (1,)), ((), ()))
f32 = jnp.float32
bf16 = jnp.bfloat16


def up(value, unit):
    return -(-value // unit) * unit


def kernel(
    dims,
    y_ref,
    kin_ref,
    scale_ref,
    pot_ref,
    cn_ref,
    fs_ref,
    fl_ref,
    pr_ref,
    atom_ref,
    coupling_ref,
    out_ref,
    hot,
    pack,
    idx,
    kin,
    pp,
    pot,
    cross,
    packs,
    coup,
    yb,
    vals,
    kinv,
    tot,
    asm,
    field,
    outg,
    in_space,
    in_slab,
    inc,
    marg,
    pack_send,
    pack_recv,
    marg_send,
    marg_recv,
    face_send,
    face_recv,
):
    n_space, n_slab = dims["n_space"], dims["n_slab"]
    width, nodes, cells, order = dims["width"], dims["nodes"], dims["cells"], dims["order"]
    atoms, nproj, pstride = dims["atoms"], dims["nproj"], dims["pstride"]
    fs, fl = dims["fs"], dims["fl"]
    op, npad = up(order, BLK), up(nodes, BLK)
    fsp, flp = up(fs, 128), up(fl, 128)
    jp = cells * op
    fp = up(2 * fsp + 2 * flp, BLK)
    lp = cells * pstride
    o_sl = 2 * fsp
    blocks = npad // BLK

    s = lax.axis_index("space")
    l = lax.axis_index("slab")
    above, below = lax.rem(s + 1, n_space), lax.rem(s + n_space - 1, n_space)
    right, left = lax.rem(l + 1, n_slab), lax.rem(l + n_slab - 1, n_slab)

    lane_cell = lax.broadcasted_iota(jnp.int32, (8, lp), 1) // pstride
    atom_row = jnp.zeros((8, lp), f32)
    for c in range(cells):
        atom_row = jnp.where(lane_cell == c, atom_ref[c].astype(f32), atom_row)
    pack[...] = jnp.zeros(pack.shape, f32)
    for i in range(atoms):
        part = slice(i * pstride, (i + 1) * pstride)
        pack[i * pstride : i * pstride + nproj, 0:nproj] = coupling_ref[:, i, :]
        once = pack[part, :]
        many = once
        for c in range(1, cells):
            many = many + pltpu.roll(once, c * pstride, 1)
        pack[part, :] = many
    pack[atoms * pstride :, :] = atom_row

    barrier = pltpu.get_barrier_semaphore()
    for d in range(1, n_slab):
        pl.semaphore_signal(
            barrier, inc=1, device_id={"slab": lax.rem(l + d, n_slab)}, device_id_type=MESH
        )
    for t in (above, below):
        pl.semaphore_signal(barrier, inc=1, device_id={"space": t}, device_id_type=MESH)
    idx[...] = jnp.full(idx.shape, -1, jnp.int32)
    for c in range(cells):
        idx[0:1, c * op : c * op + order] = cn_ref[c : c + 1, :]
    for k in range(2):
        idx[0:1, jp + k * fsp : jp + k * fsp + fs] = fs_ref[k : k + 1, :]
        off = jp + o_sl + k * flp
        idx[0:1, off : off + fl] = fl_ref[k : k + 1, :]

    for b in range(blocks):
        count = min(BLK, nodes - b * BLK)
        rows = slice(b * width, (b + 1) * width)
        if count < BLK:
            yb[rows, :] = jnp.zeros((width, BLK), bf16)
        yb[rows, 0:count] = y_ref[:, b * BLK : b * BLK + count]
    kin[...] = jnp.zeros(kin.shape, bf16)
    kin[0:order, 0:order] = kin_ref[...]
    pp[...] = jnp.zeros(pp.shape, bf16)
    pot[...] = jnp.zeros(pot.shape, f32)
    pot[0:cells, 0:order] = pot_ref[...]
    for c in range(cells):
        pp[c * pstride : c * pstride + nproj, c * op : c * op + order] = pr_ref[:, c, :]

    lane_rows = lax.broadcasted_iota(jnp.int32, (BLK, BLK), 0).astype(f32).astype(bf16)

    def tile(start):
        if isinstance(start, int):
            return slice(start, start + BLK)
        return pl.ds(pl.multiple_of(start, BLK), BLK)

    def low_part(at):
        low = (idx[0:1, at] & (BLK - 1)).astype(f32).astype(bf16)
        hit = lane_rows == jnp.broadcast_to(low, (BLK, BLK))
        return jnp.where(hit, jnp.ones((), bf16), jnp.zeros((), bf16))

    def gather(source, at):
        every = jnp.dot(source[...], hot[:, at], preferred_element_type=f32)
        high = jnp.broadcast_to(idx[0:1, at] >> SHIFT, (width, BLK))
        got = jnp.zeros((width, BLK), f32)
        for b in range(blocks):
            got = jnp.where(high == b, every[b * width : (b + 1) * width], got)
        return got.astype(bf16)

    def spread(pieces):
        left_side, right_side = [], []
        for value, at in pieces:
            high = (idx[0:1, at] >> SHIFT).astype(f32).astype(bf16)
            high = jnp.broadcast_to(high, (width, BLK))
            none = jnp.zeros((), bf16)
            left_side.append(
                jnp.concatenate(
                    [jnp.where(high == jnp.full((), b, bf16), value, none) for b in range(blocks)], axis=0
                )
            )
            right_side.append(hot[:, at])
        return lax.dot_general(
            jnp.concatenate(left_side, axis=1),
            jnp.concatenate(right_side, axis=1),
            NT,
            preferred_element_type=f32,
        )

    per_cell = op // BLK
    tiles = cells * per_cell
    group = 2 if tiles % 2 == 0 else 1

    def take_cells(source, build):
        def body(i):
            for u in range(group):
                j = i * group + u
                at = tile(j * BLK)
                if build:
                    hot[:, at] = low_part(at)
                row = pl.ds(pl.multiple_of(j // per_cell * width, width), width)
                vals[row, tile(j % per_cell * BLK)] = gather(source, at)

        return body

    for k in range(fp // BLK):
        at = tile(jp + k * BLK)
        hot[:, at] = low_part(at)
    slab_row = idx[0:1, jp + o_sl : jp + o_sl + 2 * flp].astype(f32)
    slab_row = jnp.where(slab_row < 0, -2.0, slab_row)
    for k in range(2 * fsp // 128):
        row = idx[0:1, jp + k * 128 : jp + (k + 1) * 128].astype(f32)
        col = jnp.broadcast_to(row, (128, 128)).T
        cross[k * 128 : (k + 1) * 128, :] = jnp.where(col[:, 0:1] == slab_row, 1.0, 0.0).astype(bf16)

    pl.semaphore_wait(barrier, n_slab + 1)
    pack_copies = []
    for d in range(1, n_slab):
        copy = pltpu.make_async_remote_copy(
            src_ref=pack,
            dst_ref=packs.at[d - 1],
            send_sem=pack_send.at[d - 1],
            recv_sem=pack_recv.at[d - 1],
            device_id={"slab": lax.rem(l + d, n_slab)},
            device_id_type=MESH,
        )
        copy.start()
        pack_copies.append(copy)

    pl.loop(0, tiles // group)(take_cells(yb, True))

    for copy in pack_copies:
        copy.wait()
    own_row = pack[atoms * pstride : atoms * pstride + 1, :]
    own_col = jnp.broadcast_to(own_row, (lp, lp)).T
    chosen = jnp.zeros((lp, lp), f32)
    for d in range(n_slab):
        source = lax.rem(l + n_slab - d, n_slab)
        for i in range(atoms):
            part = slice(i * pstride, (i + 1) * pstride)
            block = pack[part, :] if d == 0 else packs[d - 1, part, :]
            tiled = jnp.concatenate([block] * cells, axis=0)
            chosen += jnp.where(own_col == (source * atoms + i).astype(f32), tiled, 0.0)
    for d in range(n_slab):
        last = slice(atoms * pstride, atoms * pstride + 1)
        row = pack[last, :] if d == 0 else packs[d - 1, last, :]
        coup[d] = jnp.where(own_col == row, chosen, 0.0)

    lanes = lax.broadcasted_iota(jnp.int32, (1, fp), 1)
    has_below, has_above = s > 0, s < n_space - 1
    has_left, has_right = l > 0, l < n_slab - 1
    keep = (
        ((lanes < fsp) & has_below)
        | ((lanes >= fsp) & (lanes < o_sl) & has_above)
        | ((lanes >= o_sl) & (lanes < o_sl + flp) & has_left)
        | ((lanes >= o_sl + flp) & (lanes < o_sl + 2 * flp) & has_right)
    ).astype(f32)

    inc[...] = jnp.zeros(inc.shape, bf16)

    def face_copy(step, which, src, landing, device):
        count = landing.shape[-1]
        return pltpu.make_async_remote_copy(
            src_ref=outg.at[step, :, src : src + count],
            dst_ref=landing.at[step, which % 2],
            send_sem=face_send.at[step, which],
            recv_sem=face_recv.at[step, which],
            device_id=device,
            device_id_type=MESH,
        )

    for step in range(2):
        if step == 1:
            pl.loop(0, tiles // group)(take_cells(yb, False))
        margin = jnp.zeros((width, lp), f32)
        for c in range(cells):
            margin += lax.dot_general(
                vals[c * width : (c + 1) * width, :],
                pp[:, c * op : (c + 1) * op],
                NT,
                preferred_element_type=f32,
            )
        marg[step, 0] = margin
        marg_copies = []
        for d in range(1, n_slab):
            copy = pltpu.make_async_remote_copy(
                src_ref=marg.at[step, 0],
                dst_ref=marg.at[step, d],
                send_sem=marg_send.at[step, d - 1],
                recv_sem=marg_recv.at[step, d - 1],
                device_id={"slab": lax.rem(l + d, n_slab)},
                device_id_type=MESH,
            )
            copy.start()
            marg_copies.append(copy)

        kinv[...] = jnp.dot(vals[...], kin[...], preferred_element_type=f32)
        coupled = lax.dot_general(
            margin, coup[0], NT, precision=lax.Precision.HIGHEST, preferred_element_type=f32
        )
        for d in range(1, n_slab):
            marg_copies[d - 1].wait()
            coupled += lax.dot_general(
                marg[step, d], coup[d], NT, precision=lax.Precision.HIGHEST, preferred_element_type=f32
            )
        coupled = coupled.astype(bf16)
        for c in range(cells):
            cols = slice(c * op, (c + 1) * op)
            rows = slice(c * width, (c + 1) * width)
            total = jnp.dot(coupled, pp[:, cols], preferred_element_type=f32)
            total += scale_ref[c] * kinv[rows, :] + pot[c : c + 1, :] * vals[rows, :].astype(f32)
            tot[rows, :] = total.astype(bf16)

        asm[...] = jnp.zeros(asm.shape, f32)

        @pl.loop(0, cells)
        def _(c):
            row = pl.ds(pl.multiple_of(c * width, width), width)
            asm[...] += spread(
                [(tot[row, tile(n * BLK)], tile(c * op + n * BLK)) for n in range(per_cell)]
            )

        yb[...] = asm[...].astype(bf16)

        def take_faces(first, last):
            for k in range(first // BLK, last // BLK):
                outg[step, :, tile(k * BLK)] = gather(yb, tile(jp + k * BLK))

        cut = up(o_sl, BLK)
        take_faces(0, cut)
        space_copies = [
            face_copy(step, 0, fsp, in_space, {"space": above}),
            face_copy(step, 1, 0, in_space, {"space": below}),
        ]
        for copy in space_copies:
            copy.start()
        take_faces(cut, fp)

        if step == 0:
            for b in range(blocks):
                rows = slice(b * width, (b + 1) * width)
                count = min(BLK, nodes - b * BLK)
                field[rows, 0:count] = asm[rows, 0:count] - filter_centre * y_ref[
                    :, b * BLK : b * BLK + count
                ].astype(f32)
                if count < BLK:
                    field[rows, count:] = jnp.zeros((width, BLK - count), f32)
        else:
            for b in range(blocks):
                rows = slice(b * width, (b + 1) * width)
                count = min(BLK, nodes - b * BLK)
                start = y_ref[:, b * BLK : b * BLK + count].astype(f32)
                asm[rows, 0:count] = (
                    2.0 / filter_half * asm[rows, 0:count]
                    - 2.0 * filter_centre / filter_half * field[rows, 0:count]
                    - start
                )

        for k, copy in enumerate(space_copies):
            copy.wait()
            part = slice(k * fsp, (k + 1) * fsp)
            inc[step, :, part] = (in_space[step, k].astype(f32) * keep[:, part]).astype(bf16)
        extra = jnp.dot(inc[step, :, 0:o_sl], cross[...], preferred_element_type=f32)
        part = slice(o_sl, o_sl + 2 * flp)
        outg[step, :, part] = (outg[step, :, part].astype(f32) + extra).astype(bf16)
        slab_copies = [
            face_copy(step, 2, o_sl + flp, in_slab, {"slab": right}),
            face_copy(step, 3, o_sl, in_slab, {"slab": left}),
        ]
        for copy in slab_copies:
            copy.start()

        def add_faces(first, last):
            return spread(
                [
                    (inc[step, :, tile(k * BLK)], tile(jp + k * BLK))
                    for k in range(first // BLK, last // BLK)
                ]
            )

        whole = o_sl // BLK * BLK
        gain = 1.0 if step == 0 else 2.0 / filter_half
        into = field if step == 0 else asm
        if whole:
            into[...] += gain * add_faces(0, whole)

        for k, copy in enumerate(slab_copies):
            copy.wait()
            part = slice(o_sl + k * flp, o_sl + (k + 1) * flp)
            inc[step, :, part] = (in_slab[step, k].astype(f32) * keep[:, part]).astype(bf16)
        rest = into[...] + gain * add_faces(whole, fp)
        if step == 0:
            rest = rest / filter_half
            field[...] = rest
            yb[...] = rest.astype(bf16)
        else:
            for b in range(blocks):
                count = min(BLK, nodes - b * BLK)
                out_ref[:, b * BLK : b * BLK + count] = rest[b * width : (b + 1) * width, 0:count]


def shards(
    wavefunctions,
    kinetic,
    cell_scale,
    potential,
    cell_nodes,
    face_space,
    face_slab,
    projectors,
    cell_atom,
    coupling,
):
    width, nodes = wavefunctions.shape
    cells, order = cell_nodes.shape
    atoms, nproj = coupling.shape[0], coupling.shape[1]
    n_space, n_slab = lax.axis_size("space"), lax.axis_size("slab")
    fs, fl = face_space.shape[1], face_slab.shape[1]
    pstride = up(nproj, 16)
    while cells * pstride % 128:
        pstride += 16
    dims = dict(
        n_space=n_space, n_slab=n_slab, width=width, nodes=nodes, cells=cells, order=order,
        atoms=atoms, nproj=nproj, pstride=pstride, fs=fs, fl=fl,
    )
    op, npad = up(order, BLK), up(nodes, BLK)
    fsp, flp = up(fs, 128), up(fl, 128)
    jp = cells * op
    fp = up(2 * fsp + 2 * flp, BLK)
    lp = cells * pstride
    others = max(n_slab - 1, 1)
    vmem = pl.BlockSpec(memory_space=pltpu.VMEM)
    smem = pl.BlockSpec(memory_space=pltpu.SMEM)
    dma = pltpu.SemaphoreType.DMA
    return pl.pallas_call(
        functools.partial(kernel, dims),
        out_shape=jax.ShapeDtypeStruct((width, nodes), f32),
        in_specs=[vmem, vmem, smem] + [vmem] * 5 + [smem, vmem],
        out_specs=vmem,
        scratch_shapes=[
            pltpu.VMEM((BLK, jp + fp), bf16),
            pltpu.VMEM((atoms * pstride + 8, lp), f32),
            pltpu.VMEM((8, jp + fp), jnp.int32),
            pltpu.VMEM((op, op), bf16),
            pltpu.VMEM((lp, jp), bf16),
            pltpu.VMEM((up(cells, 8), op), f32),
            pltpu.VMEM((2 * fsp, 2 * flp), bf16),
            pltpu.VMEM((others, atoms * pstride + 8, lp), f32),
            pltpu.VMEM((n_slab, lp, lp), f32),
            pltpu.VMEM((npad // BLK * width, BLK), bf16),
            pltpu.VMEM((cells * width, op), bf16),
            pltpu.VMEM((cells * width, op), f32),
            pltpu.VMEM((cells * width, op), bf16),
            pltpu.VMEM((npad // BLK * width, BLK), f32),
            pltpu.VMEM((npad // BLK * width, BLK), f32),
            pltpu.VMEM((2, width, fp), bf16),
            pltpu.VMEM((2, 2, width, fsp), bf16),
            pltpu.VMEM((2, 2, width, flp), bf16),
            pltpu.VMEM((2, width, fp), bf16),
            pltpu.VMEM((2, n_slab, width, lp), f32),
            dma((others,)),
            dma((others,)),
            dma((2, others)),
            dma((2, others)),
            dma((2, 4)),
            dma((2, 4)),
        ],
        compiler_params=pltpu.CompilerParams(
            collective_id=0, has_side_effects=True, vmem_limit_bytes=60 * 1024 * 1024
        ),
    )(
        wavefunctions, kinetic, cell_scale, potential, cell_nodes, face_space, face_slab,
        projectors.transpose(1, 0, 2), cell_atom, coupling.transpose(1, 0, 2),
    )


def solution(mesh):
    placed = (
        P(None, ("space", "slab")),
        P(),
        P(("space", "slab")),
        P(("space", "slab"), None),
        P(("space", "slab"), None),
        P(("space", "slab"), None),
        P(("space", "slab"), None),
        P(("space", "slab"), None, None),
        P(("space", "slab")),
        P(("space", "slab"), None, None),
    )
    return jax.shard_map(
        shards, mesh=mesh, in_specs=placed, out_specs=P(None, ("space", "slab")), check_vma=False
    )
```

```python
import functools

import jax
import jax.numpy as jnp
from jax import lax
from jax.experimental import pallas as pl
from jax.experimental.pallas import tpu as pltpu
from jax.sharding import PartitionSpec as P

filter_centre = 8.0
filter_half = 8.0
BLK = 256
SHIFT = 8
EDGE = 128
MESH = pl.DeviceIdType.MESH
NT = (((1,), (1,)), ((), ()))
f32 = jnp.float32
bf16 = jnp.bfloat16


def up(value, unit):
    return -(-value // unit) * unit


def kernel(
    dims,
    y_ref,
    kin_ref,
    scale_ref,
    pot_ref,
    cn_ref,
    fs_ref,
    fl_ref,
    pr_ref,
    atom_ref,
    coupling_ref,
    out_ref,
    hot,
    pack,
    idx,
    kin,
    pp,
    pot,
    cross,
    packs,
    coup,
    yb,
    vals,
    kinv,
    tot,
    asm,
    field,
    outg,
    in_slab,
    inc,
    marg,
    pn,
    ct,
    spot,
    edge_send,
    in_edge,
    pack_send,
    pack_recv,
    marg_send,
    marg_recv,
    face_send,
    face_recv,
    edge_sem,
    edge_got,
):
    n_space, n_slab = dims["n_space"], dims["n_slab"]
    width, nodes, cells, order = dims["width"], dims["nodes"], dims["cells"], dims["order"]
    atoms, nproj, pstride = dims["atoms"], dims["nproj"], dims["pstride"]
    fs, fl = dims["fs"], dims["fl"]
    op, npad = up(order, BLK), up(nodes, BLK)
    fsp, flp = up(fs, 128), up(fl, 128)
    jp = cells * op
    fp = up(2 * fsp + 2 * flp, BLK)
    lp = cells * pstride
    o_sl = 2 * fsp
    blocks = npad // BLK

    s = lax.axis_index("space")
    l = lax.axis_index("slab")
    above, below = lax.rem(s + 1, n_space), lax.rem(s + n_space - 1, n_space)
    right, left = lax.rem(l + 1, n_slab), lax.rem(l + n_slab - 1, n_slab)
    to_space, to_slab = (below, above), (left, right)
    has_space, has_slab = (s > 0, s < n_space - 1), (l > 0, l < n_slab - 1)
    corners = [(a, b) for a in range(2) for b in range(2)]

    barrier = pltpu.get_barrier_semaphore()

    def greet(exists, device):
        @pl.when(exists)
        def _():
            pl.semaphore_signal(barrier, inc=1, device_id=device, device_id_type=MESH)

        return exists.astype(jnp.int32)

    for d in range(1, n_slab):
        pl.semaphore_signal(
            barrier, inc=1, device_id={"slab": lax.rem(l + d, n_slab)}, device_id_type=MESH
        )
    greeted = n_slab - 1
    for a in range(2):
        greeted += greet(has_space[a], {"space": to_space[a]})
    for a, b in corners:
        greeted += greet(has_space[a] & has_slab[b], {"space": to_space[a], "slab": to_slab[b]})
    for a in range(2):

        @pl.when(jnp.logical_not(has_space[a]))
        def _():
            for step in range(2):
                inc[step, :, a * fsp : (a + 1) * fsp] = jnp.zeros((width, fsp), bf16)

        @pl.when(jnp.logical_not(has_slab[a]))
        def _():
            for step in range(2):
                in_slab[step, a] = jnp.zeros((width, flp), bf16)

    for a, b in corners:

        @pl.when(jnp.logical_not(has_space[a] & has_slab[b]))
        def _():
            for step in range(2):
                in_edge[step, b, :, a * EDGE : (a + 1) * EDGE] = jnp.zeros((width, EDGE), bf16)

    if fp > 2 * fsp + 2 * flp:
        for step in range(2):
            inc[step, :, 2 * fsp + 2 * flp :] = jnp.zeros((width, fp - 2 * fsp - 2 * flp), bf16)

    lane_cell = lax.broadcasted_iota(jnp.int32, (8, lp), 1) // pstride
    atom_row = jnp.zeros((8, lp), f32)
    for c in range(cells):
        atom_row = jnp.where(lane_cell == c, atom_ref[c].astype(f32), atom_row)
    pack[...] = jnp.zeros(pack.shape, f32)
    for i in range(atoms):
        part = slice(i * pstride, (i + 1) * pstride)
        pack[i * pstride : i * pstride + nproj, 0:nproj] = coupling_ref[:, i, :]
        once = pack[part, :]
        many = once
        for c in range(1, cells):
            many = many + pltpu.roll(once, c * pstride, 1)
        pack[part, :] = many
    pack[atoms * pstride : atoms * pstride + 8, :] = atom_row

    idx[...] = jnp.full(idx.shape, -1, jnp.int32)
    for c in range(cells):
        idx[0:1, c * op : c * op + order] = cn_ref[c : c + 1, :]
    for k in range(2):
        idx[0:1, jp + k * fsp : jp + k * fsp + fs] = fs_ref[k : k + 1, :]
        off = jp + o_sl + k * flp
        idx[0:1, off : off + fl] = fl_ref[k : k + 1, :]

    for b in range(blocks):
        count = min(BLK, nodes - b * BLK)
        rows = slice(b * width, (b + 1) * width)
        if count < BLK:
            yb[rows, :] = jnp.zeros((width, BLK), bf16)
        yb[rows, 0:count] = y_ref[:, b * BLK : b * BLK + count]
    kin[...] = jnp.zeros(kin.shape, bf16)
    kin[0:order, 0:order] = kin_ref[...]
    pp[...] = jnp.zeros(pp.shape, bf16)
    pot[...] = jnp.zeros(pot.shape, f32)
    pot[0:cells, 0:order] = pot_ref[...]
    for c in range(cells):
        pp[c * pstride : c * pstride + nproj, c * op : c * op + order] = pr_ref[:, c, :]

    lane_rows = lax.broadcasted_iota(jnp.int32, (BLK, BLK), 0).astype(f32).astype(bf16)

    def tile(start):
        if isinstance(start, int):
            return slice(start, start + BLK)
        return pl.ds(pl.multiple_of(start, BLK), BLK)

    def low_part(at):
        low = (idx[0:1, at] & (BLK - 1)).astype(f32).astype(bf16)
        hit = lane_rows == jnp.broadcast_to(low, (BLK, BLK))
        return jnp.where(hit, jnp.ones((), bf16), jnp.zeros((), bf16))

    def gather(source, at):
        every = jnp.dot(source[...], hot[:, at], preferred_element_type=f32)
        high = jnp.broadcast_to(idx[0:1, at] >> SHIFT, (width, BLK))
        got = jnp.zeros((width, BLK), f32)
        for b in range(blocks):
            got = jnp.where(high == b, every[b * width : (b + 1) * width], got)
        return got.astype(bf16)

    def spread(pieces):
        left_side, right_side = [], []
        for value, at in pieces:
            high = (idx[0:1, at] >> SHIFT).astype(f32).astype(bf16)
            high = jnp.broadcast_to(high, value.shape)
            none = jnp.zeros((), bf16)
            left_side.append(
                jnp.concatenate(
                    [jnp.where(high == jnp.full((), b, bf16), value, none) for b in range(blocks)], axis=0
                )
            )
            right_side.append(hot[:, at])
        return lax.dot_general(
            jnp.concatenate(left_side, axis=1),
            jnp.concatenate(right_side, axis=1),
            NT,
            preferred_element_type=f32,
        )

    per_cell = op // BLK
    tiles = cells * per_cell
    group = max(g for g in (1, 2, 4) if tiles % g == 0)

    def take_cells(source, build):
        def body(i):
            for u in range(group):
                j = i * group + u
                at = tile(j * BLK)
                if build:
                    hot[:, at] = low_part(at)
                row = pl.ds(pl.multiple_of(j // per_cell * width, width), width)
                vals[row, tile(j % per_cell * BLK)] = gather(source, at)

        return body

    for k in range(fp // BLK):
        at = tile(jp + k * BLK)
        hot[:, at] = low_part(at)
    slab_row = idx[0:1, jp + o_sl : jp + o_sl + 2 * flp].astype(f32)
    slab_row = jnp.where(slab_row < 0, -2.0, slab_row)
    for k in range(2 * fsp // 128):
        row = idx[0:1, jp + k * 128 : jp + (k + 1) * 128].astype(f32)
        col = jnp.broadcast_to(row, (128, 128)).T
        cross[k * 128 : (k + 1) * 128, :] = jnp.where(col[:, 0:1] == slab_row, 1.0, 0.0).astype(bf16)

    row_at = lax.broadcasted_iota(jnp.int32, (16, flp), 0)
    counts = (lax.broadcasted_iota(jnp.int32, (16, flp), 1) + 1).astype(f32)
    probe = jnp.where(row_at == 0, 1.0, jnp.where(row_at == 1, counts, 0.0)).astype(bf16)
    row_of = lax.broadcasted_iota(jnp.int32, (16, fsp), 0)
    member, place = [], []
    for b in range(2):
        seen = lax.dot_general(
            probe, cross[:, b * flp : (b + 1) * flp], NT, preferred_element_type=f32
        )
        for a in range(2):
            member.append(jnp.broadcast_to(seen[0:1, a * fsp : (a + 1) * fsp], (16, fsp)))
            place.append(jnp.broadcast_to(seen[1:2, a * fsp : (a + 1) * fsp], (16, fsp)))
    stacked = jnp.zeros((16, fsp), f32)
    for i in range(4):
        stacked = jnp.where(row_of == i, member[i], stacked)
    tri_row = lax.broadcasted_iota(jnp.int32, (fsp, fsp), 0)
    tri_col = lax.broadcasted_iota(jnp.int32, (fsp, fsp), 1)
    before = jnp.where(tri_row < tri_col, 1.0, 0.0).astype(bf16)
    rank = jnp.dot(stacked.astype(bf16), before, preferred_element_type=f32)
    edge_row = lax.broadcasted_iota(jnp.int32, (EDGE, fsp), 0).astype(f32)
    spots = jnp.zeros((8, lp), f32)
    spot_row = lax.broadcasted_iota(jnp.int32, (8, EDGE), 0)
    for i in range(4):
        b, a = i // 2, i % 2
        label = jnp.where(member[i][0:1] > 0.5, rank[i : i + 1], -1.0)
        picked = jnp.where(edge_row == jnp.broadcast_to(label, (EDGE, fsp)), 1.0, 0.0).astype(bf16)
        ct[a, b * EDGE : (b + 1) * EDGE, :] = picked
        listed = lax.dot_general(place[i].astype(bf16), picked, NT, preferred_element_type=f32)
        spots = jnp.where(spot_row == i, listed[0:8], spots)
    pack[atoms * pstride + 8 :, :] = spots

    pl.loop(0, tiles // group)(take_cells(yb, True))

    def margin_of(step):
        margin = jnp.zeros((width, lp), f32)
        if step == 0:
            for c in range(cells):
                margin += lax.dot_general(
                    vals[c * width : (c + 1) * width, :],
                    pp[:, c * op : (c + 1) * op],
                    NT,
                    preferred_element_type=f32,
                )
        else:
            for b in range(blocks):
                margin += lax.dot_general(
                    yb[b * width : (b + 1) * width, :],
                    pn[b * lp : (b + 1) * lp, :],
                    NT,
                    preferred_element_type=f32,
                )
        marg[step, 0] = margin
        return margin

    def send_margin(step):
        copies = []
        for d in range(1, n_slab):
            copy = pltpu.make_async_remote_copy(
                src_ref=marg.at[step, 0],
                dst_ref=marg.at[step, d],
                send_sem=marg_send.at[step, d - 1],
                recv_sem=marg_recv.at[step, d - 1],
                device_id={"slab": lax.rem(l + d, n_slab)},
                device_id_type=MESH,
            )
            copy.start()
            copies.append(copy)
        return copies

    margin_of(0)
    pl.semaphore_wait(barrier, greeted)
    marg_copies = send_margin(0)
    pack_copies = []
    for d in range(1, n_slab):
        copy = pltpu.make_async_remote_copy(
            src_ref=pack,
            dst_ref=packs.at[d - 1],
            send_sem=pack_send.at[d - 1],
            recv_sem=pack_recv.at[d - 1],
            device_id={"slab": lax.rem(l + d, n_slab)},
            device_id_type=MESH,
        )
        copy.start()
        pack_copies.append(copy)

    def use_packs():
        for copy in pack_copies:
            copy.wait()
        own_row = pack[atoms * pstride : atoms * pstride + 1, :]
        own_col = jnp.broadcast_to(own_row, (lp, lp)).T
        chosen = jnp.zeros((lp, lp), f32)
        for d in range(n_slab):
            source = lax.rem(l + n_slab - d, n_slab)
            for i in range(atoms):
                part = slice(i * pstride, (i + 1) * pstride)
                block = pack[part, :] if d == 0 else packs[d - 1, part, :]
                tiled = jnp.concatenate([block] * cells, axis=0)
                chosen += jnp.where(own_col == (source * atoms + i).astype(f32), tiled, 0.0)
        for d in range(n_slab):
            last = slice(atoms * pstride, atoms * pstride + 1)
            row = pack[last, :] if d == 0 else packs[d - 1, last, :]
            coup[d] = jnp.where(own_col == row, chosen, 0.0)
        slot = lax.broadcasted_iota(jnp.int32, (flp, EDGE), 0).astype(f32) + 1.0
        for b in range(2):
            d = 1 if b == 0 else n_slab - 1
            for a in range(2):
                at = atoms * pstride + 8 + (1 - b) * 2 + a
                row = packs[max(d - 1, 0), at : at + 1, 0:EDGE]
                spot[b, :, a * EDGE : (a + 1) * EDGE] = jnp.where(
                    slot == jnp.broadcast_to(row, (flp, EDGE)), 1.0, 0.0
                ).astype(bf16)

    def place_projectors():
        @pl.loop(0, cells)
        def _(c):
            row = pl.ds(pl.multiple_of(c * pstride, pstride), pstride)
            placed = spread(
                [(pp[row, tile(c * op + n * BLK)], tile(c * op + n * BLK)) for n in range(per_cell)]
            ).astype(bf16)
            for b in range(blocks):
                to = pl.ds(pl.multiple_of(b * lp + c * pstride, pstride), pstride)
                pn[to, :] = placed[b * pstride : (b + 1) * pstride]

    def exchange(step):
        moves = []

        def move(sends, gets, source, target, out_sem, in_sem, device):
            copy = pltpu.make_async_remote_copy(
                src_ref=source,
                dst_ref=target,
                send_sem=out_sem,
                recv_sem=in_sem,
                device_id=device,
                device_id_type=MESH,
            )
            pl.when(sends)(copy.start)
            moves.append((sends, gets, copy))

        cut = up(o_sl, BLK)
        take_faces(step, 0, cut)
        for a in range(2):
            seg = slice(a * fsp, (a + 1) * fsp)
            other = slice((1 - a) * fsp, (2 - a) * fsp)
            move(
                has_space[a],
                has_space[1 - a],
                outg.at[step, :, seg],
                inc.at[step, :, other],
                face_send.at[step, a],
                face_recv.at[step, a],
                {"space": to_space[a]},
            )
        for a in range(2):
            edge_send[step, a] = lax.dot_general(
                outg[step, :, a * fsp : (a + 1) * fsp], ct[a], NT, preferred_element_type=f32
            ).astype(bf16)
        for a, b in corners:
            move(
                has_space[a] & has_slab[b],
                has_space[1 - a] & has_slab[1 - b],
                edge_send.at[step, a, :, b * EDGE : (b + 1) * EDGE],
                in_edge.at[step, 1 - b, :, (1 - a) * EDGE : (2 - a) * EDGE],
                edge_sem.at[step, 2 * a + b],
                edge_got.at[step, 2 * a + b],
                {"space": to_space[a], "slab": to_slab[b]},
            )
        take_faces(step, cut, fp)
        for b in range(2):
            move(
                has_slab[b],
                has_slab[1 - b],
                outg.at[step, :, o_sl + b * flp : o_sl + (b + 1) * flp],
                in_slab.at[step, 1 - b],
                face_send.at[step, 2 + b],
                face_recv.at[step, 2 + b],
                {"slab": to_slab[b]},
            )
        return moves

    def finish(step, moves):
        for sends, gets, copy in moves:
            pl.when(gets)(copy.wait_recv)
        for sends, gets, copy in moves:
            pl.when(sends)(copy.wait_send)
        for b in range(2):
            part = slice(o_sl + b * flp, o_sl + (b + 1) * flp)
            corner = lax.dot_general(in_edge[step, b], spot[b], NT, preferred_element_type=f32)
            inc[step, :, part] = (in_slab[step, b].astype(f32) + corner).astype(bf16)
        return spread([(inc[step, :, tile(k * BLK)], tile(jp + k * BLK)) for k in range(fp // BLK)])

    def take_faces(step, first, last):
        for k in range(first // BLK, last // BLK):
            outg[step, :, tile(k * BLK)] = gather(yb, tile(jp + k * BLK))

    for step in range(2):
        if step == 1:
            margin_of(1)
            marg_copies = send_margin(1)
            pl.loop(0, tiles // group)(take_cells(yb, False))
        kinv[...] = jnp.dot(vals[...], kin[...], preferred_element_type=f32)
        for c in range(cells):
            rows = slice(c * width, (c + 1) * width)
            total = scale_ref[c] * kinv[rows, :] + pot[c : c + 1, :] * vals[rows, :].astype(f32)
            tot[rows, :] = total.astype(bf16)

        asm[...] = jnp.zeros(asm.shape, f32)

        @pl.loop(0, cells)
        def _(c):
            row = pl.ds(pl.multiple_of(c * width, width), width)
            asm[...] += spread(
                [(tot[row, tile(n * BLK)], tile(c * op + n * BLK)) for n in range(per_cell)]
            )

        if step == 0:
            place_projectors()
            use_packs()
        coupled = jnp.zeros((width, lp), f32)
        for d in range(n_slab):
            if d > 0:
                marg_copies[d - 1].wait()
            coupled += lax.dot_general(
                marg[step, d], coup[d], NT, precision=lax.Precision.HIGHEST, preferred_element_type=f32
            )
        coupled = coupled.astype(bf16)
        for b in range(blocks):
            rows = slice(b * width, (b + 1) * width)
            whole = asm[rows, :] + jnp.dot(
                coupled, pn[b * lp : (b + 1) * lp, :], preferred_element_type=f32
            )
            asm[rows, :] = whole
            yb[rows, :] = whole.astype(bf16)

        moves = exchange(step)

        if step == 0:
            for b in range(blocks):
                rows = slice(b * width, (b + 1) * width)
                count = min(BLK, nodes - b * BLK)
                field[rows, 0:count] = asm[rows, 0:count] - filter_centre * y_ref[
                    :, b * BLK : b * BLK + count
                ].astype(f32)
                if count < BLK:
                    field[rows, count:] = jnp.zeros((width, BLK - count), f32)
            fresh = (field[...] + finish(step, moves)) / filter_half
            field[...] = fresh
            yb[...] = fresh.astype(bf16)
        else:
            for b in range(blocks):
                rows = slice(b * width, (b + 1) * width)
                count = min(BLK, nodes - b * BLK)
                start = y_ref[:, b * BLK : b * BLK + count].astype(f32)
                asm[rows, 0:count] = (
                    2.0 / filter_half * asm[rows, 0:count]
                    - 2.0 * filter_centre / filter_half * field[rows, 0:count]
                    - start
                )
            added = finish(step, moves)
            for b in range(blocks):
                rows = slice(b * width, (b + 1) * width)
                count = min(BLK, nodes - b * BLK)
                out_ref[:, b * BLK : b * BLK + count] = (
                    asm[rows, 0:count] + 2.0 / filter_half * added[rows, 0:count]
                )


def shards(
    wavefunctions,
    kinetic,
    cell_scale,
    potential,
    cell_nodes,
    face_space,
    face_slab,
    projectors,
    cell_atom,
    coupling,
):
    width, nodes = wavefunctions.shape
    cells, order = cell_nodes.shape
    atoms, nproj = coupling.shape[0], coupling.shape[1]
    n_space, n_slab = lax.axis_size("space"), lax.axis_size("slab")
    fs, fl = face_space.shape[1], face_slab.shape[1]
    pstride = up(nproj, 16)
    while cells * pstride % 128:
        pstride += 16
    dims = dict(
        n_space=n_space, n_slab=n_slab, width=width, nodes=nodes, cells=cells, order=order,
        atoms=atoms, nproj=nproj, pstride=pstride, fs=fs, fl=fl,
    )
    op, npad = up(order, BLK), up(nodes, BLK)
    fsp, flp = up(fs, 128), up(fl, 128)
    jp = cells * op
    fp = up(2 * fsp + 2 * flp, BLK)
    lp = cells * pstride
    others = max(n_slab - 1, 1)
    vmem = pl.BlockSpec(memory_space=pltpu.VMEM)
    smem = pl.BlockSpec(memory_space=pltpu.SMEM)
    dma = pltpu.SemaphoreType.DMA
    return pl.pallas_call(
        functools.partial(kernel, dims),
        out_shape=jax.ShapeDtypeStruct((width, nodes), f32),
        in_specs=[vmem, vmem, smem] + [vmem] * 5 + [smem, vmem],
        out_specs=vmem,
        scratch_shapes=[
            pltpu.VMEM((BLK, jp + fp), bf16),
            pltpu.VMEM((atoms * pstride + 16, lp), f32),
            pltpu.VMEM((8, jp + fp), jnp.int32),
            pltpu.VMEM((op, op), bf16),
            pltpu.VMEM((lp, jp), bf16),
            pltpu.VMEM((up(cells, 8), op), f32),
            pltpu.VMEM((2 * fsp, 2 * flp), bf16),
            pltpu.VMEM((others, atoms * pstride + 16, lp), f32),
            pltpu.VMEM((n_slab, lp, lp), f32),
            pltpu.VMEM((npad // BLK * width, BLK), bf16),
            pltpu.VMEM((cells * width, op), bf16),
            pltpu.VMEM((cells * width, op), f32),
            pltpu.VMEM((cells * width, op), bf16),
            pltpu.VMEM((npad // BLK * width, BLK), f32),
            pltpu.VMEM((npad // BLK * width, BLK), f32),
            pltpu.VMEM((2, width, fp), bf16),
            pltpu.VMEM((2, 2, width, flp), bf16),
            pltpu.VMEM((2, width, fp), bf16),
            pltpu.VMEM((2, n_slab, width, lp), f32),
            pltpu.VMEM((npad // BLK * lp, BLK), bf16),
            pltpu.VMEM((2, 2 * EDGE, fsp), bf16),
            pltpu.VMEM((2, flp, 2 * EDGE), bf16),
            pltpu.VMEM((2, 2, width, 2 * EDGE), bf16),
            pltpu.VMEM((2, 2, width, 2 * EDGE), bf16),
            dma((others,)),
            dma((others,)),
            dma((2, others)),
            dma((2, others)),
            dma((2, 4)),
            dma((2, 4)),
            dma((2, 4)),
            dma((2, 4)),
        ],
        compiler_params=pltpu.CompilerParams(
            collective_id=0, has_side_effects=True, vmem_limit_bytes=60 * 1024 * 1024
        ),
    )(
        wavefunctions, kinetic, cell_scale, potential, cell_nodes, face_space, face_slab,
        projectors.transpose(1, 0, 2), cell_atom, coupling.transpose(1, 0, 2),
    )


def solution(mesh):
    placed = (
        P(None, ("space", "slab")),
        P(),
        P(("space", "slab")),
        P(("space", "slab"), None),
        P(("space", "slab"), None),
        P(("space", "slab"), None),
        P(("space", "slab"), None),
        P(("space", "slab"), None, None),
        P(("space", "slab")),
        P(("space", "slab"), None, None),
    )
    return jax.shard_map(
        shards, mesh=mesh, in_specs=placed, out_specs=P(None, ("space", "slab")), check_vma=False
    )
```

```python
import functools

import jax
import jax.numpy as jnp
from jax import lax
from jax.experimental import pallas as pl
from jax.experimental.pallas import tpu as pltpu
from jax.sharding import PartitionSpec as P

filter_centre = 8.0
filter_half = 8.0
BLK = 256
SHIFT = 8
EDGE = 128
MESH = pl.DeviceIdType.MESH
NT = (((1,), (1,)), ((), ()))
f32 = jnp.float32
bf16 = jnp.bfloat16


def up(value, unit):
    return -(-value // unit) * unit


def kernel(
    dims,
    y_hbm,
    kin_hbm,
    scale_hbm,
    pot_hbm,
    cn_hbm,
    fs_hbm,
    fl_hbm,
    pr_hbm,
    atom_hbm,
    coupling_hbm,
    out_ref,
    y_ref,
    kin_ref,
    scale_ref,
    pot_ref,
    cn_ref,
    fs_ref,
    fl_ref,
    pr_ref,
    atom_ref,
    coupling_ref,
    in_sem,
    hot,
    pack,
    idx,
    kin,
    pp,
    pot,
    cross,
    packs,
    coup,
    yb,
    vals,
    kinv,
    tot,
    asm,
    field,
    outg,
    in_slab,
    inc,
    marg,
    pn,
    ct,
    spot,
    edge_send,
    in_edge,
    pack_send,
    pack_recv,
    marg_send,
    marg_recv,
    face_send,
    face_recv,
    edge_sem,
    edge_got,
):
    n_space, n_slab = dims["n_space"], dims["n_slab"]
    width, nodes, cells, order = dims["width"], dims["nodes"], dims["cells"], dims["order"]
    atoms, nproj, pstride = dims["atoms"], dims["nproj"], dims["pstride"]
    fs, fl = dims["fs"], dims["fl"]
    op, npad = up(order, BLK), up(nodes, BLK)
    fsp, flp = up(fs, 128), up(fl, 128)
    jp = cells * op
    fp = up(2 * fsp + 2 * flp, BLK)
    lp = cells * pstride
    o_sl = 2 * fsp
    wide = up(max(atoms * pstride, lp, EDGE), 128)
    blocks = npad // BLK

    outside = (
        y_hbm, kin_hbm, scale_hbm, pot_hbm, cn_hbm, fs_hbm, fl_hbm, pr_hbm, atom_hbm, coupling_hbm
    )
    inside = (
        y_ref, kin_ref, scale_ref, pot_ref, cn_ref, fs_ref, fl_ref, pr_ref, atom_ref, coupling_ref
    )
    loads = [
        pltpu.make_async_copy(outside[i], inside[i], in_sem.at[i]) for i in range(len(outside))
    ]
    for i in (4, 5, 6, 0, 8, 9, 7, 1, 2, 3):
        loads[i].start()

    s = lax.axis_index("space")
    l = lax.axis_index("slab")
    above, below = lax.rem(s + 1, n_space), lax.rem(s + n_space - 1, n_space)
    right, left = lax.rem(l + 1, n_slab), lax.rem(l + n_slab - 1, n_slab)
    to_space, to_slab = (below, above), (left, right)
    has_space, has_slab = (s > 0, s < n_space - 1), (l > 0, l < n_slab - 1)
    corners = [(a, b) for a in range(2) for b in range(2)]

    barrier = pltpu.get_barrier_semaphore()

    def greet(exists, device):
        @pl.when(exists)
        def _():
            pl.semaphore_signal(barrier, inc=1, device_id=device, device_id_type=MESH)

        return exists.astype(jnp.int32)

    for d in range(1, n_slab):
        pl.semaphore_signal(
            barrier, inc=1, device_id={"slab": lax.rem(l + d, n_slab)}, device_id_type=MESH
        )
    greeted = n_slab - 1
    for a in range(2):
        greeted += greet(has_space[a], {"space": to_space[a]})
    for a, b in corners:
        greeted += greet(has_space[a] & has_slab[b], {"space": to_space[a], "slab": to_slab[b]})
    for a in range(2):

        @pl.when(jnp.logical_not(has_space[a]))
        def _():
            for step in range(2):
                inc[step, :, a * fsp : (a + 1) * fsp] = jnp.zeros((width, fsp), bf16)

        @pl.when(jnp.logical_not(has_slab[a]))
        def _():
            for step in range(2):
                in_slab[step, a] = jnp.zeros((width, flp), bf16)

    for a, b in corners:

        @pl.when(jnp.logical_not(has_space[a] & has_slab[b]))
        def _():
            for step in range(2):
                in_edge[step, b, :, a * EDGE : (a + 1) * EDGE] = jnp.zeros((width, EDGE), bf16)

    if fp > 2 * fsp + 2 * flp:
        for step in range(2):
            inc[step, :, 2 * fsp + 2 * flp :] = jnp.zeros((width, fp - 2 * fsp - 2 * flp), bf16)

    for i in (4, 5, 6):
        loads[i].wait()
    idx[...] = jnp.full(idx.shape, -1, jnp.int32)
    for c in range(cells):
        idx[0:1, c * op : c * op + order] = cn_ref[c : c + 1, :]
    for k in range(2):
        idx[0:1, jp + k * fsp : jp + k * fsp + fs] = fs_ref[k : k + 1, :]
        off = jp + o_sl + k * flp
        idx[0:1, off : off + fl] = fl_ref[k : k + 1, :]

    loads[0].wait()
    for b in range(blocks):
        count = min(BLK, nodes - b * BLK)
        rows = slice(b * width, (b + 1) * width)
        if count < BLK:
            yb[rows, :] = jnp.zeros((width, BLK), bf16)
        yb[rows, 0:count] = y_ref[:, b * BLK : b * BLK + count]
    lane_rows = lax.broadcasted_iota(jnp.int32, (BLK, BLK), 0).astype(f32).astype(bf16)

    def tile(start):
        if isinstance(start, int):
            return slice(start, start + BLK)
        return pl.ds(pl.multiple_of(start, BLK), BLK)

    def low_part(at):
        low = (idx[0:1, at] & (BLK - 1)).astype(f32).astype(bf16)
        hit = lane_rows == jnp.broadcast_to(low, (BLK, BLK))
        return jnp.where(hit, jnp.ones((), bf16), jnp.zeros((), bf16))

    def gather(source, at):
        every = jnp.dot(source[...], hot[:, at], preferred_element_type=f32)
        high = jnp.broadcast_to(idx[0:1, at] >> SHIFT, (width, BLK))
        got = jnp.zeros((width, BLK), f32)
        for b in range(blocks):
            got = jnp.where(high == b, every[b * width : (b + 1) * width], got)
        return got.astype(bf16)

    def spread(pieces):
        left_side, right_side = [], []
        for value, at in pieces:
            high = (idx[0:1, at] >> SHIFT).astype(f32).astype(bf16)
            high = jnp.broadcast_to(high, value.shape)
            none = jnp.zeros((), bf16)
            left_side.append(
                jnp.concatenate(
                    [jnp.where(high == jnp.full((), b, bf16), value, none) for b in range(blocks)], axis=0
                )
            )
            right_side.append(hot[:, at])
        return lax.dot_general(
            jnp.concatenate(left_side, axis=1),
            jnp.concatenate(right_side, axis=1),
            NT,
            preferred_element_type=f32,
        )

    per_cell = op // BLK
    tiles = cells * per_cell
    group = max(g for g in (1, 2, 4) if tiles % g == 0)

    def take_cells(source, build):
        def body(i):
            for u in range(group):
                j = i * group + u
                at = tile(j * BLK)
                if build:
                    hot[:, at] = low_part(at)
                row = pl.ds(pl.multiple_of(j // per_cell * width, width), width)
                vals[row, tile(j % per_cell * BLK)] = gather(source, at)

        return body

    for k in range(fp // BLK):
        at = tile(jp + k * BLK)
        hot[:, at] = low_part(at)
    slab_row = idx[0:1, jp + o_sl : jp + o_sl + 2 * flp].astype(f32)
    slab_row = jnp.where(slab_row < 0, -2.0, slab_row)
    for k in range(2 * fsp // 128):
        row = idx[0:1, jp + k * 128 : jp + (k + 1) * 128].astype(f32)
        col = jnp.broadcast_to(row, (128, 128)).T
        cross[k * 128 : (k + 1) * 128, :] = jnp.where(col[:, 0:1] == slab_row, 1.0, 0.0).astype(bf16)

    loads[8].wait()
    loads[9].wait()
    lane_cell = lax.broadcasted_iota(jnp.int32, (8, lp), 1) // pstride
    atom_row = jnp.zeros((8, lp), f32)
    for c in range(cells):
        atom_row = jnp.where(lane_cell == c, atom_ref[c].astype(f32), atom_row)
    pack[...] = jnp.zeros(pack.shape, f32)
    for i in range(atoms):
        pack[0:nproj, i * pstride : i * pstride + nproj] = coupling_ref[:, i, :]
    pack[pstride : pstride + 8, 0:lp] = atom_row
    loads[7].wait()
    pp[...] = jnp.zeros(pp.shape, bf16)
    for c in range(cells):
        pp[c * pstride : c * pstride + nproj, c * op : c * op + order] = pr_ref[:, c, :]
    for i in (1, 2, 3):
        loads[i].wait()
    kin[...] = jnp.zeros(kin.shape, bf16)
    kin[0:order, 0:order] = kin_ref[...]
    pot[...] = jnp.zeros(pot.shape, f32)
    pot[0:cells, 0:order] = pot_ref[...]
    row_at = lax.broadcasted_iota(jnp.int32, (16, flp), 0)
    counts = (lax.broadcasted_iota(jnp.int32, (16, flp), 1) + 1).astype(f32)
    probe = jnp.where(row_at == 0, 1.0, jnp.where(row_at == 1, counts, 0.0)).astype(bf16)
    row_of = lax.broadcasted_iota(jnp.int32, (16, fsp), 0)
    member, place = [], []
    for b in range(2):
        seen = lax.dot_general(
            probe, cross[:, b * flp : (b + 1) * flp], NT, preferred_element_type=f32
        )
        for a in range(2):
            member.append(jnp.broadcast_to(seen[0:1, a * fsp : (a + 1) * fsp], (16, fsp)))
            place.append(jnp.broadcast_to(seen[1:2, a * fsp : (a + 1) * fsp], (16, fsp)))
    stacked = jnp.zeros((16, fsp), f32)
    for i in range(4):
        stacked = jnp.where(row_of == i, member[i], stacked)
    tri_row = lax.broadcasted_iota(jnp.int32, (fsp, fsp), 0)
    tri_col = lax.broadcasted_iota(jnp.int32, (fsp, fsp), 1)
    before = jnp.where(tri_row < tri_col, 1.0, 0.0).astype(bf16)
    rank = jnp.dot(stacked.astype(bf16), before, preferred_element_type=f32)
    edge_row = lax.broadcasted_iota(jnp.int32, (EDGE, fsp), 0).astype(f32)
    spots = jnp.zeros((8, EDGE), f32)
    spot_row = lax.broadcasted_iota(jnp.int32, (8, EDGE), 0)
    for i in range(4):
        b, a = i // 2, i % 2
        label = jnp.where(member[i][0:1] > 0.5, rank[i : i + 1], -1.0)
        picked = jnp.where(edge_row == jnp.broadcast_to(label, (EDGE, fsp)), 1.0, 0.0).astype(bf16)
        ct[a, b * EDGE : (b + 1) * EDGE, :] = picked
        listed = lax.dot_general(place[i].astype(bf16), picked, NT, preferred_element_type=f32)
        spots = jnp.where(spot_row == i, listed[0:8], spots)
    pack[pstride + 8 :, 0:EDGE] = spots

    pl.loop(0, tiles // group)(take_cells(yb, True))

    def margin_of(step):
        margin = jnp.zeros((width, lp), f32)
        if step == 0:
            for c in range(cells):
                margin += lax.dot_general(
                    vals[c * width : (c + 1) * width, :],
                    pp[:, c * op : (c + 1) * op],
                    NT,
                    preferred_element_type=f32,
                )
        else:
            for b in range(blocks):
                margin += lax.dot_general(
                    yb[b * width : (b + 1) * width, :],
                    pn[b * lp : (b + 1) * lp, :],
                    NT,
                    preferred_element_type=f32,
                )
        marg[step, 0] = margin
        return margin

    def send_margin(step):
        copies = []
        for d in range(1, n_slab):
            copy = pltpu.make_async_remote_copy(
                src_ref=marg.at[step, 0],
                dst_ref=marg.at[step, d],
                send_sem=marg_send.at[step, d - 1],
                recv_sem=marg_recv.at[step, d - 1],
                device_id={"slab": lax.rem(l + d, n_slab)},
                device_id_type=MESH,
            )
            copy.start()
            copies.append(copy)
        return copies

    def place_projectors(first, last):
        @pl.loop(first, last)
        def _(c):
            row = pl.ds(pl.multiple_of(c * pstride, pstride), pstride)
            placed = spread(
                [(pp[row, tile(c * op + n * BLK)], tile(c * op + n * BLK)) for n in range(per_cell)]
            ).astype(bf16)
            for b in range(blocks):
                to = pl.ds(pl.multiple_of(b * lp + c * pstride, pstride), pstride)
                pn[to, :] = placed[b * pstride : (b + 1) * pstride]

    def local_part():
        kinv[...] = jnp.dot(vals[...], kin[...], preferred_element_type=f32)
        for c in range(cells):
            rows = slice(c * width, (c + 1) * width)
            total = scale_ref[c] * kinv[rows, :] + pot[c : c + 1, :] * vals[rows, :].astype(f32)
            tot[rows, :] = total.astype(bf16)

    span = 1

    def scatter():
        def some(first):
            return spread(
                [
                    (tot[rows_of(first, c), tile(n * BLK)], tile((first + c) * op + n * BLK))
                    for c in range(span)
                    for n in range(per_cell)
                ]
            )

        def rows_of(first, c):
            start = (first + c) * width
            if isinstance(start, int):
                return slice(start, start + width)
            return pl.ds(pl.multiple_of(start, width), width)

        asm[...] = some(0)
        if cells > span:

            @pl.loop(1, cells // span)
            def _(i):
                asm[...] += some(i * span)

    margin_of(0)
    local_part()
    early = 0
    place_projectors(0, early)
    pl.semaphore_wait(barrier, greeted)
    marg_copies = send_margin(0)
    pack_copies = []
    for d in range(1, n_slab):
        copy = pltpu.make_async_remote_copy(
            src_ref=pack,
            dst_ref=packs.at[d - 1],
            send_sem=pack_send.at[d - 1],
            recv_sem=pack_recv.at[d - 1],
            device_id={"slab": lax.rem(l + d, n_slab)},
            device_id_type=MESH,
        )
        copy.start()
        pack_copies.append(copy)

    def use_packs():
        for copy in pack_copies:
            copy.wait()
        own_row = pack[pstride : pstride + 1, 0:lp]
        own_col = jnp.broadcast_to(own_row, (lp, lp)).T
        segment = lax.broadcasted_iota(jnp.int32, (pstride, wide), 1) // pstride
        chosen = jnp.zeros((lp, lp), f32)
        for d in range(n_slab):
            source = lax.rem(l + n_slab - d, n_slab)
            table = pack[0:pstride, :] if d == 0 else packs[d - 1, 0:pstride, :]
            for i in range(atoms):
                once = jnp.where(segment == i, table, 0.0)
                many = once
                for c in range(cells):
                    if c != i:
                        many = many + pltpu.roll(once, (c - i) * pstride % wide, 1)
                tiled = jnp.concatenate([many[:, 0:lp]] * cells, axis=0)
                chosen += jnp.where(own_col == (source * atoms + i).astype(f32), tiled, 0.0)
        for d in range(n_slab):
            last = slice(pstride, pstride + 1)
            row = pack[last, 0:lp] if d == 0 else packs[d - 1, last, 0:lp]
            coup[d] = jnp.where(own_col == row, chosen, 0.0)
        slot = lax.broadcasted_iota(jnp.int32, (flp, EDGE), 0).astype(f32) + 1.0
        for b in range(2):
            d = 1 if b == 0 else n_slab - 1
            for a in range(2):
                at = pstride + 8 + (1 - b) * 2 + a
                row = packs[max(d - 1, 0), at : at + 1, 0:EDGE]
                spot[b, :, a * EDGE : (a + 1) * EDGE] = jnp.where(
                    slot == jnp.broadcast_to(row, (flp, EDGE)), 1.0, 0.0
                ).astype(bf16)

    def exchange(step):
        moves = []

        def move(sends, gets, source, target, out_sem, in_sem, device):
            copy = pltpu.make_async_remote_copy(
                src_ref=source,
                dst_ref=target,
                send_sem=out_sem,
                recv_sem=in_sem,
                device_id=device,
                device_id_type=MESH,
            )
            pl.when(sends)(copy.start)
            moves.append((sends, gets, copy))

        cut = up(o_sl, BLK)
        take_faces(step, 0, cut)
        for a in range(2):
            seg = slice(a * fsp, (a + 1) * fsp)
            other = slice((1 - a) * fsp, (2 - a) * fsp)
            move(
                has_space[a],
                has_space[1 - a],
                outg.at[step, :, seg],
                inc.at[step, :, other],
                face_send.at[step, a],
                face_recv.at[step, a],
                {"space": to_space[a]},
            )
        for a in range(2):
            edge_send[step, a] = lax.dot_general(
                outg[step, :, a * fsp : (a + 1) * fsp], ct[a], NT, preferred_element_type=f32
            ).astype(bf16)
        for a, b in corners:
            move(
                has_space[a] & has_slab[b],
                has_space[1 - a] & has_slab[1 - b],
                edge_send.at[step, a, :, b * EDGE : (b + 1) * EDGE],
                in_edge.at[step, 1 - b, :, (1 - a) * EDGE : (2 - a) * EDGE],
                edge_sem.at[step, 2 * a + b],
                edge_got.at[step, 2 * a + b],
                {"space": to_space[a], "slab": to_slab[b]},
            )
        take_faces(step, cut, fp)
        for b in range(2):
            move(
                has_slab[b],
                has_slab[1 - b],
                outg.at[step, :, o_sl + b * flp : o_sl + (b + 1) * flp],
                in_slab.at[step, 1 - b],
                face_send.at[step, 2 + b],
                face_recv.at[step, 2 + b],
                {"slab": to_slab[b]},
            )
        return moves

    def finish(step, moves):
        for sends, gets, copy in moves:
            pl.when(gets)(copy.wait_recv)
        for sends, gets, copy in moves:
            pl.when(sends)(copy.wait_send)
        for b in range(2):
            part = slice(o_sl + b * flp, o_sl + (b + 1) * flp)
            corner = lax.dot_general(in_edge[step, b], spot[b], NT, preferred_element_type=f32)
            inc[step, :, part] = (in_slab[step, b].astype(f32) + corner).astype(bf16)
        return spread([(inc[step, :, tile(k * BLK)], tile(jp + k * BLK)) for k in range(fp // BLK)])

    def take_faces(step, first, last):
        for k in range(first // BLK, last // BLK):
            outg[step, :, tile(k * BLK)] = gather(yb, tile(jp + k * BLK))

    for step in range(2):
        if step == 1:
            margin_of(1)
            marg_copies = send_margin(1)
            pl.loop(0, tiles // group)(take_cells(yb, False))
            local_part()
        scatter()

        if step == 0:
            place_projectors(early, cells)
            use_packs()
        coupled = jnp.zeros((width, lp), f32)
        for d in range(n_slab):
            if d > 0:
                marg_copies[d - 1].wait()
            coupled += lax.dot_general(
                marg[step, d], coup[d], NT, precision=lax.Precision.HIGHEST, preferred_element_type=f32
            )
        coupled = coupled.astype(bf16)
        for b in range(blocks):
            rows = slice(b * width, (b + 1) * width)
            whole = asm[rows, :] + jnp.dot(
                coupled, pn[b * lp : (b + 1) * lp, :], preferred_element_type=f32
            )
            asm[rows, :] = whole
            yb[rows, :] = whole.astype(bf16)

        moves = exchange(step)

        if step == 0:
            for b in range(blocks):
                rows = slice(b * width, (b + 1) * width)
                count = min(BLK, nodes - b * BLK)
                field[rows, 0:count] = asm[rows, 0:count] - filter_centre * y_ref[
                    :, b * BLK : b * BLK + count
                ].astype(f32)
                if count < BLK:
                    field[rows, count:] = jnp.zeros((width, BLK - count), f32)
            fresh = (field[...] + finish(step, moves)) / filter_half
            field[...] = fresh
            yb[...] = fresh.astype(bf16)
        else:
            for b in range(blocks):
                rows = slice(b * width, (b + 1) * width)
                count = min(BLK, nodes - b * BLK)
                start = y_ref[:, b * BLK : b * BLK + count].astype(f32)
                asm[rows, 0:count] = (
                    2.0 / filter_half * asm[rows, 0:count]
                    - 2.0 * filter_centre / filter_half * field[rows, 0:count]
                    - start
                )
            added = finish(step, moves)
            for b in range(blocks):
                rows = slice(b * width, (b + 1) * width)
                count = min(BLK, nodes - b * BLK)
                out_ref[:, b * BLK : b * BLK + count] = (
                    asm[rows, 0:count] + 2.0 / filter_half * added[rows, 0:count]
                )


def shards(
    wavefunctions,
    kinetic,
    cell_scale,
    potential,
    cell_nodes,
    face_space,
    face_slab,
    projectors,
    cell_atom,
    coupling,
):
    width, nodes = wavefunctions.shape
    cells, order = cell_nodes.shape
    atoms, nproj = coupling.shape[0], coupling.shape[1]
    n_space, n_slab = lax.axis_size("space"), lax.axis_size("slab")
    fs, fl = face_space.shape[1], face_slab.shape[1]
    pstride = up(nproj, 16)
    while cells * pstride % 128:
        pstride += 16
    dims = dict(
        n_space=n_space, n_slab=n_slab, width=width, nodes=nodes, cells=cells, order=order,
        atoms=atoms, nproj=nproj, pstride=pstride, fs=fs, fl=fl,
    )
    op, npad = up(order, BLK), up(nodes, BLK)
    fsp, flp = up(fs, 128), up(fl, 128)
    jp = cells * op
    fp = up(2 * fsp + 2 * flp, BLK)
    lp = cells * pstride
    others = max(n_slab - 1, 1)
    wide = up(max(atoms * pstride, lp, EDGE), 128)
    vmem = pl.BlockSpec(memory_space=pltpu.VMEM)
    dma = pltpu.SemaphoreType.DMA
    return pl.pallas_call(
        functools.partial(kernel, dims),
        out_shape=pltpu.VMEM((width, nodes), f32),
        in_specs=[pl.BlockSpec(memory_space=pl.ANY)] * 10,
        out_specs=vmem,
        scratch_shapes=[
            pltpu.VMEM((width, nodes), bf16),
            pltpu.VMEM((order, order), bf16),
            pltpu.SMEM((cells,), f32),
            pltpu.VMEM((cells, order), f32),
            pltpu.VMEM((cells, order), jnp.int32),
            pltpu.VMEM((2, fs), jnp.int32),
            pltpu.VMEM((2, fl), jnp.int32),
            pltpu.VMEM((nproj, cells, order), bf16),
            pltpu.SMEM((cells,), jnp.int32),
            pltpu.VMEM((nproj, atoms, nproj), f32),
            dma((10,)),
            pltpu.VMEM((BLK, jp + fp), bf16),
            pltpu.VMEM((pstride + 16, wide), f32),
            pltpu.VMEM((8, jp + fp), jnp.int32),
            pltpu.VMEM((op, op), bf16),
            pltpu.VMEM((lp, jp), bf16),
            pltpu.VMEM((up(cells, 8), op), f32),
            pltpu.VMEM((2 * fsp, 2 * flp), bf16),
            pltpu.VMEM((others, pstride + 16, wide), f32),
            pltpu.VMEM((n_slab, lp, lp), f32),
            pltpu.VMEM((npad // BLK * width, BLK), bf16),
            pltpu.VMEM((cells * width, op), bf16),
            pltpu.VMEM((cells * width, op), f32),
            pltpu.VMEM((cells * width, op), bf16),
            pltpu.VMEM((npad // BLK * width, BLK), f32),
            pltpu.VMEM((npad // BLK * width, BLK), f32),
            pltpu.VMEM((2, width, fp), bf16),
            pltpu.VMEM((2, 2, width, flp), bf16),
            pltpu.VMEM((2, width, fp), bf16),
            pltpu.VMEM((2, n_slab, width, lp), f32),
            pltpu.VMEM((npad // BLK * lp, BLK), bf16),
            pltpu.VMEM((2, 2 * EDGE, fsp), bf16),
            pltpu.VMEM((2, flp, 2 * EDGE), bf16),
            pltpu.VMEM((2, 2, width, 2 * EDGE), bf16),
            pltpu.VMEM((2, 2, width, 2 * EDGE), bf16),
            dma((others,)),
            dma((others,)),
            dma((2, others)),
            dma((2, others)),
            dma((2, 4)),
            dma((2, 4)),
            dma((2, 4)),
            dma((2, 4)),
        ],
        compiler_params=pltpu.CompilerParams(
            collective_id=0, has_side_effects=True, vmem_limit_bytes=60 * 1024 * 1024
        ),
    )(
        wavefunctions, kinetic, cell_scale, potential, cell_nodes, face_space, face_slab,
        projectors.transpose(1, 0, 2), cell_atom, coupling.transpose(1, 0, 2),
    )


def solution(mesh):
    placed = (
        P(None, ("space", "slab")),
        P(),
        P(("space", "slab")),
        P(("space", "slab"), None),
        P(("space", "slab"), None),
        P(("space", "slab"), None),
        P(("space", "slab"), None),
        P(("space", "slab"), None, None),
        P(("space", "slab")),
        P(("space", "slab"), None, None),
    )
    return jax.shard_map(
        shards, mesh=mesh, in_specs=placed, out_specs=P(None, ("space", "slab")), check_vma=False
    )
```

```python
import functools

import jax
import jax.numpy as jnp
from jax import lax
from jax.experimental import pallas as pl
from jax.experimental.pallas import tpu as pltpu
from jax.sharding import PartitionSpec as P

filter_centre = 8.0
filter_half = 8.0
BLK = 256
SHIFT = 8
EDGE = 128
MESH = pl.DeviceIdType.MESH
NT = (((1,), (1,)), ((), ()))
f32 = jnp.float32
bf16 = jnp.bfloat16


def up(value, unit):
    return -(-value // unit) * unit


def kernel(
    dims,
    y_hbm,
    kin_hbm,
    scale_hbm,
    pot_hbm,
    cn_hbm,
    fs_hbm,
    fl_hbm,
    pr_hbm,
    atom_hbm,
    coupling_hbm,
    out_ref,
    y_ref,
    kin_ref,
    scale_ref,
    pot_ref,
    cn_ref,
    fs_ref,
    fl_ref,
    pr_ref,
    atom_ref,
    coupling_ref,
    in_sem,
    hot,
    pack,
    idx,
    kin,
    pp,
    pot,
    cross,
    packs,
    coup,
    yb,
    vals,
    kinv,
    tot,
    asm,
    field,
    outg,
    in_slab,
    inc,
    marg,
    pn,
    ct,
    spot,
    edge_send,
    in_edge,
    pack_send,
    pack_recv,
    marg_send,
    marg_recv,
    face_send,
    face_recv,
    edge_sem,
    edge_got,
):
    n_space, n_slab = dims["n_space"], dims["n_slab"]
    width, nodes, cells, order = dims["width"], dims["nodes"], dims["cells"], dims["order"]
    atoms, nproj, pstride = dims["atoms"], dims["nproj"], dims["pstride"]
    fs, fl = dims["fs"], dims["fl"]
    op, npad = up(order, BLK), up(nodes, BLK)
    fsp, flp = up(fs, 128), up(fl, 128)
    jp = cells * op
    fp = up(2 * fsp + 2 * flp, BLK)
    lp = cells * pstride
    o_sl = 2 * fsp
    wide = up(max(atoms * pstride, lp, EDGE), 128)
    blocks = npad // BLK

    outside = (
        y_hbm, kin_hbm, scale_hbm, pot_hbm, cn_hbm, fs_hbm, fl_hbm, pr_hbm, atom_hbm, coupling_hbm
    )
    inside = (
        y_ref, kin_ref, scale_ref, pot_ref, cn_ref, fs_ref, fl_ref, pr_ref, atom_ref, coupling_ref
    )
    loads = [
        pltpu.make_async_copy(outside[i], inside[i], in_sem.at[i]) for i in range(len(outside))
    ]
    for i in (4, 5, 6, 0, 8, 9, 7, 1, 2, 3):
        loads[i].start()

    s = lax.axis_index("space")
    l = lax.axis_index("slab")
    above, below = lax.rem(s + 1, n_space), lax.rem(s + n_space - 1, n_space)
    right, left = lax.rem(l + 1, n_slab), lax.rem(l + n_slab - 1, n_slab)
    to_space, to_slab = (below, above), (left, right)
    has_space, has_slab = (s > 0, s < n_space - 1), (l > 0, l < n_slab - 1)
    corners = [(a, b) for a in range(2) for b in range(2)]

    barrier = pltpu.get_barrier_semaphore()

    def greet(exists, device):
        @pl.when(exists)
        def _():
            pl.semaphore_signal(barrier, inc=1, device_id=device, device_id_type=MESH)

        return exists.astype(jnp.int32)

    for d in range(1, n_slab):
        pl.semaphore_signal(
            barrier, inc=1, device_id={"slab": lax.rem(l + d, n_slab)}, device_id_type=MESH
        )
    greeted = n_slab - 1
    for a in range(2):
        greeted += greet(has_space[a], {"space": to_space[a]})
    for a, b in corners:
        greeted += greet(has_space[a] & has_slab[b], {"space": to_space[a], "slab": to_slab[b]})
    for a in range(2):

        @pl.when(jnp.logical_not(has_space[a]))
        def _():
            for step in range(2):
                inc[step, :, a * fsp : (a + 1) * fsp] = jnp.zeros((width, fsp), bf16)

        @pl.when(jnp.logical_not(has_slab[a]))
        def _():
            for step in range(2):
                in_slab[step, a] = jnp.zeros((width, flp), bf16)

    for a, b in corners:

        @pl.when(jnp.logical_not(has_space[a] & has_slab[b]))
        def _():
            for step in range(2):
                in_edge[step, b, :, a * EDGE : (a + 1) * EDGE] = jnp.zeros((width, EDGE), bf16)

    if fp > 2 * fsp + 2 * flp:
        for step in range(2):
            inc[step, :, 2 * fsp + 2 * flp :] = jnp.zeros((width, fp - 2 * fsp - 2 * flp), bf16)

    for i in (4, 5, 6):
        loads[i].wait()
    idx[...] = jnp.full(idx.shape, -1, jnp.int32)
    for c in range(cells):
        idx[0:1, c * op : c * op + order] = cn_ref[c : c + 1, :]
    for k in range(2):
        idx[0:1, jp + k * fsp : jp + k * fsp + fs] = fs_ref[k : k + 1, :]
        off = jp + o_sl + k * flp
        idx[0:1, off : off + fl] = fl_ref[k : k + 1, :]

    loads[0].wait()
    for b in range(blocks):
        count = min(BLK, nodes - b * BLK)
        rows = slice(b * width, (b + 1) * width)
        if count < BLK:
            yb[rows, :] = jnp.zeros((width, BLK), bf16)
        yb[rows, 0:count] = y_ref[:, b * BLK : b * BLK + count]
    lane_rows = lax.broadcasted_iota(jnp.int32, (BLK, BLK), 0).astype(f32).astype(bf16)

    def tile(start):
        if isinstance(start, int):
            return slice(start, start + BLK)
        return pl.ds(pl.multiple_of(start, BLK), BLK)

    def low_part(at):
        low = (idx[0:1, at] & (BLK - 1)).astype(f32).astype(bf16)
        hit = lane_rows == jnp.broadcast_to(low, (BLK, BLK))
        return jnp.where(hit, jnp.ones((), bf16), jnp.zeros((), bf16))

    def gather(source, at):
        every = jnp.dot(source[...], hot[:, at], preferred_element_type=f32)
        high = jnp.broadcast_to(idx[0:1, at] >> SHIFT, (width, BLK))
        got = jnp.zeros((width, BLK), f32)
        for b in range(blocks):
            got = jnp.where(high == b, every[b * width : (b + 1) * width], got)
        return got.astype(bf16)

    def spread(pieces):
        left_side, right_side = [], []
        for value, at in pieces:
            high = (idx[0:1, at] >> SHIFT).astype(f32).astype(bf16)
            high = jnp.broadcast_to(high, value.shape)
            none = jnp.zeros((), bf16)
            left_side.append(
                jnp.concatenate(
                    [jnp.where(high == jnp.full((), b, bf16), value, none) for b in range(blocks)], axis=0
                )
            )
            right_side.append(hot[:, at])
        return lax.dot_general(
            jnp.concatenate(left_side, axis=1),
            jnp.concatenate(right_side, axis=1),
            NT,
            preferred_element_type=f32,
        )

    per_cell = op // BLK
    tiles = cells * per_cell
    group = max(g for g in (1, 2, 4) if tiles % g == 0)

    def take_cells(source, build):
        def body(i):
            for u in range(group):
                j = i * group + u
                at = tile(j * BLK)
                if build:
                    hot[:, at] = low_part(at)
                row = pl.ds(pl.multiple_of(j // per_cell * width, width), width)
                vals[row, tile(j % per_cell * BLK)] = gather(source, at)

        return body

    for k in range(fp // BLK):
        at = tile(jp + k * BLK)
        hot[:, at] = low_part(at)
    slab_row = idx[0:1, jp + o_sl : jp + o_sl + 2 * flp].astype(f32)
    slab_row = jnp.where(slab_row < 0, -2.0, slab_row)
    for k in range(2 * fsp // 128):
        row = idx[0:1, jp + k * 128 : jp + (k + 1) * 128].astype(f32)
        col = jnp.broadcast_to(row, (128, 128)).T
        cross[k * 128 : (k + 1) * 128, :] = jnp.where(col[:, 0:1] == slab_row, 1.0, 0.0).astype(bf16)

    loads[8].wait()
    loads[9].wait()
    lane_cell = lax.broadcasted_iota(jnp.int32, (8, lp), 1) // pstride
    atom_row = jnp.zeros((8, lp), f32)
    for c in range(cells):
        atom_row = jnp.where(lane_cell == c, atom_ref[c].astype(f32), atom_row)
    pack[...] = jnp.zeros(pack.shape, f32)
    for i in range(atoms):
        pack[0:nproj, i * pstride : i * pstride + nproj] = coupling_ref[:, i, :]
    pack[pstride : pstride + 8, 0:lp] = atom_row
    loads[7].wait()
    pp[...] = jnp.zeros(pp.shape, bf16)
    for c in range(cells):
        pp[c * pstride : c * pstride + nproj, c * op : c * op + order] = pr_ref[:, c, :]
    for i in (1, 2, 3):
        loads[i].wait()
    kin[...] = jnp.zeros(kin.shape, bf16)
    kin[0:order, 0:order] = kin_ref[...]
    pot[...] = jnp.zeros(pot.shape, f32)
    pot[0:cells, 0:order] = pot_ref[...]
    row_at = lax.broadcasted_iota(jnp.int32, (16, flp), 0)
    counts = (lax.broadcasted_iota(jnp.int32, (16, flp), 1) + 1).astype(f32)
    probe = jnp.where(row_at == 0, 1.0, jnp.where(row_at == 1, counts, 0.0)).astype(bf16)
    row_of = lax.broadcasted_iota(jnp.int32, (16, fsp), 0)
    member, place = [], []
    for b in range(2):
        seen = lax.dot_general(
            probe, cross[:, b * flp : (b + 1) * flp], NT, preferred_element_type=f32
        )
        for a in range(2):
            member.append(jnp.broadcast_to(seen[0:1, a * fsp : (a + 1) * fsp], (16, fsp)))
            place.append(jnp.broadcast_to(seen[1:2, a * fsp : (a + 1) * fsp], (16, fsp)))
    stacked = jnp.zeros((16, fsp), f32)
    for i in range(4):
        stacked = jnp.where(row_of == i, member[i], stacked)
    tri_row = lax.broadcasted_iota(jnp.int32, (fsp, fsp), 0)
    tri_col = lax.broadcasted_iota(jnp.int32, (fsp, fsp), 1)
    before = jnp.where(tri_row < tri_col, 1.0, 0.0).astype(bf16)
    rank = jnp.dot(stacked.astype(bf16), before, preferred_element_type=f32)
    edge_row = lax.broadcasted_iota(jnp.int32, (EDGE, fsp), 0).astype(f32)
    spots = jnp.zeros((8, EDGE), f32)
    spot_row = lax.broadcasted_iota(jnp.int32, (8, EDGE), 0)
    for i in range(4):
        b, a = i // 2, i % 2
        label = jnp.where(member[i][0:1] > 0.5, rank[i : i + 1], -1.0)
        picked = jnp.where(edge_row == jnp.broadcast_to(label, (EDGE, fsp)), 1.0, 0.0).astype(bf16)
        ct[a, b * EDGE : (b + 1) * EDGE, :] = picked
        listed = lax.dot_general(place[i].astype(bf16), picked, NT, preferred_element_type=f32)
        spots = jnp.where(spot_row == i, listed[0:8], spots)
    pack[pstride + 8 :, 0:EDGE] = spots

    pl.loop(0, 1)(take_cells(yb, True))
    pl.semaphore_wait(barrier, greeted)
    pack_copies = []
    for d in range(1, n_slab):
        copy = pltpu.make_async_remote_copy(
            src_ref=pack,
            dst_ref=packs.at[d - 1],
            send_sem=pack_send.at[d - 1],
            recv_sem=pack_recv.at[d - 1],
            device_id={"slab": lax.rem(l + d, n_slab)},
            device_id_type=MESH,
        )
        copy.start()
        pack_copies.append(copy)

    pl.loop(1, tiles // group)(take_cells(yb, True))

    def margin_of(step):
        margin = jnp.zeros((width, lp), f32)
        if step == 0:
            for c in range(cells):
                margin += lax.dot_general(
                    vals[c * width : (c + 1) * width, :],
                    pp[:, c * op : (c + 1) * op],
                    NT,
                    preferred_element_type=f32,
                )
        else:
            for b in range(blocks):
                margin += lax.dot_general(
                    yb[b * width : (b + 1) * width, :],
                    pn[b * lp : (b + 1) * lp, :],
                    NT,
                    preferred_element_type=f32,
                )
        marg[step, 0] = margin
        return margin

    def send_margin(step):
        copies = []
        for d in range(1, n_slab):
            copy = pltpu.make_async_remote_copy(
                src_ref=marg.at[step, 0],
                dst_ref=marg.at[step, d],
                send_sem=marg_send.at[step, d - 1],
                recv_sem=marg_recv.at[step, d - 1],
                device_id={"slab": lax.rem(l + d, n_slab)},
                device_id_type=MESH,
            )
            copy.start()
            copies.append(copy)
        return copies

    def local_part():
        kinv[...] = jnp.dot(vals[...], kin[...], preferred_element_type=f32)
        for c in range(cells):
            rows = slice(c * width, (c + 1) * width)
            total = scale_ref[c] * kinv[rows, :] + pot[c : c + 1, :] * vals[rows, :].astype(f32)
            tot[rows, :] = total.astype(bf16)

    def scatter(step):
        def one(c, fresh):
            row = c * width if isinstance(c, int) else pl.multiple_of(c * width, width)
            low = c * pstride if isinstance(c, int) else pl.multiple_of(c * pstride, pstride)
            pieces = []
            for n in range(per_cell):
                at = tile(c * op + n * BLK)
                value = tot[pl.ds(row, width), tile(n * BLK)]
                if step == 0:
                    value = jnp.concatenate([value, pp[pl.ds(low, pstride), at]], axis=0)
                pieces.append((value, at))
            result = spread(pieces)
            each = width if step else width + pstride
            for b in range(blocks):
                rows = slice(b * width, (b + 1) * width)
                part = result[b * each : b * each + width]
                asm[rows, :] = part if fresh else asm[rows, :] + part
                if step == 0:
                    to = pl.ds(b * lp + low, pstride)
                    pn[to, :] = result[b * each + width : (b + 1) * each].astype(bf16)

        one(0, True)

        @pl.loop(1, cells)
        def _(c):
            one(c, False)

    margin_of(0)
    marg_copies = send_margin(0)
    local_part()
    def use_packs():
        for copy in pack_copies:
            copy.wait()
        own_row = pack[pstride : pstride + 1, 0:lp]
        own_col = jnp.broadcast_to(own_row, (lp, lp)).T
        segment = lax.broadcasted_iota(jnp.int32, (pstride, wide), 1) // pstride
        chosen = jnp.zeros((lp, lp), f32)
        for d in range(n_slab):
            source = lax.rem(l + n_slab - d, n_slab)
            table = pack[0:pstride, :] if d == 0 else packs[d - 1, 0:pstride, :]
            for i in range(atoms):
                once = jnp.where(segment == i, table, 0.0)
                many = once
                for c in range(cells):
                    if c != i:
                        many = many + pltpu.roll(once, (c - i) * pstride % wide, 1)
                tiled = jnp.concatenate([many[:, 0:lp]] * cells, axis=0)
                chosen += jnp.where(own_col == (source * atoms + i).astype(f32), tiled, 0.0)
        for d in range(n_slab):
            last = slice(pstride, pstride + 1)
            row = pack[last, 0:lp] if d == 0 else packs[d - 1, last, 0:lp]
            used = jnp.where(own_col == row, chosen, 0.0)
            high = used.astype(bf16)
            coup[d, :, 0:lp] = high
            coup[d, :, lp : 2 * lp] = high
            coup[d, :, 2 * lp : 3 * lp] = (used - high.astype(f32)).astype(bf16)
        slot = lax.broadcasted_iota(jnp.int32, (flp, EDGE), 0).astype(f32) + 1.0
        for b in range(2):
            d = 1 if b == 0 else n_slab - 1
            for a in range(2):
                at = pstride + 8 + (1 - b) * 2 + a
                row = packs[max(d - 1, 0), at : at + 1, 0:EDGE]
                spot[b, :, a * EDGE : (a + 1) * EDGE] = jnp.where(
                    slot == jnp.broadcast_to(row, (flp, EDGE)), 1.0, 0.0
                ).astype(bf16)

    def exchange(step):
        moves = []

        def move(sends, gets, source, target, out_sem, in_sem, device):
            copy = pltpu.make_async_remote_copy(
                src_ref=source,
                dst_ref=target,
                send_sem=out_sem,
                recv_sem=in_sem,
                device_id=device,
                device_id_type=MESH,
            )
            pl.when(sends)(copy.start)
            moves.append((sends, gets, copy))

        cut = up(o_sl, BLK)
        take_faces(step, 0, cut)
        for a in range(2):
            seg = slice(a * fsp, (a + 1) * fsp)
            other = slice((1 - a) * fsp, (2 - a) * fsp)
            move(
                has_space[a],
                has_space[1 - a],
                outg.at[step, :, seg],
                inc.at[step, :, other],
                face_send.at[step, a],
                face_recv.at[step, a],
                {"space": to_space[a]},
            )
        for a in range(2):
            edge_send[step, a] = lax.dot_general(
                outg[step, :, a * fsp : (a + 1) * fsp], ct[a], NT, preferred_element_type=f32
            ).astype(bf16)
        for a, b in corners:
            move(
                has_space[a] & has_slab[b],
                has_space[1 - a] & has_slab[1 - b],
                edge_send.at[step, a, :, b * EDGE : (b + 1) * EDGE],
                in_edge.at[step, 1 - b, :, (1 - a) * EDGE : (2 - a) * EDGE],
                edge_sem.at[step, 2 * a + b],
                edge_got.at[step, 2 * a + b],
                {"space": to_space[a], "slab": to_slab[b]},
            )
        take_faces(step, cut, fp)
        for b in range(2):
            move(
                has_slab[b],
                has_slab[1 - b],
                outg.at[step, :, o_sl + b * flp : o_sl + (b + 1) * flp],
                in_slab.at[step, 1 - b],
                face_send.at[step, 2 + b],
                face_recv.at[step, 2 + b],
                {"slab": to_slab[b]},
            )
        return moves

    def finish(step, moves):
        for sends, gets, copy in moves:
            pl.when(gets)(copy.wait_recv)
        for sends, gets, copy in moves:
            pl.when(sends)(copy.wait_send)
        for b in range(2):
            part = slice(o_sl + b * flp, o_sl + (b + 1) * flp)
            corner = lax.dot_general(in_edge[step, b], spot[b], NT, preferred_element_type=f32)
            inc[step, :, part] = (in_slab[step, b].astype(f32) + corner).astype(bf16)
        return spread([(inc[step, :, tile(k * BLK)], tile(jp + k * BLK)) for k in range(fp // BLK)])

    def take_faces(step, first, last):
        for k in range(first // BLK, last // BLK):
            outg[step, :, tile(k * BLK)] = gather(yb, tile(jp + k * BLK))

    for step in range(2):
        if step == 1:
            margin_of(1)
            marg_copies = send_margin(1)
            pl.loop(0, tiles // group)(take_cells(yb, False))
            local_part()
        scatter(step)

        if step == 0:
            use_packs()
        coupled = jnp.zeros((width, lp), f32)
        for d in range(n_slab):
            if d > 0:
                marg_copies[d - 1].wait()
            whole = marg[step, d]
            high = whole.astype(bf16)
            low = (whole - high.astype(f32)).astype(bf16)
            coupled += lax.dot_general(
                jnp.concatenate([high, low, high], axis=1), coup[d], NT, preferred_element_type=f32
            )
        coupled = coupled.astype(bf16)
        for b in range(blocks):
            rows = slice(b * width, (b + 1) * width)
            whole = asm[rows, :] + jnp.dot(
                coupled, pn[b * lp : (b + 1) * lp, :], preferred_element_type=f32
            )
            asm[rows, :] = whole
            yb[rows, :] = whole.astype(bf16)

        moves = exchange(step)

        if step == 0:
            for b in range(blocks):
                rows = slice(b * width, (b + 1) * width)
                count = min(BLK, nodes - b * BLK)
                field[rows, 0:count] = asm[rows, 0:count] - filter_centre * y_ref[
                    :, b * BLK : b * BLK + count
                ].astype(f32)
                if count < BLK:
                    field[rows, count:] = jnp.zeros((width, BLK - count), f32)
            fresh = (field[...] + finish(step, moves)) / filter_half
            field[...] = fresh
            yb[...] = fresh.astype(bf16)
        else:
            for b in range(blocks):
                rows = slice(b * width, (b + 1) * width)
                count = min(BLK, nodes - b * BLK)
                start = y_ref[:, b * BLK : b * BLK + count].astype(f32)
                asm[rows, 0:count] = (
                    2.0 / filter_half * asm[rows, 0:count]
                    - 2.0 * filter_centre / filter_half * field[rows, 0:count]
                    - start
                )
            added = finish(step, moves)
            for b in range(blocks):
                rows = slice(b * width, (b + 1) * width)
                count = min(BLK, nodes - b * BLK)
                out_ref[:, b * BLK : b * BLK + count] = (
                    asm[rows, 0:count] + 2.0 / filter_half * added[rows, 0:count]
                )


def shards(
    wavefunctions,
    kinetic,
    cell_scale,
    potential,
    cell_nodes,
    face_space,
    face_slab,
    projectors,
    cell_atom,
    coupling,
):
    width, nodes = wavefunctions.shape
    cells, order = cell_nodes.shape
    atoms, nproj = coupling.shape[0], coupling.shape[1]
    n_space, n_slab = lax.axis_size("space"), lax.axis_size("slab")
    fs, fl = face_space.shape[1], face_slab.shape[1]
    pstride = up(nproj, 16)
    while cells * pstride % 128:
        pstride += 16
    dims = dict(
        n_space=n_space, n_slab=n_slab, width=width, nodes=nodes, cells=cells, order=order,
        atoms=atoms, nproj=nproj, pstride=pstride, fs=fs, fl=fl,
    )
    op, npad = up(order, BLK), up(nodes, BLK)
    fsp, flp = up(fs, 128), up(fl, 128)
    jp = cells * op
    fp = up(2 * fsp + 2 * flp, BLK)
    lp = cells * pstride
    others = max(n_slab - 1, 1)
    wide = up(max(atoms * pstride, lp, EDGE), 128)
    vmem = pl.BlockSpec(memory_space=pltpu.VMEM)
    dma = pltpu.SemaphoreType.DMA
    return pl.pallas_call(
        functools.partial(kernel, dims),
        out_shape=pltpu.VMEM((width, nodes), f32),
        in_specs=[pl.BlockSpec(memory_space=pl.ANY)] * 10,
        out_specs=vmem,
        scratch_shapes=[
            pltpu.VMEM((width, nodes), bf16),
            pltpu.VMEM((order, order), bf16),
            pltpu.SMEM((cells,), f32),
            pltpu.VMEM((cells, order), f32),
            pltpu.VMEM((cells, order), jnp.int32),
            pltpu.VMEM((2, fs), jnp.int32),
            pltpu.VMEM((2, fl), jnp.int32),
            pltpu.VMEM((nproj, cells, order), bf16),
            pltpu.SMEM((cells,), jnp.int32),
            pltpu.VMEM((nproj, atoms, nproj), f32),
            dma((10,)),
            pltpu.VMEM((BLK, jp + fp), bf16),
            pltpu.VMEM((pstride + 16, wide), f32),
            pltpu.VMEM((8, jp + fp), jnp.int32),
            pltpu.VMEM((op, op), bf16),
            pltpu.VMEM((lp, jp), bf16),
            pltpu.VMEM((up(cells, 8), op), f32),
            pltpu.VMEM((2 * fsp, 2 * flp), bf16),
            pltpu.VMEM((others, pstride + 16, wide), f32),
            pltpu.VMEM((n_slab, lp, 3 * lp), bf16),
            pltpu.VMEM((npad // BLK * width, BLK), bf16),
            pltpu.VMEM((cells * width, op), bf16),
            pltpu.VMEM((cells * width, op), f32),
            pltpu.VMEM((cells * width, op), bf16),
            pltpu.VMEM((npad // BLK * width, BLK), f32),
            pltpu.VMEM((npad // BLK * width, BLK), f32),
            pltpu.VMEM((2, width, fp), bf16),
            pltpu.VMEM((2, 2, width, flp), bf16),
            pltpu.VMEM((2, width, fp), bf16),
            pltpu.VMEM((2, n_slab, width, lp), f32),
            pltpu.VMEM((npad // BLK * lp, BLK), bf16),
            pltpu.VMEM((2, 2 * EDGE, fsp), bf16),
            pltpu.VMEM((2, flp, 2 * EDGE), bf16),
            pltpu.VMEM((2, 2, width, 2 * EDGE), bf16),
            pltpu.VMEM((2, 2, width, 2 * EDGE), bf16),
            dma((others,)),
            dma((others,)),
            dma((2, others)),
            dma((2, others)),
            dma((2, 4)),
            dma((2, 4)),
            dma((2, 4)),
            dma((2, 4)),
        ],
        compiler_params=pltpu.CompilerParams(
            collective_id=0, has_side_effects=True, vmem_limit_bytes=60 * 1024 * 1024
        ),
    )(
        wavefunctions, kinetic, cell_scale, potential, cell_nodes, face_space, face_slab,
        projectors.transpose(1, 0, 2), cell_atom, coupling.transpose(1, 0, 2),
    )


def solution(mesh):
    placed = (
        P(None, ("space", "slab")),
        P(),
        P(("space", "slab")),
        P(("space", "slab"), None),
        P(("space", "slab"), None),
        P(("space", "slab"), None),
        P(("space", "slab"), None),
        P(("space", "slab"), None, None),
        P(("space", "slab")),
        P(("space", "slab"), None, None),
    )
    return jax.shard_map(
        shards, mesh=mesh, in_specs=placed, out_specs=P(None, ("space", "slab")), check_vma=False
    )
```

```python
import functools

import jax
import jax.numpy as jnp
from jax import lax
from jax.experimental import pallas as pl
from jax.experimental.pallas import tpu as pltpu
from jax.sharding import PartitionSpec as P

filter_centre = 8.0
filter_half = 8.0
BLK = 256
SHIFT = 8
EDGE = 128
MESH = pl.DeviceIdType.MESH
NT = (((1,), (1,)), ((), ()))
f32 = jnp.float32
bf16 = jnp.bfloat16


def up(value, unit):
    return -(-value // unit) * unit


def kernel(
    dims,
    y_hbm,
    kin_hbm,
    scale_hbm,
    pot_hbm,
    cn_hbm,
    fs_hbm,
    fl_hbm,
    pr_hbm,
    atom_hbm,
    coupling_hbm,
    out_ref,
    y_ref,
    kin_ref,
    scale_ref,
    pot_ref,
    cn_ref,
    fs_ref,
    fl_ref,
    pr_ref,
    atom_ref,
    coupling_ref,
    in_sem,
    hot,
    pack,
    idx,
    kin,
    pp,
    pot,
    cross,
    packs,
    coup,
    yb,
    vals,
    kinv,
    tot,
    asm,
    field,
    outg,
    in_slab,
    inc,
    marg,
    pn,
    ct,
    spot,
    edge_send,
    in_edge,
    pack_send,
    pack_recv,
    marg_send,
    marg_recv,
    face_send,
    face_recv,
    edge_sem,
    edge_got,
):
    n_space, n_slab = dims["n_space"], dims["n_slab"]
    width, nodes, cells, order = dims["width"], dims["nodes"], dims["cells"], dims["order"]
    atoms, nproj, pstride = dims["atoms"], dims["nproj"], dims["pstride"]
    fs, fl = dims["fs"], dims["fl"]
    op, npad = up(order, BLK), up(nodes, BLK)
    fsp, flp = up(fs, 128), up(fl, 128)
    jp = cells * op
    fp = up(2 * fsp + 2 * flp, BLK)
    lp = cells * pstride
    o_sl = 2 * fsp
    wide = up(max(atoms * pstride, lp, EDGE), 128)
    blocks = npad // BLK

    outside = (
        y_hbm, kin_hbm, scale_hbm, pot_hbm, cn_hbm, fs_hbm, fl_hbm, pr_hbm, atom_hbm, coupling_hbm
    )
    inside = (
        y_ref, kin_ref, scale_ref, pot_ref, cn_ref, fs_ref, fl_ref, pr_ref, atom_ref, coupling_ref
    )
    loads = [
        pltpu.make_async_copy(outside[i], inside[i], in_sem.at[i]) for i in range(len(outside))
    ]
    for i in (4, 5, 6, 0, 8, 9, 7, 1, 2, 3):
        loads[i].start()

    s = lax.axis_index("space")
    l = lax.axis_index("slab")
    above, below = lax.rem(s + 1, n_space), lax.rem(s + n_space - 1, n_space)
    right, left = lax.rem(l + 1, n_slab), lax.rem(l + n_slab - 1, n_slab)
    to_space, to_slab = (below, above), (left, right)
    has_space, has_slab = (s > 0, s < n_space - 1), (l > 0, l < n_slab - 1)
    corners = [(a, b) for a in range(2) for b in range(2)]

    barrier = pltpu.get_barrier_semaphore()

    def greet(exists, device):
        @pl.when(exists)
        def _():
            pl.semaphore_signal(barrier, inc=1, device_id=device, device_id_type=MESH)

        return exists.astype(jnp.int32)

    for d in range(1, n_slab):
        pl.semaphore_signal(
            barrier, inc=1, device_id={"slab": lax.rem(l + d, n_slab)}, device_id_type=MESH
        )
    greeted = n_slab - 1
    for a in range(2):
        greeted += greet(has_space[a], {"space": to_space[a]})
    for a, b in corners:
        greeted += greet(has_space[a] & has_slab[b], {"space": to_space[a], "slab": to_slab[b]})
    for a in range(2):

        @pl.when(jnp.logical_not(has_space[a]))
        def _():
            for step in range(2):
                inc[step, :, a * fsp : (a + 1) * fsp] = jnp.zeros((width, fsp), bf16)

        @pl.when(jnp.logical_not(has_slab[a]))
        def _():
            for step in range(2):
                in_slab[step, a] = jnp.zeros((width, flp), bf16)

    for a, b in corners:

        @pl.when(jnp.logical_not(has_space[a] & has_slab[b]))
        def _():
            for step in range(2):
                in_edge[step, b, :, a * EDGE : (a + 1) * EDGE] = jnp.zeros((width, EDGE), bf16)

    if fp > 2 * fsp + 2 * flp:
        for step in range(2):
            inc[step, :, 2 * fsp + 2 * flp :] = jnp.zeros((width, fp - 2 * fsp - 2 * flp), bf16)

    for i in (4, 5, 6):
        loads[i].wait()
    idx[...] = jnp.full(idx.shape, -1, jnp.int32)
    for c in range(cells):
        idx[0:1, c * op : c * op + order] = cn_ref[c : c + 1, :]
    for k in range(2):
        idx[0:1, jp + k * fsp : jp + k * fsp + fs] = fs_ref[k : k + 1, :]
        off = jp + o_sl + k * flp
        idx[0:1, off : off + fl] = fl_ref[k : k + 1, :]

    loads[0].wait()
    for b in range(blocks):
        count = min(BLK, nodes - b * BLK)
        rows = slice(b * width, (b + 1) * width)
        if count < BLK:
            yb[rows, :] = jnp.zeros((width, BLK), bf16)
        yb[rows, 0:count] = y_ref[:, b * BLK : b * BLK + count]
    lane_rows = lax.broadcasted_iota(jnp.int32, (BLK, BLK), 0).astype(f32).astype(bf16)

    def tile(start):
        if isinstance(start, int):
            return slice(start, start + BLK)
        return pl.ds(pl.multiple_of(start, BLK), BLK)

    def low_part(at):
        low = (idx[0:1, at] & (BLK - 1)).astype(f32).astype(bf16)
        hit = lane_rows == jnp.broadcast_to(low, (BLK, BLK))
        return jnp.where(hit, jnp.ones((), bf16), jnp.zeros((), bf16))

    def gather(source, at):
        every = jnp.dot(source[...], hot[:, at], preferred_element_type=f32)
        high = jnp.broadcast_to(idx[0:1, at] >> SHIFT, (width, BLK))
        got = jnp.zeros((width, BLK), f32)
        for b in range(blocks):
            got = jnp.where(high == b, every[b * width : (b + 1) * width], got)
        return got.astype(bf16)

    def spread(pieces):
        left_side, right_side = [], []
        for value, at in pieces:
            high = (idx[0:1, at] >> SHIFT).astype(f32).astype(bf16)
            high = jnp.broadcast_to(high, value.shape)
            none = jnp.zeros((), bf16)
            left_side.append(
                jnp.concatenate(
                    [jnp.where(high == jnp.full((), b, bf16), value, none) for b in range(blocks)], axis=0
                )
            )
            right_side.append(hot[:, at])
        return lax.dot_general(
            jnp.concatenate(left_side, axis=1),
            jnp.concatenate(right_side, axis=1),
            NT,
            preferred_element_type=f32,
        )

    per_cell = op // BLK
    tiles = cells * per_cell
    group = max(g for g in (1, 2, 3, 6) if tiles % g == 0)

    def take_cells(source, build):
        def body(i):
            for u in range(group):
                j = i * group + u
                at = tile(j * BLK)
                if build:
                    hot[:, at] = low_part(at)
                row = pl.ds(pl.multiple_of(j // per_cell * width, width), width)
                vals[row, tile(j % per_cell * BLK)] = gather(source, at)

        return body

    for k in range(fp // BLK):
        at = tile(jp + k * BLK)
        hot[:, at] = low_part(at)
    slab_row = idx[0:1, jp + o_sl : jp + o_sl + 2 * flp].astype(f32)
    slab_row = jnp.where(slab_row < 0, -2.0, slab_row)
    for k in range(2 * fsp // 128):
        row = idx[0:1, jp + k * 128 : jp + (k + 1) * 128].astype(f32)
        col = jnp.broadcast_to(row, (128, 128)).T
        cross[k * 128 : (k + 1) * 128, :] = jnp.where(col[:, 0:1] == slab_row, 1.0, 0.0).astype(bf16)

    loads[8].wait()
    loads[9].wait()
    lane_cell = lax.broadcasted_iota(jnp.int32, (8, lp), 1) // pstride
    atom_row = jnp.zeros((8, lp), f32)
    for c in range(cells):
        atom_row = jnp.where(lane_cell == c, atom_ref[c].astype(f32), atom_row)
    pack[...] = jnp.zeros(pack.shape, f32)
    for i in range(atoms):
        pack[0:nproj, i * pstride : i * pstride + nproj] = coupling_ref[:, i, :]
    pack[pstride : pstride + 8, 0:lp] = atom_row
    loads[7].wait()
    pp[...] = jnp.zeros(pp.shape, bf16)
    for c in range(cells):
        pp[c * pstride : c * pstride + nproj, c * op : c * op + order] = pr_ref[:, c, :]
    for i in (1, 2, 3):
        loads[i].wait()
    kin[...] = jnp.zeros(kin.shape, bf16)
    kin[0:order, 0:order] = kin_ref[...]
    pot[...] = jnp.zeros(pot.shape, f32)
    pot[0:cells, 0:order] = pot_ref[...]
    row_at = lax.broadcasted_iota(jnp.int32, (16, flp), 0)
    counts = (lax.broadcasted_iota(jnp.int32, (16, flp), 1) + 1).astype(f32)
    probe = jnp.where(row_at == 0, 1.0, jnp.where(row_at == 1, counts, 0.0)).astype(bf16)
    row_of = lax.broadcasted_iota(jnp.int32, (16, fsp), 0)
    member, place = [], []
    for b in range(2):
        seen = lax.dot_general(
            probe, cross[:, b * flp : (b + 1) * flp], NT, preferred_element_type=f32
        )
        for a in range(2):
            member.append(jnp.broadcast_to(seen[0:1, a * fsp : (a + 1) * fsp], (16, fsp)))
            place.append(jnp.broadcast_to(seen[1:2, a * fsp : (a + 1) * fsp], (16, fsp)))
    stacked = jnp.zeros((16, fsp), f32)
    for i in range(4):
        stacked = jnp.where(row_of == i, member[i], stacked)
    tri_row = lax.broadcasted_iota(jnp.int32, (fsp, fsp), 0)
    tri_col = lax.broadcasted_iota(jnp.int32, (fsp, fsp), 1)
    before = jnp.where(tri_row < tri_col, 1.0, 0.0).astype(bf16)
    rank = jnp.dot(stacked.astype(bf16), before, preferred_element_type=f32)
    edge_row = lax.broadcasted_iota(jnp.int32, (EDGE, fsp), 0).astype(f32)
    spots = jnp.zeros((8, EDGE), f32)
    spot_row = lax.broadcasted_iota(jnp.int32, (8, EDGE), 0)
    for i in range(4):
        b, a = i // 2, i % 2
        label = jnp.where(member[i][0:1] > 0.5, rank[i : i + 1], -1.0)
        picked = jnp.where(edge_row == jnp.broadcast_to(label, (EDGE, fsp)), 1.0, 0.0).astype(bf16)
        ct[a, b * EDGE : (b + 1) * EDGE, :] = picked
        listed = lax.dot_general(place[i].astype(bf16), picked, NT, preferred_element_type=f32)
        spots = jnp.where(spot_row == i, listed[0:8], spots)
    pack[pstride + 8 :, 0:EDGE] = spots

    pl.loop(0, 1)(take_cells(yb, True))
    pl.semaphore_wait(barrier, greeted)
    pack_copies = []
    for d in range(1, n_slab):
        copy = pltpu.make_async_remote_copy(
            src_ref=pack,
            dst_ref=packs.at[d - 1],
            send_sem=pack_send.at[d - 1],
            recv_sem=pack_recv.at[d - 1],
            device_id={"slab": lax.rem(l + d, n_slab)},
            device_id_type=MESH,
        )
        copy.start()
        pack_copies.append(copy)

    pl.loop(1, tiles // group)(take_cells(yb, True))

    def margin_of(step):
        margin = jnp.zeros((width, lp), f32)
        if step == 0:
            for c in range(cells):
                margin += lax.dot_general(
                    vals[c * width : (c + 1) * width, :],
                    pp[:, c * op : (c + 1) * op],
                    NT,
                    preferred_element_type=f32,
                )
        else:
            for b in range(blocks):
                margin += lax.dot_general(
                    yb[b * width : (b + 1) * width, :],
                    pn[b * lp : (b + 1) * lp, :],
                    NT,
                    preferred_element_type=f32,
                )
        marg[step, 0] = margin
        return margin

    def send_margin(step):
        copies = []
        for d in range(1, n_slab):
            copy = pltpu.make_async_remote_copy(
                src_ref=marg.at[step, 0],
                dst_ref=marg.at[step, d],
                send_sem=marg_send.at[step, d - 1],
                recv_sem=marg_recv.at[step, d - 1],
                device_id={"slab": lax.rem(l + d, n_slab)},
                device_id_type=MESH,
            )
            copy.start()
            copies.append(copy)
        return copies

    def local_part():
        kinv[...] = jnp.dot(vals[...], kin[...], preferred_element_type=f32)
        for c in range(cells):
            rows = slice(c * width, (c + 1) * width)
            total = scale_ref[c] * kinv[rows, :] + pot[c : c + 1, :] * vals[rows, :].astype(f32)
            tot[rows, :] = total.astype(bf16)

    def scatter(step):
        pair = 2 if cells % 2 == 0 else 1

        def one(c):
            row = pl.multiple_of(c * width, width)
            low = pl.multiple_of(c * pstride, pstride)
            pieces = []
            for n in range(per_cell):
                at = tile(c * op + n * BLK)
                value = tot[pl.ds(row, width), tile(n * BLK)]
                if step == 0:
                    value = jnp.concatenate([value, pp[pl.ds(low, pstride), at]], axis=0)
                pieces.append((value, at))
            result = spread(pieces)
            each = width if step else width + pstride
            for b in range(blocks):
                rows = slice(b * width, (b + 1) * width)
                asm[rows, :] += result[b * each : b * each + width]
                if step == 0:
                    to = pl.ds(b * lp + low, pstride)
                    pn[to, :] = result[b * each + width : (b + 1) * each].astype(bf16)

        asm[...] = jnp.zeros(asm.shape, f32)

        @pl.loop(0, cells // pair)
        def _(c):
            for u in range(pair):
                one(pair * c + u)

    margin_of(0)
    marg_copies = send_margin(0)
    local_part()
    def use_packs():
        for copy in pack_copies:
            copy.wait()
        own_row = pack[pstride : pstride + 1, 0:lp]
        own_col = jnp.broadcast_to(own_row, (lp, lp)).T
        segment = lax.broadcasted_iota(jnp.int32, (pstride, wide), 1) // pstride
        chosen = jnp.zeros((lp, lp), f32)
        for d in range(n_slab):
            source = lax.rem(l + n_slab - d, n_slab)
            table = pack[0:pstride, :] if d == 0 else packs[d - 1, 0:pstride, :]
            for i in range(atoms):
                once = jnp.where(segment == i, table, 0.0)
                many = once
                for c in range(cells):
                    if c != i:
                        many = many + pltpu.roll(once, (c - i) * pstride % wide, 1)
                tiled = jnp.concatenate([many[:, 0:lp]] * cells, axis=0)
                chosen += jnp.where(own_col == (source * atoms + i).astype(f32), tiled, 0.0)
        for d in range(n_slab):
            last = slice(pstride, pstride + 1)
            row = pack[last, 0:lp] if d == 0 else packs[d - 1, last, 0:lp]
            used = jnp.where(own_col == row, chosen, 0.0)
            high = used.astype(bf16)
            coup[d, :, 0:lp] = high
            coup[d, :, lp : 2 * lp] = high
            coup[d, :, 2 * lp : 3 * lp] = (used - high.astype(f32)).astype(bf16)
        slot = lax.broadcasted_iota(jnp.int32, (flp, EDGE), 0).astype(f32) + 1.0
        for b in range(2):
            d = 1 if b == 0 else n_slab - 1
            for a in range(2):
                at = pstride + 8 + (1 - b) * 2 + a
                row = packs[max(d - 1, 0), at : at + 1, 0:EDGE]
                spot[b, :, a * EDGE : (a + 1) * EDGE] = jnp.where(
                    slot == jnp.broadcast_to(row, (flp, EDGE)), 1.0, 0.0
                ).astype(bf16)

    def exchange(step):
        moves = []

        def move(sends, gets, source, target, out_sem, in_sem, device):
            copy = pltpu.make_async_remote_copy(
                src_ref=source,
                dst_ref=target,
                send_sem=out_sem,
                recv_sem=in_sem,
                device_id=device,
                device_id_type=MESH,
            )
            pl.when(sends)(copy.start)
            moves.append((sends, gets, copy))

        cut = up(o_sl, BLK)
        take_faces(step, 0, cut)
        for a in range(2):
            seg = slice(a * fsp, (a + 1) * fsp)
            other = slice((1 - a) * fsp, (2 - a) * fsp)
            move(
                has_space[a],
                has_space[1 - a],
                outg.at[step, :, seg],
                inc.at[step, :, other],
                face_send.at[step, a],
                face_recv.at[step, a],
                {"space": to_space[a]},
            )
        for a in range(2):
            edge_send[step, a] = lax.dot_general(
                outg[step, :, a * fsp : (a + 1) * fsp], ct[a], NT, preferred_element_type=f32
            ).astype(bf16)
        for a, b in corners:
            move(
                has_space[a] & has_slab[b],
                has_space[1 - a] & has_slab[1 - b],
                edge_send.at[step, a, :, b * EDGE : (b + 1) * EDGE],
                in_edge.at[step, 1 - b, :, (1 - a) * EDGE : (2 - a) * EDGE],
                edge_sem.at[step, 2 * a + b],
                edge_got.at[step, 2 * a + b],
                {"space": to_space[a], "slab": to_slab[b]},
            )
        take_faces(step, cut, fp)
        for b in range(2):
            move(
                has_slab[b],
                has_slab[1 - b],
                outg.at[step, :, o_sl + b * flp : o_sl + (b + 1) * flp],
                in_slab.at[step, 1 - b],
                face_send.at[step, 2 + b],
                face_recv.at[step, 2 + b],
                {"slab": to_slab[b]},
            )
        return moves

    def finish(step, moves):
        for sends, gets, copy in moves:
            pl.when(gets)(copy.wait_recv)
        for sends, gets, copy in moves:
            pl.when(sends)(copy.wait_send)
        for b in range(2):
            part = slice(o_sl + b * flp, o_sl + (b + 1) * flp)
            corner = lax.dot_general(in_edge[step, b], spot[b], NT, preferred_element_type=f32)
            inc[step, :, part] = (in_slab[step, b].astype(f32) + corner).astype(bf16)
        return spread([(inc[step, :, tile(k * BLK)], tile(jp + k * BLK)) for k in range(fp // BLK)])

    def take_faces(step, first, last):
        for k in range(first // BLK, last // BLK):
            outg[step, :, tile(k * BLK)] = gather(yb, tile(jp + k * BLK))

    for step in range(2):
        if step == 1:
            margin_of(1)
            marg_copies = send_margin(1)
            pl.loop(0, tiles // group)(take_cells(yb, False))
            local_part()
        scatter(step)

        if step == 0:
            use_packs()
        coupled = jnp.zeros((width, lp), f32)
        for d in range(n_slab):
            if d > 0:
                marg_copies[d - 1].wait()
            whole = marg[step, d]
            high = whole.astype(bf16)
            low = (whole - high.astype(f32)).astype(bf16)
            coupled += lax.dot_general(
                jnp.concatenate([high, low, high], axis=1), coup[d], NT, preferred_element_type=f32
            )
        coupled = coupled.astype(bf16)
        for b in range(blocks):
            rows = slice(b * width, (b + 1) * width)
            whole = asm[rows, :] + jnp.dot(
                coupled, pn[b * lp : (b + 1) * lp, :], preferred_element_type=f32
            )
            asm[rows, :] = whole
            yb[rows, :] = whole.astype(bf16)

        moves = exchange(step)

        if step == 0:
            for b in range(blocks):
                rows = slice(b * width, (b + 1) * width)
                count = min(BLK, nodes - b * BLK)
                field[rows, 0:count] = asm[rows, 0:count] - filter_centre * y_ref[
                    :, b * BLK : b * BLK + count
                ].astype(f32)
                if count < BLK:
                    field[rows, count:] = jnp.zeros((width, BLK - count), f32)
            fresh = (field[...] + finish(step, moves)) / filter_half
            field[...] = fresh
            yb[...] = fresh.astype(bf16)
        else:
            for b in range(blocks):
                rows = slice(b * width, (b + 1) * width)
                count = min(BLK, nodes - b * BLK)
                start = y_ref[:, b * BLK : b * BLK + count].astype(f32)
                asm[rows, 0:count] = (
                    2.0 / filter_half * asm[rows, 0:count]
                    - 2.0 * filter_centre / filter_half * field[rows, 0:count]
                    - start
                )
            added = finish(step, moves)
            for b in range(blocks):
                rows = slice(b * width, (b + 1) * width)
                count = min(BLK, nodes - b * BLK)
                out_ref[:, b * BLK : b * BLK + count] = (
                    asm[rows, 0:count] + 2.0 / filter_half * added[rows, 0:count]
                )


def shards(
    wavefunctions,
    kinetic,
    cell_scale,
    potential,
    cell_nodes,
    face_space,
    face_slab,
    projectors,
    cell_atom,
    coupling,
):
    width, nodes = wavefunctions.shape
    cells, order = cell_nodes.shape
    atoms, nproj = coupling.shape[0], coupling.shape[1]
    n_space, n_slab = lax.axis_size("space"), lax.axis_size("slab")
    fs, fl = face_space.shape[1], face_slab.shape[1]
    pstride = up(nproj, 16)
    while cells * pstride % 128:
        pstride += 16
    dims = dict(
        n_space=n_space, n_slab=n_slab, width=width, nodes=nodes, cells=cells, order=order,
        atoms=atoms, nproj=nproj, pstride=pstride, fs=fs, fl=fl,
    )
    op, npad = up(order, BLK), up(nodes, BLK)
    fsp, flp = up(fs, 128), up(fl, 128)
    jp = cells * op
    fp = up(2 * fsp + 2 * flp, BLK)
    lp = cells * pstride
    others = max(n_slab - 1, 1)
    wide = up(max(atoms * pstride, lp, EDGE), 128)
    vmem = pl.BlockSpec(memory_space=pltpu.VMEM)
    dma = pltpu.SemaphoreType.DMA
    return pl.pallas_call(
        functools.partial(kernel, dims),
        out_shape=pltpu.VMEM((width, nodes), f32),
        in_specs=[pl.BlockSpec(memory_space=pl.ANY)] * 10,
        out_specs=vmem,
        scratch_shapes=[
            pltpu.VMEM((width, nodes), bf16),
            pltpu.VMEM((order, order), bf16),
            pltpu.SMEM((cells,), f32),
            pltpu.VMEM((cells, order), f32),
            pltpu.VMEM((cells, order), jnp.int32),
            pltpu.VMEM((2, fs), jnp.int32),
            pltpu.VMEM((2, fl), jnp.int32),
            pltpu.VMEM((nproj, cells, order), bf16),
            pltpu.SMEM((cells,), jnp.int32),
            pltpu.VMEM((nproj, atoms, nproj), f32),
            dma((10,)),
            pltpu.VMEM((BLK, jp + fp), bf16),
            pltpu.VMEM((pstride + 16, wide), f32),
            pltpu.VMEM((8, jp + fp), jnp.int32),
            pltpu.VMEM((op, op), bf16),
            pltpu.VMEM((lp, jp), bf16),
            pltpu.VMEM((up(cells, 8), op), f32),
            pltpu.VMEM((2 * fsp, 2 * flp), bf16),
            pltpu.VMEM((others, pstride + 16, wide), f32),
            pltpu.VMEM((n_slab, lp, 3 * lp), bf16),
            pltpu.VMEM((npad // BLK * width, BLK), bf16),
            pltpu.VMEM((cells * width, op), bf16),
            pltpu.VMEM((cells * width, op), f32),
            pltpu.VMEM((cells * width, op), bf16),
            pltpu.VMEM((npad // BLK * width, BLK), f32),
            pltpu.VMEM((npad // BLK * width, BLK), f32),
            pltpu.VMEM((2, width, fp), bf16),
            pltpu.VMEM((2, 2, width, flp), bf16),
            pltpu.VMEM((2, width, fp), bf16),
            pltpu.VMEM((2, n_slab, width, lp), f32),
            pltpu.VMEM((npad // BLK * lp, BLK), bf16),
            pltpu.VMEM((2, 2 * EDGE, fsp), bf16),
            pltpu.VMEM((2, flp, 2 * EDGE), bf16),
            pltpu.VMEM((2, 2, width, 2 * EDGE), bf16),
            pltpu.VMEM((2, 2, width, 2 * EDGE), bf16),
            dma((others,)),
            dma((others,)),
            dma((2, others)),
            dma((2, others)),
            dma((2, 4)),
            dma((2, 4)),
            dma((2, 4)),
            dma((2, 4)),
        ],
        compiler_params=pltpu.CompilerParams(
            collective_id=0, has_side_effects=True, vmem_limit_bytes=60 * 1024 * 1024
        ),
    )(
        wavefunctions, kinetic, cell_scale, potential, cell_nodes, face_space, face_slab,
        projectors.transpose(1, 0, 2), cell_atom, coupling.transpose(1, 0, 2),
    )


def solution(mesh):
    placed = (
        P(None, ("space", "slab")),
        P(),
        P(("space", "slab")),
        P(("space", "slab"), None),
        P(("space", "slab"), None),
        P(("space", "slab"), None),
        P(("space", "slab"), None),
        P(("space", "slab"), None, None),
        P(("space", "slab")),
        P(("space", "slab"), None, None),
    )
    return jax.shard_map(
        shards, mesh=mesh, in_specs=placed, out_specs=P(None, ("space", "slab")), check_vma=False
    )
```

```python
import functools

import jax
import jax.numpy as jnp
from jax import lax
from jax.experimental import pallas as pl
from jax.experimental.pallas import tpu as pltpu
from jax.sharding import PartitionSpec as P

filter_centre = 8.0
filter_half = 8.0
BLK = 256
SHIFT = 8
EDGE = 128
MESH = pl.DeviceIdType.MESH
NT = (((1,), (1,)), ((), ()))
f32 = jnp.float32
bf16 = jnp.bfloat16


def up(value, unit):
    return -(-value // unit) * unit


def kernel(
    dims,
    y_hbm,
    kin_hbm,
    scale_hbm,
    pot_hbm,
    cn_hbm,
    fs_hbm,
    fl_hbm,
    pr_hbm,
    atom_hbm,
    coupling_hbm,
    out_ref,
    y_ref,
    kin_ref,
    scale_ref,
    pot_ref,
    cn_ref,
    fs_ref,
    fl_ref,
    pr_ref,
    atom_ref,
    coupling_ref,
    in_sem,
    hot,
    pack,
    idx,
    kin,
    pp,
    pot,
    cross,
    packs,
    coup,
    yb,
    vals,
    kinv,
    tot,
    asm,
    field,
    origin,
    outg,
    in_slab,
    inc,
    marg,
    pn,
    ct,
    spot,
    edge_send,
    in_edge,
    pack_send,
    pack_recv,
    marg_send,
    marg_recv,
    face_send,
    face_recv,
    edge_sem,
    edge_got,
):
    n_space, n_slab = dims["n_space"], dims["n_slab"]
    width, nodes, cells, order = dims["width"], dims["nodes"], dims["cells"], dims["order"]
    atoms, nproj, pstride = dims["atoms"], dims["nproj"], dims["pstride"]
    fs, fl = dims["fs"], dims["fl"]
    op, npad = up(order, BLK), up(nodes, BLK)
    fsp, flp = up(fs, 128), up(fl, 128)
    jp = cells * op
    fp = up(2 * fsp + 2 * flp, BLK)
    lp = cells * pstride
    o_sl = 2 * fsp
    wide = up(max(atoms * pstride, lp, EDGE), 128)
    blocks = npad // BLK

    outside = (
        y_hbm, kin_hbm, scale_hbm, pot_hbm, cn_hbm, fs_hbm, fl_hbm, pr_hbm, atom_hbm, coupling_hbm
    )
    inside = (
        y_ref, kin_ref, scale_ref, pot_ref, cn_ref, fs_ref, fl_ref, pr_ref, atom_ref, coupling_ref
    )
    loads = [
        pltpu.make_async_copy(outside[i], inside[i], in_sem.at[i]) for i in range(len(outside))
    ]
    for i in (4, 5, 6, 0, 8, 9, 7, 1, 2, 3):
        loads[i].start()

    s = lax.axis_index("space")
    l = lax.axis_index("slab")
    above, below = lax.rem(s + 1, n_space), lax.rem(s + n_space - 1, n_space)
    right, left = lax.rem(l + 1, n_slab), lax.rem(l + n_slab - 1, n_slab)
    to_space, to_slab = (below, above), (left, right)
    has_space, has_slab = (s > 0, s < n_space - 1), (l > 0, l < n_slab - 1)
    corners = [(a, b) for a in range(2) for b in range(2)]

    barrier = pltpu.get_barrier_semaphore()

    def greet(exists, device):
        @pl.when(exists)
        def _():
            pl.semaphore_signal(barrier, inc=1, device_id=device, device_id_type=MESH)

        return exists.astype(jnp.int32)

    for d in range(1, n_slab):
        pl.semaphore_signal(
            barrier, inc=1, device_id={"slab": lax.rem(l + d, n_slab)}, device_id_type=MESH
        )
    greeted = n_slab - 1
    for a in range(2):
        greeted += greet(has_space[a], {"space": to_space[a]})
    for a, b in corners:
        greeted += greet(has_space[a] & has_slab[b], {"space": to_space[a], "slab": to_slab[b]})
    for a in range(2):

        @pl.when(jnp.logical_not(has_space[a]))
        def _():
            for step in range(2):
                inc[step, :, a * fsp : (a + 1) * fsp] = jnp.zeros((width, fsp), bf16)

        @pl.when(jnp.logical_not(has_slab[a]))
        def _():
            for step in range(2):
                in_slab[step, a] = jnp.zeros((width, flp), bf16)

    for a, b in corners:

        @pl.when(jnp.logical_not(has_space[a] & has_slab[b]))
        def _():
            for step in range(2):
                in_edge[step, b, :, a * EDGE : (a + 1) * EDGE] = jnp.zeros((width, EDGE), bf16)

    if fp > 2 * fsp + 2 * flp:
        for step in range(2):
            inc[step, :, 2 * fsp + 2 * flp :] = jnp.zeros((width, fp - 2 * fsp - 2 * flp), bf16)

    for i in (4, 5, 6):
        loads[i].wait()
    idx[...] = jnp.full(idx.shape, -1, jnp.int32)
    for c in range(cells):
        idx[0:1, c * op : c * op + order] = cn_ref[c : c + 1, :]
    for k in range(2):
        idx[0:1, jp + k * fsp : jp + k * fsp + fs] = fs_ref[k : k + 1, :]
        off = jp + o_sl + k * flp
        idx[0:1, off : off + fl] = fl_ref[k : k + 1, :]

    loads[0].wait()
    for b in range(blocks):
        count = min(BLK, nodes - b * BLK)
        rows = slice(b * width, (b + 1) * width)
        if count < BLK:
            yb[rows, :] = jnp.zeros((width, BLK), bf16)
        yb[rows, 0:count] = y_ref[:, b * BLK : b * BLK + count]
    lane_rows = lax.broadcasted_iota(jnp.int32, (BLK, BLK), 0).astype(f32).astype(bf16)

    def tile(start):
        if isinstance(start, int):
            return slice(start, start + BLK)
        return pl.ds(pl.multiple_of(start, BLK), BLK)

    def low_part(at):
        low = (idx[0:1, at] & (BLK - 1)).astype(f32).astype(bf16)
        hit = lane_rows == jnp.broadcast_to(low, (BLK, BLK))
        return jnp.where(hit, jnp.ones((), bf16), jnp.zeros((), bf16))

    def gather(source, at):
        every = jnp.dot(source[...], hot[:, at], preferred_element_type=f32)
        high = jnp.broadcast_to(idx[0:1, at] >> SHIFT, (width, BLK))
        got = jnp.zeros((width, BLK), f32)
        for b in range(blocks):
            got = jnp.where(high == b, every[b * width : (b + 1) * width], got)
        return got.astype(bf16)

    def spread(pieces):
        left_side, right_side = [], []
        for value, at in pieces:
            high = (idx[0:1, at] >> SHIFT).astype(f32).astype(bf16)
            high = jnp.broadcast_to(high, value.shape)
            none = jnp.zeros((), bf16)
            left_side.append(
                jnp.concatenate(
                    [jnp.where(high == jnp.full((), b, bf16), value, none) for b in range(blocks)], axis=0
                )
            )
            right_side.append(hot[:, at])
        return lax.dot_general(
            jnp.concatenate(left_side, axis=1),
            jnp.concatenate(right_side, axis=1),
            NT,
            preferred_element_type=f32,
        )

    per_cell = op // BLK
    tiles = cells * per_cell
    group = max(g for g in range(1, 13) if tiles % g == 0)

    def take_cells(source):
        def body(i):
            for u in range(group):
                j = i * group + u
                at = tile(j * BLK)
                row = pl.ds(pl.multiple_of(j // per_cell * width, width), width)
                vals[row, tile(j % per_cell * BLK)] = gather(source, at)

        return body

    @pl.loop(0, cells)
    def _(k):
        for u in range(per_cell):
            at = tile((per_cell * k + u) * BLK)
            hot[:, at] = low_part(at)

    for k in range(fp // BLK):
        hot[:, tile(jp + k * BLK)] = low_part(tile(jp + k * BLK))

    slab_row = idx[0:1, jp + o_sl : jp + o_sl + 2 * flp].astype(f32)
    slab_row = jnp.where(slab_row < 0, -2.0, slab_row)
    for k in range(2 * fsp // 128):
        row = idx[0:1, jp + k * 128 : jp + (k + 1) * 128].astype(f32)
        col = jnp.broadcast_to(row, (128, 128)).T
        cross[k * 128 : (k + 1) * 128, :] = jnp.where(col[:, 0:1] == slab_row, 1.0, 0.0).astype(bf16)

    loads[8].wait()
    loads[9].wait()
    lane_cell = lax.broadcasted_iota(jnp.int32, (8, lp), 1) // pstride
    atom_row = jnp.zeros((8, lp), f32)
    for c in range(cells):
        atom_row = jnp.where(lane_cell == c, atom_ref[c].astype(f32), atom_row)
    pack[...] = jnp.zeros(pack.shape, f32)
    for i in range(atoms):
        pack[0:nproj, i * pstride : i * pstride + nproj] = coupling_ref[:, i, :]
    pack[pstride : pstride + 8, 0:lp] = atom_row
    loads[7].wait()
    pp[...] = jnp.zeros(pp.shape, bf16)
    for c in range(cells):
        pp[c * pstride : c * pstride + nproj, c * op : c * op + order] = pr_ref[:, c, :]
    for i in (1, 2, 3):
        loads[i].wait()
    origin[...] = yb[...]
    field[...] = yb[...].astype(f32)
    kin[...] = jnp.zeros(kin.shape, bf16)
    kin[0:order, 0:order] = kin_ref[...]
    pot[...] = jnp.zeros(pot.shape, f32)
    pot[0:cells, 0:order] = pot_ref[...]
    row_at = lax.broadcasted_iota(jnp.int32, (16, flp), 0)
    counts = (lax.broadcasted_iota(jnp.int32, (16, flp), 1) + 1).astype(f32)
    probe = jnp.where(row_at == 0, 1.0, jnp.where(row_at == 1, counts, 0.0)).astype(bf16)
    row_of = lax.broadcasted_iota(jnp.int32, (16, fsp), 0)
    member, place = [], []
    for b in range(2):
        seen = lax.dot_general(
            probe, cross[:, b * flp : (b + 1) * flp], NT, preferred_element_type=f32
        )
        for a in range(2):
            member.append(jnp.broadcast_to(seen[0:1, a * fsp : (a + 1) * fsp], (16, fsp)))
            place.append(jnp.broadcast_to(seen[1:2, a * fsp : (a + 1) * fsp], (16, fsp)))
    stacked = jnp.zeros((16, fsp), f32)
    for i in range(4):
        stacked = jnp.where(row_of == i, member[i], stacked)
    tri_row = lax.broadcasted_iota(jnp.int32, (fsp, fsp), 0)
    tri_col = lax.broadcasted_iota(jnp.int32, (fsp, fsp), 1)
    before = jnp.where(tri_row < tri_col, 1.0, 0.0).astype(bf16)
    rank = jnp.dot(stacked.astype(bf16), before, preferred_element_type=f32)
    edge_row = lax.broadcasted_iota(jnp.int32, (EDGE, fsp), 0).astype(f32)
    spots = jnp.zeros((8, EDGE), f32)
    spot_row = lax.broadcasted_iota(jnp.int32, (8, EDGE), 0)
    for i in range(4):
        b, a = i // 2, i % 2
        label = jnp.where(member[i][0:1] > 0.5, rank[i : i + 1], -1.0)
        picked = jnp.where(edge_row == jnp.broadcast_to(label, (EDGE, fsp)), 1.0, 0.0).astype(bf16)
        ct[a, b * EDGE : (b + 1) * EDGE, :] = picked
        listed = lax.dot_general(place[i].astype(bf16), picked, NT, preferred_element_type=f32)
        spots = jnp.where(spot_row == i, listed[0:8], spots)
    pack[pstride + 8 :, 0:EDGE] = spots

    pl.semaphore_wait(barrier, greeted)
    pack_copies = []
    for d in range(1, n_slab):
        copy = pltpu.make_async_remote_copy(
            src_ref=pack,
            dst_ref=packs.at[d - 1],
            send_sem=pack_send.at[d - 1],
            recv_sem=pack_recv.at[d - 1],
            device_id={"slab": lax.rem(l + d, n_slab)},
            device_id_type=MESH,
        )
        copy.start()
        pack_copies.append(copy)

    def margin_of(step, first):
        margin = jnp.zeros((width, lp), f32)
        if first:
            for c in range(cells):
                margin += lax.dot_general(
                    vals[c * width : (c + 1) * width, :],
                    pp[:, c * op : (c + 1) * op],
                    NT,
                    preferred_element_type=f32,
                )
        else:
            for b in range(blocks):
                margin += lax.dot_general(
                    yb[b * width : (b + 1) * width, :],
                    pn[b * lp : (b + 1) * lp, :],
                    NT,
                    preferred_element_type=f32,
                )
        marg[step, 0] = margin

    def margin_copies(step):
        copies = []
        for d in range(1, n_slab):
            copy = pltpu.make_async_remote_copy(
                src_ref=marg.at[step, 0],
                dst_ref=marg.at[step, d],
                send_sem=marg_send.at[step, d - 1],
                recv_sem=marg_recv.at[step, d - 1],
                device_id={"slab": lax.rem(l + d, n_slab)},
                device_id_type=MESH,
            )
            copies.append(copy)
        return copies

    def local_part():
        kinv[...] = jnp.dot(vals[...], kin[...], preferred_element_type=f32)
        for c in range(cells):
            rows = slice(c * width, (c + 1) * width)
            total = scale_ref[c] * kinv[rows, :] + pot[c : c + 1, :] * vals[rows, :].astype(f32)
            tot[rows, :] = total.astype(bf16)

    def scatter():
        pair = max(g for g in range(1, 5) if cells % g == 0)

        def one(c):
            row = pl.multiple_of(c * width, width)
            pieces = []
            for n in range(per_cell):
                value = tot[pl.ds(row, width), tile(n * BLK)]
                pieces.append((value, tile(c * op + n * BLK)))
            asm[...] += spread(pieces)

        asm[...] = jnp.zeros(asm.shape, f32)

        @pl.loop(0, cells // pair)
        def _(c):
            for u in range(pair):
                one(pair * c + u)

    def place_projectors():
        turn = 2 if cells % 2 == 0 else 1

        @pl.loop(0, cells // turn)
        def _(h):
            for u in range(turn):
                c = h * turn + u
                row = pl.ds(pl.multiple_of(c * pstride, pstride), pstride)
                placed = spread(
                    [(pp[row, tile(c * op + n * BLK)], tile(c * op + n * BLK)) for n in range(per_cell)]
                ).astype(bf16)
                for b in range(blocks):
                    to = pl.ds(pl.multiple_of(b * lp + c * pstride, pstride), pstride)
                    pn[to, :] = placed[b * pstride : (b + 1) * pstride]

    def use_packs():
        for copy in pack_copies:
            copy.wait()
        own_row = pack[pstride : pstride + 1, 0:lp]
        own_col = jnp.broadcast_to(own_row, (lp, lp)).T
        segment = lax.broadcasted_iota(jnp.int32, (pstride, wide), 1) // pstride
        chosen = jnp.zeros((lp, lp), f32)
        for d in range(n_slab):
            source = lax.rem(l + n_slab - d, n_slab)
            table = pack[0:pstride, :] if d == 0 else packs[d - 1, 0:pstride, :]
            for i in range(atoms):
                once = jnp.where(segment == i, table, 0.0)
                many = once
                for c in range(cells):
                    if c != i:
                        many = many + pltpu.roll(once, (c - i) * pstride % wide, 1)
                tiled = jnp.concatenate([many[:, 0:lp]] * cells, axis=0)
                chosen += jnp.where(own_col == (source * atoms + i).astype(f32), tiled, 0.0)
        for d in range(n_slab):
            last = slice(pstride, pstride + 1)
            row = pack[last, 0:lp] if d == 0 else packs[d - 1, last, 0:lp]
            used = jnp.where(own_col == row, chosen, 0.0)
            high = used.astype(bf16)
            coup[d, :, 0:lp] = high
            coup[d, :, lp : 2 * lp] = high
            coup[d, :, 2 * lp : 3 * lp] = (used - high.astype(f32)).astype(bf16)
        slot = lax.broadcasted_iota(jnp.int32, (flp, EDGE), 0).astype(f32) + 1.0
        for b in range(2):
            d = 1 if b == 0 else n_slab - 1
            for a in range(2):
                at = pstride + 8 + (1 - b) * 2 + a
                row = packs[max(d - 1, 0), at : at + 1, 0:EDGE]
                spot[b, :, a * EDGE : (a + 1) * EDGE] = jnp.where(
                    slot == jnp.broadcast_to(row, (flp, EDGE)), 1.0, 0.0
                ).astype(bf16)

    def exchange(step):
        moves = []

        def move(sends, gets, source, target, out_sem, in_sem, device):
            copy = pltpu.make_async_remote_copy(
                src_ref=source,
                dst_ref=target,
                send_sem=out_sem,
                recv_sem=in_sem,
                device_id=device,
                device_id_type=MESH,
            )
            pl.when(sends)(copy.start)
            moves.append((sends, gets, copy))

        cut = up(o_sl, BLK)
        take_faces(step, 0, cut)
        for a in range(2):
            seg = slice(a * fsp, (a + 1) * fsp)
            other = slice((1 - a) * fsp, (2 - a) * fsp)
            move(
                has_space[a],
                has_space[1 - a],
                outg.at[step, :, seg],
                inc.at[step, :, other],
                face_send.at[step, a],
                face_recv.at[step, a],
                {"space": to_space[a]},
            )
        for a in range(2):
            edge_send[step, a] = lax.dot_general(
                outg[step, :, a * fsp : (a + 1) * fsp], ct[a], NT, preferred_element_type=f32
            ).astype(bf16)
        for a, b in corners:
            move(
                has_space[a] & has_slab[b],
                has_space[1 - a] & has_slab[1 - b],
                edge_send.at[step, a, :, b * EDGE : (b + 1) * EDGE],
                in_edge.at[step, 1 - b, :, (1 - a) * EDGE : (2 - a) * EDGE],
                edge_sem.at[step, 2 * a + b],
                edge_got.at[step, 2 * a + b],
                {"space": to_space[a], "slab": to_slab[b]},
            )
        take_faces(step, cut, fp)
        for b in range(2):
            move(
                has_slab[b],
                has_slab[1 - b],
                outg.at[step, :, o_sl + b * flp : o_sl + (b + 1) * flp],
                in_slab.at[step, 1 - b],
                face_send.at[step, 2 + b],
                face_recv.at[step, 2 + b],
                {"slab": to_slab[b]},
            )
        return moves

    def finish(step, moves):
        for sends, gets, copy in moves:
            pl.when(gets)(copy.wait_recv)
        for sends, gets, copy in moves:
            pl.when(sends)(copy.wait_send)
        for b in range(2):
            part = slice(o_sl + b * flp, o_sl + (b + 1) * flp)
            corner = lax.dot_general(in_edge[step, b], spot[b], NT, preferred_element_type=f32)
            inc[step, :, part] = (in_slab[step, b].astype(f32) + corner).astype(bf16)
        return spread([(inc[step, :, tile(k * BLK)], tile(jp + k * BLK)) for k in range(fp // BLK)])

    def take_faces(step, first, last):
        for k in range(first // BLK, last // BLK):
            outg[step, :, tile(k * BLK)] = gather(yb, tile(jp + k * BLK))

    @pl.loop(0, 2)
    def _(step):
        marg_copies = margin_copies(step)
        later = (step > 0).astype(f32)

        @pl.when(step > 0)
        def _():
            margin_of(step, False)
            for copy in marg_copies:
                copy.start()

        pl.loop(0, tiles // group)(take_cells(yb))

        @pl.when(step == 0)
        def _():
            margin_of(step, True)
            for copy in marg_copies:
                copy.start()

        local_part()

        scatter()

        @pl.when(step == 0)
        def _():
            place_projectors()
            use_packs()

        coupled = jnp.zeros((width, lp), f32)
        for d in range(n_slab):
            if d > 0:
                marg_copies[d - 1].wait()
            whole = marg[step, d]
            high = whole.astype(bf16)
            low = (whole - high.astype(f32)).astype(bf16)
            coupled += lax.dot_general(
                jnp.concatenate([high, low, high], axis=1), coup[d], NT, preferred_element_type=f32
            )
        coupled = coupled.astype(bf16)
        for b in range(blocks):
            rows = slice(b * width, (b + 1) * width)
            whole = asm[rows, :] + jnp.dot(
                coupled, pn[b * lp : (b + 1) * lp, :], preferred_element_type=f32
            )
            asm[rows, :] = whole
            yb[rows, :] = whole.astype(bf16)

        moves = exchange(step)
        gain = (1.0 + later) / filter_half
        asm[...] = (
            gain * asm[...]
            - gain * filter_centre * field[...]
            - later * origin[...].astype(f32)
        )
        fresh = asm[...] + gain * finish(step, moves)
        field[...] = fresh
        yb[...] = fresh.astype(bf16)

    for b in range(blocks):
        count = min(BLK, nodes - b * BLK)
        out_ref[:, b * BLK : b * BLK + count] = field[b * width : (b + 1) * width, 0:count]


def shards(
    wavefunctions,
    kinetic,
    cell_scale,
    potential,
    cell_nodes,
    face_space,
    face_slab,
    projectors,
    cell_atom,
    coupling,
):
    width, nodes = wavefunctions.shape
    cells, order = cell_nodes.shape
    atoms, nproj = coupling.shape[0], coupling.shape[1]
    n_space, n_slab = lax.axis_size("space"), lax.axis_size("slab")
    fs, fl = face_space.shape[1], face_slab.shape[1]
    pstride = up(nproj, 16)
    while cells * pstride % 128:
        pstride += 16
    dims = dict(
        n_space=n_space, n_slab=n_slab, width=width, nodes=nodes, cells=cells, order=order,
        atoms=atoms, nproj=nproj, pstride=pstride, fs=fs, fl=fl,
    )
    op, npad = up(order, BLK), up(nodes, BLK)
    fsp, flp = up(fs, 128), up(fl, 128)
    jp = cells * op
    fp = up(2 * fsp + 2 * flp, BLK)
    lp = cells * pstride
    others = max(n_slab - 1, 1)
    wide = up(max(atoms * pstride, lp, EDGE), 128)
    vmem = pl.BlockSpec(memory_space=pltpu.VMEM)
    dma = pltpu.SemaphoreType.DMA
    return pl.pallas_call(
        functools.partial(kernel, dims),
        out_shape=pltpu.VMEM((width, nodes), f32),
        in_specs=[pl.BlockSpec(memory_space=pl.ANY)] * 10,
        out_specs=vmem,
        scratch_shapes=[
            pltpu.VMEM((width, nodes), bf16),
            pltpu.VMEM((order, order), bf16),
            pltpu.SMEM((cells,), f32),
            pltpu.VMEM((cells, order), f32),
            pltpu.VMEM((cells, order), jnp.int32),
            pltpu.VMEM((2, fs), jnp.int32),
            pltpu.VMEM((2, fl), jnp.int32),
            pltpu.VMEM((nproj, cells, order), bf16),
            pltpu.SMEM((cells,), jnp.int32),
            pltpu.VMEM((nproj, atoms, nproj), f32),
            dma((10,)),
            pltpu.VMEM((BLK, jp + fp), bf16),
            pltpu.VMEM((pstride + 16, wide), f32),
            pltpu.VMEM((8, jp + fp), jnp.int32),
            pltpu.VMEM((op, op), bf16),
            pltpu.VMEM((lp, jp), bf16),
            pltpu.VMEM((up(cells, 8), op), f32),
            pltpu.VMEM((2 * fsp, 2 * flp), bf16),
            pltpu.VMEM((others, pstride + 16, wide), f32),
            pltpu.VMEM((n_slab, lp, 3 * lp), bf16),
            pltpu.VMEM((npad // BLK * width, BLK), bf16),
            pltpu.VMEM((cells * width, op), bf16),
            pltpu.VMEM((cells * width, op), f32),
            pltpu.VMEM((cells * width, op), bf16),
            pltpu.VMEM((npad // BLK * width, BLK), f32),
            pltpu.VMEM((npad // BLK * width, BLK), f32),
            pltpu.VMEM((npad // BLK * width, BLK), bf16),
            pltpu.VMEM((2, width, fp), bf16),
            pltpu.VMEM((2, 2, width, flp), bf16),
            pltpu.VMEM((2, width, fp), bf16),
            pltpu.VMEM((2, n_slab, width, lp), f32),
            pltpu.VMEM((npad // BLK * lp, BLK), bf16),
            pltpu.VMEM((2, 2 * EDGE, fsp), bf16),
            pltpu.VMEM((2, flp, 2 * EDGE), bf16),
            pltpu.VMEM((2, 2, width, 2 * EDGE), bf16),
            pltpu.VMEM((2, 2, width, 2 * EDGE), bf16),
            dma((others,)),
            dma((others,)),
            dma((2, others)),
            dma((2, others)),
            dma((2, 4)),
            dma((2, 4)),
            dma((2, 4)),
            dma((2, 4)),
        ],
        compiler_params=pltpu.CompilerParams(
            collective_id=0, has_side_effects=True, vmem_limit_bytes=60 * 1024 * 1024
        ),
    )(
        wavefunctions, kinetic, cell_scale, potential, cell_nodes, face_space, face_slab,
        projectors.transpose(1, 0, 2), cell_atom, coupling.transpose(1, 0, 2),
    )


def solution(mesh):
    placed = (
        P(None, ("space", "slab")),
        P(),
        P(("space", "slab")),
        P(("space", "slab"), None),
        P(("space", "slab"), None),
        P(("space", "slab"), None),
        P(("space", "slab"), None),
        P(("space", "slab"), None, None),
        P(("space", "slab")),
        P(("space", "slab"), None, None),
    )
    return jax.shard_map(
        shards, mesh=mesh, in_specs=placed, out_specs=P(None, ("space", "slab")), check_vma=False
    )
```

```python
import functools

import jax
import jax.numpy as jnp
from jax import lax
from jax.experimental import pallas as pl
from jax.experimental.pallas import tpu as pltpu
from jax.sharding import PartitionSpec as P

filter_centre = 8.0
filter_half = 8.0
BLK = 256
SHIFT = 8
EDGE = 128
MESH = pl.DeviceIdType.MESH
NT = (((1,), (1,)), ((), ()))
f32 = jnp.float32
bf16 = jnp.bfloat16


def up(value, unit):
    return -(-value // unit) * unit


def kernel(
    dims,
    y_hbm,
    kin_hbm,
    scale_hbm,
    pot_hbm,
    cn_hbm,
    fs_hbm,
    fl_hbm,
    pr_hbm,
    atom_hbm,
    coupling_hbm,
    out_ref,
    y_ref,
    kin_ref,
    scale_ref,
    pot_ref,
    cn_ref,
    fs_ref,
    fl_ref,
    pr_ref,
    atom_ref,
    coupling_ref,
    in_sem,
    hot,
    pack,
    idx,
    kin,
    pp,
    pot,
    cross,
    packs,
    coup,
    yb,
    vals,
    kinv,
    tot,
    asm,
    field,
    origin,
    outg,
    in_slab,
    inc,
    marg,
    pn,
    ct,
    spot,
    edge_send,
    in_edge,
    pack_send,
    pack_recv,
    marg_send,
    marg_recv,
    face_send,
    face_recv,
    edge_sem,
    edge_got,
):
    n_space, n_slab = dims["n_space"], dims["n_slab"]
    width, nodes, cells, order = dims["width"], dims["nodes"], dims["cells"], dims["order"]
    atoms, nproj, pstride = dims["atoms"], dims["nproj"], dims["pstride"]
    fs, fl = dims["fs"], dims["fl"]
    op, npad = up(order, BLK), up(nodes, BLK)
    fsp, flp = up(fs, 128), up(fl, 128)
    jp = cells * op
    fp = up(2 * fsp + 2 * flp, BLK)
    lp = cells * pstride
    o_sl = 2 * fsp
    wide = up(max(atoms * pstride, lp, EDGE), 128)
    blocks = npad // BLK

    outside = (
        y_hbm, kin_hbm, scale_hbm, pot_hbm, cn_hbm, fs_hbm, fl_hbm, pr_hbm, atom_hbm, coupling_hbm
    )
    inside = (
        y_ref, kin_ref, scale_ref, pot_ref, cn_ref, fs_ref, fl_ref, pr_ref, atom_ref, coupling_ref
    )
    loads = [
        pltpu.make_async_copy(outside[i], inside[i], in_sem.at[i]) for i in range(len(outside))
    ]
    for i in (4, 5, 6, 0, 8, 9, 7, 1, 2, 3):
        loads[i].start()

    s = lax.axis_index("space")
    l = lax.axis_index("slab")
    above, below = lax.rem(s + 1, n_space), lax.rem(s + n_space - 1, n_space)
    right, left = lax.rem(l + 1, n_slab), lax.rem(l + n_slab - 1, n_slab)
    to_space, to_slab = (below, above), (left, right)
    has_space, has_slab = (s > 0, s < n_space - 1), (l > 0, l < n_slab - 1)
    corners = [(a, b) for a in range(2) for b in range(2)]

    barrier = pltpu.get_barrier_semaphore()

    def greet(exists, device):
        @pl.when(exists)
        def _():
            pl.semaphore_signal(barrier, inc=1, device_id=device, device_id_type=MESH)

        return exists.astype(jnp.int32)

    for d in range(1, n_slab):
        pl.semaphore_signal(
            barrier, inc=1, device_id={"slab": lax.rem(l + d, n_slab)}, device_id_type=MESH
        )
    greeted = n_slab - 1
    for a in range(2):
        greeted += greet(has_space[a], {"space": to_space[a]})
    for a, b in corners:
        greeted += greet(has_space[a] & has_slab[b], {"space": to_space[a], "slab": to_slab[b]})
    for a in range(2):

        @pl.when(jnp.logical_not(has_space[a]))
        def _():
            for step in range(2):
                inc[step, :, a * fsp : (a + 1) * fsp] = jnp.zeros((width, fsp), bf16)

        @pl.when(jnp.logical_not(has_slab[a]))
        def _():
            for step in range(2):
                in_slab[step, a] = jnp.zeros((width, flp), bf16)

    for a, b in corners:

        @pl.when(jnp.logical_not(has_space[a] & has_slab[b]))
        def _():
            for step in range(2):
                in_edge[step, b, :, a * EDGE : (a + 1) * EDGE] = jnp.zeros((width, EDGE), bf16)

    if fp > 2 * fsp + 2 * flp:
        for step in range(2):
            inc[step, :, 2 * fsp + 2 * flp :] = jnp.zeros((width, fp - 2 * fsp - 2 * flp), bf16)

    for i in (4, 5, 6):
        loads[i].wait()
    idx[...] = jnp.full(idx.shape, -1, jnp.int32)
    for c in range(cells):
        idx[0:1, c * op : c * op + order] = cn_ref[c : c + 1, :]
    for k in range(2):
        idx[0:1, jp + k * fsp : jp + k * fsp + fs] = fs_ref[k : k + 1, :]
        off = jp + o_sl + k * flp
        idx[0:1, off : off + fl] = fl_ref[k : k + 1, :]

    loads[0].wait()
    for b in range(blocks):
        count = min(BLK, nodes - b * BLK)
        rows = slice(b * width, (b + 1) * width)
        if count < BLK:
            yb[rows, :] = jnp.zeros((width, BLK), bf16)
        yb[rows, 0:count] = y_ref[:, b * BLK : b * BLK + count]
    lane_rows = lax.broadcasted_iota(jnp.int32, (BLK, BLK), 0).astype(f32).astype(bf16)

    def tile(start):
        if isinstance(start, int):
            return slice(start, start + BLK)
        return pl.ds(pl.multiple_of(start, BLK), BLK)

    def low_part(at):
        low = (idx[0:1, at] & (BLK - 1)).astype(f32).astype(bf16)
        hit = lane_rows == jnp.broadcast_to(low, (BLK, BLK))
        return jnp.where(hit, jnp.ones((), bf16), jnp.zeros((), bf16))

    def gather(source, at):
        every = jnp.dot(source[...], hot[:, at], preferred_element_type=f32)
        high = jnp.broadcast_to(idx[0:1, at] >> SHIFT, (width, BLK))
        got = jnp.zeros((width, BLK), f32)
        for b in range(blocks):
            got = jnp.where(high == b, every[b * width : (b + 1) * width], got)
        return got.astype(bf16)

    def spread(pieces):
        left_side, right_side = [], []
        for value, at in pieces:
            high = (idx[0:1, at] >> SHIFT).astype(f32).astype(bf16)
            high = jnp.broadcast_to(high, value.shape)
            none = jnp.zeros((), bf16)
            left_side.append(
                jnp.concatenate(
                    [jnp.where(high == jnp.full((), b, bf16), value, none) for b in range(blocks)], axis=0
                )
            )
            right_side.append(hot[:, at])
        return lax.dot_general(
            jnp.concatenate(left_side, axis=1),
            jnp.concatenate(right_side, axis=1),
            NT,
            preferred_element_type=f32,
        )

    per_cell = op // BLK
    tiles = cells * per_cell
    group = max(g for g in range(1, 13) if tiles % g == 0)

    def take_cells(source):
        def body(i):
            for u in range(group):
                j = i * group + u
                at = tile(j * BLK)
                row = pl.ds(pl.multiple_of(j // per_cell * width, width), width)
                vals[row, tile(j % per_cell * BLK)] = gather(source, at)

        return body

    @pl.loop(0, cells)
    def _(k):
        for u in range(per_cell):
            at = tile((per_cell * k + u) * BLK)
            hot[:, at] = low_part(at)

    for k in range(fp // BLK):
        hot[:, tile(jp + k * BLK)] = low_part(tile(jp + k * BLK))

    slab_row = idx[0:1, jp + o_sl : jp + o_sl + 2 * flp].astype(f32)
    slab_row = jnp.where(slab_row < 0, -2.0, slab_row)
    for k in range(2 * fsp // 128):
        row = idx[0:1, jp + k * 128 : jp + (k + 1) * 128].astype(f32)
        col = jnp.broadcast_to(row, (128, 128)).T
        cross[k * 128 : (k + 1) * 128, :] = jnp.where(col[:, 0:1] == slab_row, 1.0, 0.0).astype(bf16)

    loads[8].wait()
    loads[9].wait()
    lane_cell = lax.broadcasted_iota(jnp.int32, (8, lp), 1) // pstride
    atom_row = jnp.zeros((8, lp), f32)
    for c in range(cells):
        atom_row = jnp.where(lane_cell == c, atom_ref[c].astype(f32), atom_row)
    pack[...] = jnp.zeros(pack.shape, f32)
    for i in range(atoms):
        pack[0:nproj, i * pstride : i * pstride + nproj] = coupling_ref[:, i, :]
    pack[pstride : pstride + 8, 0:lp] = atom_row
    loads[7].wait()
    pp[...] = jnp.zeros(pp.shape, bf16)
    for c in range(cells):
        pp[c * pstride : c * pstride + nproj, c * op : c * op + order] = pr_ref[:, c, :]
    for i in (1, 2, 3):
        loads[i].wait()
    origin[...] = yb[...]
    field[...] = yb[...].astype(f32)
    kin[...] = jnp.zeros(kin.shape, bf16)
    kin[0:order, 0:order] = kin_ref[...]
    pot[...] = jnp.zeros(pot.shape, f32)
    pot[0:cells, 0:order] = pot_ref[...]
    row_at = lax.broadcasted_iota(jnp.int32, (16, flp), 0)
    counts = (lax.broadcasted_iota(jnp.int32, (16, flp), 1) + 1).astype(f32)
    probe = jnp.where(row_at == 0, 1.0, jnp.where(row_at == 1, counts, 0.0)).astype(bf16)
    row_of = lax.broadcasted_iota(jnp.int32, (16, fsp), 0)
    member, place = [], []
    for b in range(2):
        seen = lax.dot_general(
            probe, cross[:, b * flp : (b + 1) * flp], NT, preferred_element_type=f32
        )
        for a in range(2):
            member.append(jnp.broadcast_to(seen[0:1, a * fsp : (a + 1) * fsp], (16, fsp)))
            place.append(jnp.broadcast_to(seen[1:2, a * fsp : (a + 1) * fsp], (16, fsp)))
    stacked = jnp.zeros((16, fsp), f32)
    for i in range(4):
        stacked = jnp.where(row_of == i, member[i], stacked)
    tri_row = lax.broadcasted_iota(jnp.int32, (fsp, fsp), 0)
    tri_col = lax.broadcasted_iota(jnp.int32, (fsp, fsp), 1)
    before = jnp.where(tri_row < tri_col, 1.0, 0.0).astype(bf16)
    rank = jnp.dot(stacked.astype(bf16), before, preferred_element_type=f32)
    edge_row = lax.broadcasted_iota(jnp.int32, (EDGE, fsp), 0).astype(f32)
    spots = jnp.zeros((8, EDGE), f32)
    spot_row = lax.broadcasted_iota(jnp.int32, (8, EDGE), 0)
    for i in range(4):
        b, a = i // 2, i % 2
        label = jnp.where(member[i][0:1] > 0.5, rank[i : i + 1], -1.0)
        picked = jnp.where(edge_row == jnp.broadcast_to(label, (EDGE, fsp)), 1.0, 0.0).astype(bf16)
        ct[a, b * EDGE : (b + 1) * EDGE, :] = picked
        listed = lax.dot_general(place[i].astype(bf16), picked, NT, preferred_element_type=f32)
        spots = jnp.where(spot_row == i, listed[0:8], spots)
    pack[pstride + 8 :, 0:EDGE] = spots

    pl.semaphore_wait(barrier, greeted)
    pack_copies = []
    for d in range(1, n_slab):
        copy = pltpu.make_async_remote_copy(
            src_ref=pack,
            dst_ref=packs.at[d - 1],
            send_sem=pack_send.at[d - 1],
            recv_sem=pack_recv.at[d - 1],
            device_id={"slab": lax.rem(l + d, n_slab)},
            device_id_type=MESH,
        )
        copy.start()
        pack_copies.append(copy)

    def margin_of(step, first):
        margin = jnp.zeros((width, lp), f32)
        if first:
            for c in range(cells):
                margin += lax.dot_general(
                    vals[c * width : (c + 1) * width, :],
                    pp[:, c * op : (c + 1) * op],
                    NT,
                    preferred_element_type=f32,
                )
        else:
            for b in range(blocks):
                margin += lax.dot_general(
                    yb[b * width : (b + 1) * width, :],
                    pn[b * lp : (b + 1) * lp, :],
                    NT,
                    preferred_element_type=f32,
                )
        marg[step, 0] = margin

    def margin_copies(step):
        copies = []
        for d in range(1, n_slab):
            copy = pltpu.make_async_remote_copy(
                src_ref=marg.at[step, 0],
                dst_ref=marg.at[step, d],
                send_sem=marg_send.at[step, d - 1],
                recv_sem=marg_recv.at[step, d - 1],
                device_id={"slab": lax.rem(l + d, n_slab)},
                device_id_type=MESH,
            )
            copies.append(copy)
        return copies

    def local_part():
        kinv[...] = jnp.dot(vals[...], kin[...], preferred_element_type=f32)
        for c in range(cells):
            rows = slice(c * width, (c + 1) * width)
            total = scale_ref[c] * kinv[rows, :] + pot[c : c + 1, :] * vals[rows, :].astype(f32)
            tot[rows, :] = total.astype(bf16)

    def scatter():
        asm[...] = spread(
            [
                (tot[c * width : (c + 1) * width, tile(n * BLK)], tile(c * op + n * BLK))
                for c in range(cells)
                for n in range(per_cell)
            ]
        )

    def place_projectors():
        turn = 2 if cells % 2 == 0 else 1

        @pl.loop(0, cells // turn)
        def _(h):
            for u in range(turn):
                c = h * turn + u
                row = pl.ds(pl.multiple_of(c * pstride, pstride), pstride)
                placed = spread(
                    [(pp[row, tile(c * op + n * BLK)], tile(c * op + n * BLK)) for n in range(per_cell)]
                ).astype(bf16)
                for b in range(blocks):
                    to = pl.ds(pl.multiple_of(b * lp + c * pstride, pstride), pstride)
                    pn[to, :] = placed[b * pstride : (b + 1) * pstride]

    def use_packs():
        for copy in pack_copies:
            copy.wait()
        own_row = pack[pstride : pstride + 1, 0:lp]
        own_col = jnp.broadcast_to(own_row, (lp, lp)).T
        segment = lax.broadcasted_iota(jnp.int32, (pstride, wide), 1) // pstride
        chosen = jnp.zeros((lp, lp), f32)
        for d in range(n_slab):
            source = lax.rem(l + n_slab - d, n_slab)
            table = pack[0:pstride, :] if d == 0 else packs[d - 1, 0:pstride, :]
            for i in range(atoms):
                once = jnp.where(segment == i, table, 0.0)
                many = once
                for c in range(cells):
                    if c != i:
                        many = many + pltpu.roll(once, (c - i) * pstride % wide, 1)
                tiled = jnp.concatenate([many[:, 0:lp]] * cells, axis=0)
                chosen += jnp.where(own_col == (source * atoms + i).astype(f32), tiled, 0.0)
        for d in range(n_slab):
            last = slice(pstride, pstride + 1)
            row = pack[last, 0:lp] if d == 0 else packs[d - 1, last, 0:lp]
            used = jnp.where(own_col == row, chosen, 0.0)
            high = used.astype(bf16)
            coup[d, :, 0:lp] = high
            coup[d, :, lp : 2 * lp] = high
            coup[d, :, 2 * lp : 3 * lp] = (used - high.astype(f32)).astype(bf16)
        slot = lax.broadcasted_iota(jnp.int32, (flp, EDGE), 0).astype(f32) + 1.0
        for b in range(2):
            d = 1 if b == 0 else n_slab - 1
            for a in range(2):
                at = pstride + 8 + (1 - b) * 2 + a
                row = packs[max(d - 1, 0), at : at + 1, 0:EDGE]
                spot[b, :, a * EDGE : (a + 1) * EDGE] = jnp.where(
                    slot == jnp.broadcast_to(row, (flp, EDGE)), 1.0, 0.0
                ).astype(bf16)

    def exchange(step):
        moves = []

        def move(sends, gets, source, target, out_sem, in_sem, device):
            copy = pltpu.make_async_remote_copy(
                src_ref=source,
                dst_ref=target,
                send_sem=out_sem,
                recv_sem=in_sem,
                device_id=device,
                device_id_type=MESH,
            )
            pl.when(sends)(copy.start)
            moves.append((sends, gets, copy))

        cut = up(o_sl, BLK)
        take_faces(step, 0, cut)
        for a in range(2):
            seg = slice(a * fsp, (a + 1) * fsp)
            other = slice((1 - a) * fsp, (2 - a) * fsp)
            move(
                has_space[a],
                has_space[1 - a],
                outg.at[step, :, seg],
                inc.at[step, :, other],
                face_send.at[step, a],
                face_recv.at[step, a],
                {"space": to_space[a]},
            )
        for a in range(2):
            edge_send[step, a] = lax.dot_general(
                outg[step, :, a * fsp : (a + 1) * fsp], ct[a], NT, preferred_element_type=f32
            ).astype(bf16)
        for a, b in corners:
            move(
                has_space[a] & has_slab[b],
                has_space[1 - a] & has_slab[1 - b],
                edge_send.at[step, a, :, b * EDGE : (b + 1) * EDGE],
                in_edge.at[step, 1 - b, :, (1 - a) * EDGE : (2 - a) * EDGE],
                edge_sem.at[step, 2 * a + b],
                edge_got.at[step, 2 * a + b],
                {"space": to_space[a], "slab": to_slab[b]},
            )
        take_faces(step, cut, fp)
        for b in range(2):
            move(
                has_slab[b],
                has_slab[1 - b],
                outg.at[step, :, o_sl + b * flp : o_sl + (b + 1) * flp],
                in_slab.at[step, 1 - b],
                face_send.at[step, 2 + b],
                face_recv.at[step, 2 + b],
                {"slab": to_slab[b]},
            )
        return moves

    def finish(step, moves):
        for sends, gets, copy in moves:
            pl.when(gets)(copy.wait_recv)
        for sends, gets, copy in moves:
            pl.when(sends)(copy.wait_send)
        for b in range(2):
            part = slice(o_sl + b * flp, o_sl + (b + 1) * flp)
            corner = lax.dot_general(in_edge[step, b], spot[b], NT, preferred_element_type=f32)
            inc[step, :, part] = (in_slab[step, b].astype(f32) + corner).astype(bf16)
        return spread([(inc[step, :, tile(k * BLK)], tile(jp + k * BLK)) for k in range(fp // BLK)])

    def take_faces(step, first, last):
        for k in range(first // BLK, last // BLK):
            outg[step, :, tile(k * BLK)] = gather(yb, tile(jp + k * BLK))

    @pl.loop(0, 2)
    def _(step):
        marg_copies = margin_copies(step)
        later = (step > 0).astype(f32)

        @pl.when(step > 0)
        def _():
            margin_of(step, False)
            for copy in marg_copies:
                copy.start()

        pl.loop(0, tiles // group)(take_cells(yb))

        @pl.when(step == 0)
        def _():
            margin_of(step, True)
            for copy in marg_copies:
                copy.start()

        local_part()

        scatter()

        @pl.when(step == 0)
        def _():
            place_projectors()
            use_packs()

        coupled = jnp.zeros((width, lp), f32)
        for d in range(n_slab):
            if d > 0:
                marg_copies[d - 1].wait()
            whole = marg[step, d]
            high = whole.astype(bf16)
            low = (whole - high.astype(f32)).astype(bf16)
            coupled += lax.dot_general(
                jnp.concatenate([high, low, high], axis=1), coup[d], NT, preferred_element_type=f32
            )
        coupled = coupled.astype(bf16)
        for b in range(blocks):
            rows = slice(b * width, (b + 1) * width)
            whole = asm[rows, :] + jnp.dot(
                coupled, pn[b * lp : (b + 1) * lp, :], preferred_element_type=f32
            )
            asm[rows, :] = whole
            yb[rows, :] = whole.astype(bf16)

        moves = exchange(step)
        gain = (1.0 + later) / filter_half
        asm[...] = (
            gain * asm[...]
            - gain * filter_centre * field[...]
            - later * origin[...].astype(f32)
        )
        fresh = asm[...] + gain * finish(step, moves)
        field[...] = fresh
        yb[...] = fresh.astype(bf16)

    for b in range(blocks):
        count = min(BLK, nodes - b * BLK)
        out_ref[:, b * BLK : b * BLK + count] = field[b * width : (b + 1) * width, 0:count]


def shards(
    wavefunctions,
    kinetic,
    cell_scale,
    potential,
    cell_nodes,
    face_space,
    face_slab,
    projectors,
    cell_atom,
    coupling,
):
    width, nodes = wavefunctions.shape
    cells, order = cell_nodes.shape
    atoms, nproj = coupling.shape[0], coupling.shape[1]
    n_space, n_slab = lax.axis_size("space"), lax.axis_size("slab")
    fs, fl = face_space.shape[1], face_slab.shape[1]
    pstride = up(nproj, 16)
    while cells * pstride % 128:
        pstride += 16
    dims = dict(
        n_space=n_space, n_slab=n_slab, width=width, nodes=nodes, cells=cells, order=order,
        atoms=atoms, nproj=nproj, pstride=pstride, fs=fs, fl=fl,
    )
    op, npad = up(order, BLK), up(nodes, BLK)
    fsp, flp = up(fs, 128), up(fl, 128)
    jp = cells * op
    fp = up(2 * fsp + 2 * flp, BLK)
    lp = cells * pstride
    others = max(n_slab - 1, 1)
    wide = up(max(atoms * pstride, lp, EDGE), 128)
    vmem = pl.BlockSpec(memory_space=pltpu.VMEM)
    dma = pltpu.SemaphoreType.DMA
    return pl.pallas_call(
        functools.partial(kernel, dims),
        out_shape=pltpu.VMEM((width, nodes), f32),
        in_specs=[pl.BlockSpec(memory_space=pl.ANY)] * 10,
        out_specs=vmem,
        scratch_shapes=[
            pltpu.VMEM((width, nodes), bf16),
            pltpu.VMEM((order, order), bf16),
            pltpu.SMEM((cells,), f32),
            pltpu.VMEM((cells, order), f32),
            pltpu.VMEM((cells, order), jnp.int32),
            pltpu.VMEM((2, fs), jnp.int32),
            pltpu.VMEM((2, fl), jnp.int32),
            pltpu.VMEM((nproj, cells, order), bf16),
            pltpu.SMEM((cells,), jnp.int32),
            pltpu.VMEM((nproj, atoms, nproj), f32),
            dma((10,)),
            pltpu.VMEM((BLK, jp + fp), bf16),
            pltpu.VMEM((pstride + 16, wide), f32),
            pltpu.VMEM((8, jp + fp), jnp.int32),
            pltpu.VMEM((op, op), bf16),
            pltpu.VMEM((lp, jp), bf16),
            pltpu.VMEM((up(cells, 8), op), f32),
            pltpu.VMEM((2 * fsp, 2 * flp), bf16),
            pltpu.VMEM((others, pstride + 16, wide), f32),
            pltpu.VMEM((n_slab, lp, 3 * lp), bf16),
            pltpu.VMEM((npad // BLK * width, BLK), bf16),
            pltpu.VMEM((cells * width, op), bf16),
            pltpu.VMEM((cells * width, op), f32),
            pltpu.VMEM((cells * width, op), bf16),
            pltpu.VMEM((npad // BLK * width, BLK), f32),
            pltpu.VMEM((npad // BLK * width, BLK), f32),
            pltpu.VMEM((npad // BLK * width, BLK), bf16),
            pltpu.VMEM((2, width, fp), bf16),
            pltpu.VMEM((2, 2, width, flp), bf16),
            pltpu.VMEM((2, width, fp), bf16),
            pltpu.VMEM((2, n_slab, width, lp), f32),
            pltpu.VMEM((npad // BLK * lp, BLK), bf16),
            pltpu.VMEM((2, 2 * EDGE, fsp), bf16),
            pltpu.VMEM((2, flp, 2 * EDGE), bf16),
            pltpu.VMEM((2, 2, width, 2 * EDGE), bf16),
            pltpu.VMEM((2, 2, width, 2 * EDGE), bf16),
            dma((others,)),
            dma((others,)),
            dma((2, others)),
            dma((2, others)),
            dma((2, 4)),
            dma((2, 4)),
            dma((2, 4)),
            dma((2, 4)),
        ],
        compiler_params=pltpu.CompilerParams(
            collective_id=0, has_side_effects=True, vmem_limit_bytes=60 * 1024 * 1024
        ),
    )(
        wavefunctions, kinetic, cell_scale, potential, cell_nodes, face_space, face_slab,
        projectors.transpose(1, 0, 2), cell_atom, coupling.transpose(1, 0, 2),
    )


def solution(mesh):
    placed = (
        P(None, ("space", "slab")),
        P(),
        P(("space", "slab")),
        P(("space", "slab"), None),
        P(("space", "slab"), None),
        P(("space", "slab"), None),
        P(("space", "slab"), None),
        P(("space", "slab"), None, None),
        P(("space", "slab")),
        P(("space", "slab"), None, None),
    )
    return jax.shard_map(
        shards, mesh=mesh, in_specs=placed, out_specs=P(None, ("space", "slab")), check_vma=False
    )
```

```python
import functools

import jax
import jax.numpy as jnp
from jax import lax
from jax.experimental import pallas as pl
from jax.experimental.pallas import tpu as pltpu
from jax.sharding import PartitionSpec as P

filter_centre = 8.0
filter_half = 8.0
BLK = 256
SHIFT = 8
EDGE = 128
MESH = pl.DeviceIdType.MESH
NT = (((1,), (1,)), ((), ()))
f32 = jnp.float32
bf16 = jnp.bfloat16


def up(value, unit):
    return -(-value // unit) * unit


def kernel(
    dims,
    y_hbm,
    kin_hbm,
    scale_hbm,
    pot_hbm,
    cn_hbm,
    fs_hbm,
    fl_hbm,
    pr_hbm,
    atom_hbm,
    coupling_hbm,
    out_ref,
    y_ref,
    kin_ref,
    scale_ref,
    pot_ref,
    cn_ref,
    fs_ref,
    fl_ref,
    pr_ref,
    atom_ref,
    coupling_ref,
    in_sem,
    hot,
    pack,
    idx,
    kin,
    pp,
    pot,
    cross,
    packs,
    coup,
    yb,
    vals,
    kinv,
    tot,
    asm,
    field,
    origin,
    outg,
    in_slab,
    inc,
    marg,
    pn,
    ct,
    spot,
    edge_send,
    in_edge,
    pack_send,
    pack_recv,
    marg_send,
    marg_recv,
    face_send,
    face_recv,
    edge_sem,
    edge_got,
):
    n_space, n_slab = dims["n_space"], dims["n_slab"]
    width, nodes, cells, order = dims["width"], dims["nodes"], dims["cells"], dims["order"]
    atoms, nproj, pstride = dims["atoms"], dims["nproj"], dims["pstride"]
    fs, fl = dims["fs"], dims["fl"]
    op, npad = up(order, BLK), up(nodes, BLK)
    fsp, flp = up(fs, 128), up(fl, 128)
    jp = cells * op
    fp = up(2 * fsp + 2 * flp, BLK)
    lp = cells * pstride
    o_sl = 2 * fsp
    wide = up(max(atoms * pstride, lp, EDGE), 128)
    blocks = npad // BLK

    outside = (
        y_hbm, kin_hbm, scale_hbm, pot_hbm, cn_hbm, fs_hbm, fl_hbm, pr_hbm, atom_hbm, coupling_hbm
    )
    inside = (
        y_ref, kin_ref, scale_ref, pot_ref, cn_ref, fs_ref, fl_ref, pr_ref, atom_ref, coupling_ref
    )
    loads = [
        pltpu.make_async_copy(outside[i], inside[i], in_sem.at[i]) for i in range(len(outside))
    ]
    for i in (4, 5, 6, 0, 8, 9, 7, 1, 2, 3):
        loads[i].start()

    s = lax.axis_index("space")
    l = lax.axis_index("slab")
    above, below = lax.rem(s + 1, n_space), lax.rem(s + n_space - 1, n_space)
    right, left = lax.rem(l + 1, n_slab), lax.rem(l + n_slab - 1, n_slab)
    to_space, to_slab = (below, above), (left, right)
    has_space, has_slab = (s > 0, s < n_space - 1), (l > 0, l < n_slab - 1)
    corners = [(a, b) for a in range(2) for b in range(2)]

    barrier = pltpu.get_barrier_semaphore()

    def greet(exists, device):
        @pl.when(exists)
        def _():
            pl.semaphore_signal(barrier, inc=1, device_id=device, device_id_type=MESH)

        return exists.astype(jnp.int32)

    for d in range(1, n_slab):
        pl.semaphore_signal(
            barrier, inc=1, device_id={"slab": lax.rem(l + d, n_slab)}, device_id_type=MESH
        )
    greeted = n_slab - 1
    for a in range(2):
        greeted += greet(has_space[a], {"space": to_space[a]})
    for a, b in corners:
        greeted += greet(has_space[a] & has_slab[b], {"space": to_space[a], "slab": to_slab[b]})
    for a in range(2):

        @pl.when(jnp.logical_not(has_space[a]))
        def _():
            for step in range(2):
                inc[step, :, a * fsp : (a + 1) * fsp] = jnp.zeros((width, fsp), bf16)

        @pl.when(jnp.logical_not(has_slab[a]))
        def _():
            for step in range(2):
                in_slab[step, a] = jnp.zeros((width, flp), bf16)

    for a, b in corners:

        @pl.when(jnp.logical_not(has_space[a] & has_slab[b]))
        def _():
            for step in range(2):
                in_edge[step, b, :, a * EDGE : (a + 1) * EDGE] = jnp.zeros((width, EDGE), bf16)

    if fp > 2 * fsp + 2 * flp:
        for step in range(2):
            inc[step, :, 2 * fsp + 2 * flp :] = jnp.zeros((width, fp - 2 * fsp - 2 * flp), bf16)

    for i in (4, 5, 6):
        loads[i].wait()
    idx[...] = jnp.full(idx.shape, -1, jnp.int32)
    for c in range(cells):
        idx[0:1, c * op : c * op + order] = cn_ref[c : c + 1, :]
    for k in range(2):
        idx[0:1, jp + k * fsp : jp + k * fsp + fs] = fs_ref[k : k + 1, :]
        off = jp + o_sl + k * flp
        idx[0:1, off : off + fl] = fl_ref[k : k + 1, :]

    loads[0].wait()
    for b in range(blocks):
        count = min(BLK, nodes - b * BLK)
        rows = slice(b * width, (b + 1) * width)
        if count < BLK:
            yb[rows, :] = jnp.zeros((width, BLK), bf16)
        yb[rows, 0:count] = y_ref[:, b * BLK : b * BLK + count]
    lane_rows = lax.broadcasted_iota(jnp.int32, (BLK, BLK), 0).astype(f32).astype(bf16)

    def tile(start):
        if isinstance(start, int):
            return slice(start, start + BLK)
        return pl.ds(pl.multiple_of(start, BLK), BLK)

    def low_part(at):
        low = (idx[0:1, at] & (BLK - 1)).astype(f32).astype(bf16)
        hit = lane_rows == jnp.broadcast_to(low, (BLK, BLK))
        return jnp.where(hit, jnp.ones((), bf16), jnp.zeros((), bf16))

    def gather(source, at):
        every = jnp.dot(source[...], hot[:, at], preferred_element_type=f32)
        high = jnp.broadcast_to(idx[0:1, at] >> SHIFT, (width, BLK))
        got = jnp.zeros((width, BLK), f32)
        for b in range(blocks):
            got = jnp.where(high == b, every[b * width : (b + 1) * width], got)
        return got.astype(bf16)

    def spread(pieces):
        left_side, right_side = [], []
        for value, at in pieces:
            high = (idx[0:1, at] >> SHIFT).astype(f32).astype(bf16)
            high = jnp.broadcast_to(high, value.shape)
            none = jnp.zeros((), bf16)
            left_side.append(
                jnp.concatenate(
                    [jnp.where(high == jnp.full((), b, bf16), value, none) for b in range(blocks)], axis=0
                )
            )
            right_side.append(hot[:, at])
        return lax.dot_general(
            jnp.concatenate(left_side, axis=1),
            jnp.concatenate(right_side, axis=1),
            NT,
            preferred_element_type=f32,
        )

    per_cell = op // BLK
    tiles = cells * per_cell
    group = max(g for g in range(1, 13) if tiles % g == 0)

    def take_cells(source):
        def body(i):
            for u in range(group):
                j = i * group + u
                at = tile(j * BLK)
                row = pl.ds(pl.multiple_of(j // per_cell * width, width), width)
                vals[row, tile(j % per_cell * BLK)] = gather(source, at)

        return body

    @pl.loop(0, cells)
    def _(k):
        for u in range(per_cell):
            at = tile((per_cell * k + u) * BLK)
            hot[:, at] = low_part(at)

    for k in range(fp // BLK):
        hot[:, tile(jp + k * BLK)] = low_part(tile(jp + k * BLK))

    slab_row = idx[0:1, jp + o_sl : jp + o_sl + 2 * flp].astype(f32)
    slab_row = jnp.where(slab_row < 0, -2.0, slab_row)
    for k in range(2 * fsp // 128):
        row = idx[0:1, jp + k * 128 : jp + (k + 1) * 128].astype(f32)
        col = jnp.broadcast_to(row, (128, 128)).T
        cross[k * 128 : (k + 1) * 128, :] = jnp.where(col[:, 0:1] == slab_row, 1.0, 0.0).astype(bf16)

    loads[8].wait()
    loads[9].wait()
    lane_cell = lax.broadcasted_iota(jnp.int32, (8, lp), 1) // pstride
    atom_row = jnp.zeros((8, lp), f32)
    for c in range(cells):
        atom_row = jnp.where(lane_cell == c, atom_ref[c].astype(f32), atom_row)
    pack[...] = jnp.zeros(pack.shape, f32)
    for i in range(atoms):
        pack[0:nproj, i * pstride : i * pstride + nproj] = coupling_ref[:, i, :]
    pack[pstride : pstride + 8, 0:lp] = atom_row
    loads[7].wait()
    pp[...] = jnp.zeros(pp.shape, bf16)
    for c in range(cells):
        pp[c * pstride : c * pstride + nproj, c * op : c * op + order] = pr_ref[:, c, :]
    for i in (1, 2, 3):
        loads[i].wait()
    origin[...] = yb[...]
    field[...] = yb[...].astype(f32)
    kin[...] = jnp.zeros(kin.shape, bf16)
    kin[0:order, 0:order] = kin_ref[...]
    pot[...] = jnp.zeros(pot.shape, f32)
    pot[0:cells, 0:order] = pot_ref[...]
    row_at = lax.broadcasted_iota(jnp.int32, (16, flp), 0)
    counts = (lax.broadcasted_iota(jnp.int32, (16, flp), 1) + 1).astype(f32)
    probe = jnp.where(row_at == 0, 1.0, jnp.where(row_at == 1, counts, 0.0)).astype(bf16)
    row_of = lax.broadcasted_iota(jnp.int32, (16, fsp), 0)
    member, place = [], []
    for b in range(2):
        seen = lax.dot_general(
            probe, cross[:, b * flp : (b + 1) * flp], NT, preferred_element_type=f32
        )
        for a in range(2):
            member.append(jnp.broadcast_to(seen[0:1, a * fsp : (a + 1) * fsp], (16, fsp)))
            place.append(jnp.broadcast_to(seen[1:2, a * fsp : (a + 1) * fsp], (16, fsp)))
    stacked = jnp.zeros((16, fsp), f32)
    for i in range(4):
        stacked = jnp.where(row_of == i, member[i], stacked)
    tri_row = lax.broadcasted_iota(jnp.int32, (fsp, fsp), 0)
    tri_col = lax.broadcasted_iota(jnp.int32, (fsp, fsp), 1)
    before = jnp.where(tri_row < tri_col, 1.0, 0.0).astype(bf16)
    rank = jnp.dot(stacked.astype(bf16), before, preferred_element_type=f32)
    edge_row = lax.broadcasted_iota(jnp.int32, (EDGE, fsp), 0).astype(f32)
    spots = jnp.zeros((8, EDGE), f32)
    spot_row = lax.broadcasted_iota(jnp.int32, (8, EDGE), 0)
    for i in range(4):
        b, a = i // 2, i % 2
        label = jnp.where(member[i][0:1] > 0.5, rank[i : i + 1], -1.0)
        picked = jnp.where(edge_row == jnp.broadcast_to(label, (EDGE, fsp)), 1.0, 0.0).astype(bf16)
        ct[a, b * EDGE : (b + 1) * EDGE, :] = picked
        listed = lax.dot_general(place[i].astype(bf16), picked, NT, preferred_element_type=f32)
        spots = jnp.where(spot_row == i, listed[0:8], spots)
    pack[pstride + 8 :, 0:EDGE] = spots

    pl.semaphore_wait(barrier, greeted)
    pack_copies = []
    for d in range(1, n_slab):
        copy = pltpu.make_async_remote_copy(
            src_ref=pack,
            dst_ref=packs.at[d - 1],
            send_sem=pack_send.at[d - 1],
            recv_sem=pack_recv.at[d - 1],
            device_id={"slab": lax.rem(l + d, n_slab)},
            device_id_type=MESH,
        )
        copy.start()
        pack_copies.append(copy)

    def margin_of(step, first):
        margin = jnp.zeros((width, lp), f32)
        if first:
            for c in range(cells):
                margin += lax.dot_general(
                    vals[c * width : (c + 1) * width, :],
                    pp[:, c * op : (c + 1) * op],
                    NT,
                    preferred_element_type=f32,
                )
        else:
            for b in range(blocks):
                margin += lax.dot_general(
                    yb[b * width : (b + 1) * width, :],
                    pn[b * lp : (b + 1) * lp, :],
                    NT,
                    preferred_element_type=f32,
                )
        marg[step, 0] = margin

    def margin_copies(step):
        copies = []
        for d in range(1, n_slab):
            copy = pltpu.make_async_remote_copy(
                src_ref=marg.at[step, 0],
                dst_ref=marg.at[step, d],
                send_sem=marg_send.at[step, d - 1],
                recv_sem=marg_recv.at[step, d - 1],
                device_id={"slab": lax.rem(l + d, n_slab)},
                device_id_type=MESH,
            )
            copies.append(copy)
        return copies

    def local_part():
        kinv[...] = jnp.dot(vals[...], kin[...], preferred_element_type=f32)
        for c in range(cells):
            rows = slice(c * width, (c + 1) * width)
            total = scale_ref[c] * kinv[rows, :] + pot[c : c + 1, :] * vals[rows, :].astype(f32)
            tot[rows, :] = total.astype(bf16)

    def scatter():
        pair = max(g for g in range(1, 5) if cells % g == 0)

        def one(c):
            row = pl.multiple_of(c * width, width)
            pieces = []
            for n in range(per_cell):
                value = tot[pl.ds(row, width), tile(n * BLK)]
                pieces.append((value, tile(c * op + n * BLK)))
            asm[...] += spread(pieces)

        asm[...] = jnp.zeros(asm.shape, f32)

        @pl.loop(0, cells // pair)
        def _(c):
            for u in range(pair):
                one(pair * c + u)

    def place_projectors():
        turn = 2 if cells % 2 == 0 else 1

        @pl.loop(0, cells // turn)
        def _(h):
            for u in range(turn):
                c = h * turn + u
                row = pl.ds(pl.multiple_of(c * pstride, pstride), pstride)
                placed = spread(
                    [(pp[row, tile(c * op + n * BLK)], tile(c * op + n * BLK)) for n in range(per_cell)]
                ).astype(bf16)
                for b in range(blocks):
                    to = pl.ds(pl.multiple_of(b * lp + c * pstride, pstride), pstride)
                    pn[to, :] = placed[b * pstride : (b + 1) * pstride]

    def use_packs():
        for copy in pack_copies:
            copy.wait()
        own_row = pack[pstride : pstride + 1, 0:lp]
        own_col = jnp.broadcast_to(own_row, (lp, lp)).T
        segment = lax.broadcasted_iota(jnp.int32, (pstride, wide), 1) // pstride
        chosen = jnp.zeros((lp, lp), f32)
        for d in range(n_slab):
            source = lax.rem(l + n_slab - d, n_slab)
            table = pack[0:pstride, :] if d == 0 else packs[d - 1, 0:pstride, :]
            for i in range(atoms):
                once = jnp.where(segment == i, table, 0.0)
                many = once
                for c in range(cells):
                    if c != i:
                        many = many + pltpu.roll(once, (c - i) * pstride % wide, 1)
                tiled = jnp.concatenate([many[:, 0:lp]] * cells, axis=0)
                chosen += jnp.where(own_col == (source * atoms + i).astype(f32), tiled, 0.0)
        for d in range(n_slab):
            last = slice(pstride, pstride + 1)
            row = pack[last, 0:lp] if d == 0 else packs[d - 1, last, 0:lp]
            used = jnp.where(own_col == row, chosen, 0.0)
            high = used.astype(bf16)
            coup[d, :, 0:lp] = high
            coup[d, :, lp : 2 * lp] = high
            coup[d, :, 2 * lp : 3 * lp] = (used - high.astype(f32)).astype(bf16)
        slot = lax.broadcasted_iota(jnp.int32, (flp, EDGE), 0).astype(f32) + 1.0
        for b in range(2):
            d = 1 if b == 0 else n_slab - 1
            for a in range(2):
                at = pstride + 8 + (1 - b) * 2 + a
                row = packs[max(d - 1, 0), at : at + 1, 0:EDGE]
                spot[b, :, a * EDGE : (a + 1) * EDGE] = jnp.where(
                    slot == jnp.broadcast_to(row, (flp, EDGE)), 1.0, 0.0
                ).astype(bf16)

    def exchange(step):
        moves = []

        def move(sends, gets, source, target, out_sem, in_sem, device):
            copy = pltpu.make_async_remote_copy(
                src_ref=source,
                dst_ref=target,
                send_sem=out_sem,
                recv_sem=in_sem,
                device_id=device,
                device_id_type=MESH,
            )
            pl.when(sends)(copy.start)
            moves.append((sends, gets, copy))

        cut = up(o_sl, BLK)
        take_faces(step, 0, cut)
        for a in range(2):
            seg = slice(a * fsp, (a + 1) * fsp)
            other = slice((1 - a) * fsp, (2 - a) * fsp)
            move(
                has_space[a],
                has_space[1 - a],
                outg.at[step, :, seg],
                inc.at[step, :, other],
                face_send.at[step, a],
                face_recv.at[step, a],
                {"space": to_space[a]},
            )
        for a in range(2):
            edge_send[step, a] = lax.dot_general(
                outg[step, :, a * fsp : (a + 1) * fsp], ct[a], NT, preferred_element_type=f32
            ).astype(bf16)
        for a, b in corners:
            move(
                has_space[a] & has_slab[b],
                has_space[1 - a] & has_slab[1 - b],
                edge_send.at[step, a, :, b * EDGE : (b + 1) * EDGE],
                in_edge.at[step, 1 - b, :, (1 - a) * EDGE : (2 - a) * EDGE],
                edge_sem.at[step, 2 * a + b],
                edge_got.at[step, 2 * a + b],
                {"space": to_space[a], "slab": to_slab[b]},
            )
        take_faces(step, cut, fp)
        for b in range(2):
            move(
                has_slab[b],
                has_slab[1 - b],
                outg.at[step, :, o_sl + b * flp : o_sl + (b + 1) * flp],
                in_slab.at[step, 1 - b],
                face_send.at[step, 2 + b],
                face_recv.at[step, 2 + b],
                {"slab": to_slab[b]},
            )
        return moves

    def finish(step, moves):
        for sends, gets, copy in moves:
            pl.when(gets)(copy.wait_recv)
        for b in range(2):
            part = slice(o_sl + b * flp, o_sl + (b + 1) * flp)
            corner = lax.dot_general(in_edge[step, b], spot[b], NT, preferred_element_type=f32)
            inc[step, :, part] = (in_slab[step, b].astype(f32) + corner).astype(bf16)
        halo = spread([(inc[step, :, tile(k * BLK)], tile(jp + k * BLK)) for k in range(fp // BLK)])
        return halo

    def take_faces(step, first, last):
        for k in range(first // BLK, last // BLK):
            outg[step, :, tile(k * BLK)] = gather(yb, tile(jp + k * BLK))

    @pl.loop(0, 2)
    def _(step):
        marg_copies = margin_copies(step)
        later = (step > 0).astype(f32)

        @pl.when(step > 0)
        def _():
            margin_of(step, False)
            for copy in marg_copies:
                copy.start()

        pl.loop(0, tiles // group)(take_cells(yb))

        @pl.when(step == 0)
        def _():
            margin_of(step, True)
            for copy in marg_copies:
                copy.start()

        local_part()

        scatter()

        @pl.when(step == 0)
        def _():
            place_projectors()
            use_packs()

        coupled = jnp.zeros((width, lp), f32)
        for d in range(n_slab):
            if d > 0:
                marg_copies[d - 1].wait()
            whole = marg[step, d]
            high = whole.astype(bf16)
            low = (whole - high.astype(f32)).astype(bf16)
            coupled += lax.dot_general(
                jnp.concatenate([high, low, high], axis=1), coup[d], NT, preferred_element_type=f32
            )
        coupled = coupled.astype(bf16)
        for b in range(blocks):
            rows = slice(b * width, (b + 1) * width)
            whole = asm[rows, :] + jnp.dot(
                coupled, pn[b * lp : (b + 1) * lp, :], preferred_element_type=f32
            )
            asm[rows, :] = whole
            yb[rows, :] = whole.astype(bf16)

        moves = exchange(step)
        gain = (1.0 + later) / filter_half
        asm[...] = (
            gain * asm[...]
            - gain * filter_centre * field[...]
            - later * origin[...].astype(f32)
        )
        fresh = asm[...] + gain * finish(step, moves)
        field[...] = fresh
        yb[...] = fresh.astype(bf16)
        for sends, gets, copy in moves:
            pl.when(sends)(copy.wait_send)

    for b in range(blocks):
        count = min(BLK, nodes - b * BLK)
        out_ref[:, b * BLK : b * BLK + count] = field[b * width : (b + 1) * width, 0:count]


def shards(
    wavefunctions,
    kinetic,
    cell_scale,
    potential,
    cell_nodes,
    face_space,
    face_slab,
    projectors,
    cell_atom,
    coupling,
):
    width, nodes = wavefunctions.shape
    cells, order = cell_nodes.shape
    atoms, nproj = coupling.shape[0], coupling.shape[1]
    n_space, n_slab = lax.axis_size("space"), lax.axis_size("slab")
    fs, fl = face_space.shape[1], face_slab.shape[1]
    pstride = up(nproj, 16)
    while cells * pstride % 128:
        pstride += 16
    dims = dict(
        n_space=n_space, n_slab=n_slab, width=width, nodes=nodes, cells=cells, order=order,
        atoms=atoms, nproj=nproj, pstride=pstride, fs=fs, fl=fl,
    )
    op, npad = up(order, BLK), up(nodes, BLK)
    fsp, flp = up(fs, 128), up(fl, 128)
    jp = cells * op
    fp = up(2 * fsp + 2 * flp, BLK)
    lp = cells * pstride
    others = max(n_slab - 1, 1)
    wide = up(max(atoms * pstride, lp, EDGE), 128)
    vmem = pl.BlockSpec(memory_space=pltpu.VMEM)
    dma = pltpu.SemaphoreType.DMA
    return pl.pallas_call(
        functools.partial(kernel, dims),
        out_shape=pltpu.VMEM((width, nodes), f32),
        in_specs=[pl.BlockSpec(memory_space=pl.ANY)] * 10,
        out_specs=vmem,
        scratch_shapes=[
            pltpu.VMEM((width, nodes), bf16),
            pltpu.VMEM((order, order), bf16),
            pltpu.SMEM((cells,), f32),
            pltpu.VMEM((cells, order), f32),
            pltpu.VMEM((cells, order), jnp.int32),
            pltpu.VMEM((2, fs), jnp.int32),
            pltpu.VMEM((2, fl), jnp.int32),
            pltpu.VMEM((nproj, cells, order), bf16),
            pltpu.SMEM((cells,), jnp.int32),
            pltpu.VMEM((nproj, atoms, nproj), f32),
            dma((10,)),
            pltpu.VMEM((BLK, jp + fp), bf16),
            pltpu.VMEM((pstride + 16, wide), f32),
            pltpu.VMEM((8, jp + fp), jnp.int32),
            pltpu.VMEM((op, op), bf16),
            pltpu.VMEM((lp, jp), bf16),
            pltpu.VMEM((up(cells, 8), op), f32),
            pltpu.VMEM((2 * fsp, 2 * flp), bf16),
            pltpu.VMEM((others, pstride + 16, wide), f32),
            pltpu.VMEM((n_slab, lp, 3 * lp), bf16),
            pltpu.VMEM((npad // BLK * width, BLK), bf16),
            pltpu.VMEM((cells * width, op), bf16),
            pltpu.VMEM((cells * width, op), f32),
            pltpu.VMEM((cells * width, op), bf16),
            pltpu.VMEM((npad // BLK * width, BLK), f32),
            pltpu.VMEM((npad // BLK * width, BLK), f32),
            pltpu.VMEM((npad // BLK * width, BLK), bf16),
            pltpu.VMEM((2, width, fp), bf16),
            pltpu.VMEM((2, 2, width, flp), bf16),
            pltpu.VMEM((2, width, fp), bf16),
            pltpu.VMEM((2, n_slab, width, lp), f32),
            pltpu.VMEM((npad // BLK * lp, BLK), bf16),
            pltpu.VMEM((2, 2 * EDGE, fsp), bf16),
            pltpu.VMEM((2, flp, 2 * EDGE), bf16),
            pltpu.VMEM((2, 2, width, 2 * EDGE), bf16),
            pltpu.VMEM((2, 2, width, 2 * EDGE), bf16),
            dma((others,)),
            dma((others,)),
            dma((2, others)),
            dma((2, others)),
            dma((2, 4)),
            dma((2, 4)),
            dma((2, 4)),
            dma((2, 4)),
        ],
        compiler_params=pltpu.CompilerParams(
            collective_id=0, has_side_effects=True, vmem_limit_bytes=60 * 1024 * 1024
        ),
    )(
        wavefunctions, kinetic, cell_scale, potential, cell_nodes, face_space, face_slab,
        projectors.transpose(1, 0, 2), cell_atom, coupling.transpose(1, 0, 2),
    )


def solution(mesh):
    placed = (
        P(None, ("space", "slab")),
        P(),
        P(("space", "slab")),
        P(("space", "slab"), None),
        P(("space", "slab"), None),
        P(("space", "slab"), None),
        P(("space", "slab"), None),
        P(("space", "slab"), None, None),
        P(("space", "slab")),
        P(("space", "slab"), None, None),
    )
    return jax.shard_map(
        shards, mesh=mesh, in_specs=placed, out_specs=P(None, ("space", "slab")), check_vma=False
    )
```
